768 devices in a mesh: row: 16 (over y, core), theta: 12 (over z_hi, x), group: 4 (over z_lo).
Axes of the slice: x: 4, y: 8, z: 12 (z_hi: 3, z_lo: 4; z = z_hi * 4 + z_lo), core: 2. Of those that a mesh axis runs over, the one named last changes fastest.
Arguments:
- dust: bfloat16 [32, 256, 96, 128], P('group', 'row', 'theta'), may hold values from 0.0099487305 to 1
- table: bfloat16 [32, 48], replicated, may hold values from 0.019897461 to 2
- planck: float32 [48], P('group'), may hold values from 0.05 to 0.5
- energy_old: float32 [48, 256, 96, 128], P('group', 'row', 'theta'), may hold values from 0.05 to 1
- temp_old: float32 [256, 96, 128], P('row', 'theta'), may hold values from 0.5 to 1.5
Outputs:
- energy: float32 [48, 256, 96, 128], P('group', 'row', 'theta')
- temperature: float32 [256, 96, 128], P('row', 'theta')
The draws below stay inside these ranges and needn't reach their ends.
All inputs are finite; a program needn't handle non-finite values.
Results may differ from the reference program's by a relative error of at most 0.00045.
Values may be sent and summed in bfloat16 or wider, within the bound.
No kernel may reach another device: no remote copies, remote signals or barrier semaphores. Data moves between devices by JAX's collectives and lax.ppermute only.
A program may use at most 64 MiB of HBM per device.

```python
import math
import jax
import jax.numpy as jnp
from jax import lax

BINS = 32
GROUPS = 48
ITERS = 3
NR = 256
NT = 96
NP = 128


def block_scale(own_key, extent, pieces, least, high):
    def one(position, shards_of):
        draws = jax.random.uniform(jax.random.fold_in(jax.random.fold_in(own_key, 6), position), (shards_of,), jnp.float32, least / len(pieces), high / len(pieces))
        return jnp.repeat(jnp.exp(draws), extent[position] // shards_of).reshape((-1,) + (1,) * (len(extent) - position - 1))

    gain = one(*pieces[0])
    for cut in pieces[1:]:
        gain = gain * one(*cut)
    return gain


def setup_inputs(seed: int = 0) -> dict:
    splits = jax.random.split(jax.random.key(seed), 6)
    return {
        "dust": jnp.clip(jnp.exp(math.log(1.0) - 4.61031033 * jax.random.uniform(splits[0], (BINS, NR, NT, NP), jnp.float32) ** block_scale(splits[0], (BINS, NR, NT, NP), ((0, 4), (1, 16), (2, 12)), -0.2, 0.2)), 0.0099487305, 1.0).astype(jnp.bfloat16),
        "table": jnp.clip(jnp.exp(jax.random.uniform(splits[1], (BINS, GROUPS), jnp.float32, math.log(0.019897461), math.log(2.0))), 0.019897461, 2.0).astype(jnp.bfloat16),
        "planck": jnp.clip(jnp.exp(math.log(0.5) - 2.3025851 * jax.random.uniform(splits[2], (GROUPS,), jnp.float32) ** block_scale(splits[2], (GROUPS,), ((0, 4),), -0.2, 0.2)), 0.05, 0.5),
        "energy_old": jnp.clip(jnp.exp(math.log(1.0) - 2.9957323 * jax.random.uniform(splits[3], (GROUPS, NR, NT, NP), jnp.float32) ** block_scale(splits[3], (GROUPS, NR, NT, NP), ((0, 4), (1, 16), (2, 12)), -0.2, 0.2)), 0.05, 1.0),
        "temp_old": jnp.clip(0.5 + 1.0 * jax.random.uniform(splits[4], (NR, NT, NP), jnp.float32) ** block_scale(splits[4], (NR, NT, NP), ((0, 16), (1, 12)), -0.2, 0.2), 0.5, 1.5),
    }


heat_capacity = 2.0
diffusion_reach = 20.0


def sweep(energy_g, old_g, kappa_g, emit):
    epad = jnp.pad(energy_g, ((1, 1), (1, 1), (0, 0)))
    kpad = jnp.pad(kappa_g, ((1, 1), (1, 1), (0, 0)))
    sides = [
        (epad[2:, 1:-1], kpad[2:, 1:-1]),
        (epad[:-2, 1:-1], kpad[:-2, 1:-1]),
        (epad[1:-1, 2:], kpad[1:-1, 2:]),
        (epad[1:-1, :-2], kpad[1:-1, :-2]),
        (jnp.roll(energy_g, 1, 2), jnp.roll(kappa_g, 1, 2)),
        (jnp.roll(energy_g, -1, 2), jnp.roll(kappa_g, -1, 2)),
    ]
    numer = old_g + kappa_g * emit
    denom = 1.0 + kappa_g
    for e_side, k_side in sides:
        limit = jnp.abs(e_side - energy_g) / (0.5 * (e_side + energy_g))
        weight = diffusion_reach / (1.5 * (kappa_g + k_side) + limit)
        numer = numer + weight * e_side
        denom = denom + weight
    return numer / denom


def reference(dust, table, planck, energy_old, temp_old):
    flat = dust.reshape(BINS, -1)
    gids = jnp.arange(GROUPS, dtype=jnp.int32)
    energy = energy_old
    temp = temp_old
    for step in range(ITERS):
        cube = temp * temp * temp
        fourth = cube * temp

        def one(carry, items):
            top, bottom = carry
            gid, energy_g, old_g = items
            column = lax.dynamic_slice_in_dim(table, gid, 1, 1)
            kappa_g = jnp.dot(column.T, flat, preferred_element_type=jnp.float32).reshape(NR, NT, NP)
            share = lax.dynamic_slice_in_dim(planck, gid, 1, 0)[0]
            fresh = sweep(energy_g, old_g, kappa_g, share * fourth)
            top = top + kappa_g * (fresh + 3.0 * share * fourth)
            bottom = bottom + 4.0 * kappa_g * share * cube
            return (top, bottom), fresh

        start = (jnp.zeros((NR, NT, NP), jnp.float32), jnp.zeros((NR, NT, NP), jnp.float32))
        (top, bottom), energy = lax.scan(one, start, (gids, energy, energy_old))
        temp = (heat_capacity * temp_old + top) / (heat_capacity + bottom)
    return energy, temp
```

```python
import jax
import jax.numpy as jnp
from jax import lax
from jax.experimental import pallas as pl
from jax.experimental.pallas import tpu as pltpu
from jax.sharding import PartitionSpec as P

ITERS = 3
HEAT = 2.0
REACH = 20.0


BF = jnp.bfloat16
F32 = jnp.float32
VMEM = pltpu.VMEM
SMEM = pltpu.SMEM


def vspec():
    return pl.BlockSpec(memory_space=VMEM)


def sspec():
    return pl.BlockSpec(memory_space=SMEM)


def swap_pairs(count, odd):
    pairs = []
    for i in range(odd, count - 1, 2):
        pairs += [(i, i + 1), (i + 1, i)]
    return pairs


def swap_halos(slabs):
    t1, t2, r1, r2 = slabs
    nt, nr = lax.axis_size("theta"), lax.axis_size("row")
    t2 = lax.ppermute(t2, "theta", swap_pairs(nt, 1))
    t1 = lax.ppermute(t1, "theta", swap_pairs(nt, 0))
    r2 = lax.ppermute(r2, "row", swap_pairs(nr, 1))
    r1 = lax.ppermute(r1, "row", swap_pairs(nr, 0))
    return t1, t2, r1, r2


def group_sum(x):
    x = x + lax.ppermute(x, "group", [(0, 1), (1, 0), (2, 3), (3, 2)])
    return x + lax.ppermute(x, "group", [(0, 2), (2, 0), (1, 3), (3, 1)])


def write_slabs(par, src, t1, t2, r1, r2):
    rows = src.shape[1]
    rp, tp = par[0], par[1]
    low = src[:, :, 0, :].astype(BF)
    high = src[:, :, src.shape[2] - 1, :].astype(BF)

    @pl.when(tp == 0)
    def _():
        t1[...] = high
        t2[...] = low

    @pl.when(tp == 1)
    def _():
        t1[...] = low
        t2[...] = high

    r1[...] = src[:, (rows - 1) * (1 - rp)].astype(BF)
    r2[...] = src[:, (rows - 1) * rp].astype(BF)


def slab_shapes(shape):
    g, r, t, p = shape
    return [
        jax.ShapeDtypeStruct((g, r, p), BF),
        jax.ShapeDtypeStruct((g, r, p), BF),
        jax.ShapeDtypeStruct((g, t, p), BF),
        jax.ShapeDtypeStruct((g, t, p), BF),
    ]


def pack_kernel(par, e, t1, t2, r1, r2):
    write_slabs(par, e, t1, t2, r1, r2)


def pack(par, e):
    return pl.pallas_call(
        pack_kernel,
        out_shape=slab_shapes(e.shape),
        in_specs=[sspec(), vspec()],
        out_specs=[vspec()] * 4,
        name="pack",
    )(par, e)


def kappa_kernel(par, tab, d0, d1, d2a, d2b, d3a, d3b, kap, t1, t2, r1, r2, wide):
    bins, rows = d0.shape[0], d0.shape[1]
    groups = kap.shape[0]
    for b in range(bins):
        wide[b] = d0[b].astype(F32)
        wide[bins + b] = d1[b].astype(F32)
        wide[2 * bins + b] = d2a[b].astype(F32) + d2b[b].astype(F32)
        wide[3 * bins + b] = d3a[b].astype(F32) + d3b[b].astype(F32)

    def one(g, carry):
        acc = tab[g] * wide[0]
        for b in range(1, 4 * bins):
            acc = acc + tab[b * groups + g] * wide[b]
        kap[g] = acc
        return carry

    lax.fori_loop(0, groups, one, 0)
    write_slabs(par, kap, t1, t2, r1, r2)


def kappa_call(par, tab, blocks, groups):
    shape = (groups,) + blocks[0].shape[1:]
    return pl.pallas_call(
        kappa_kernel,
        out_shape=[jax.ShapeDtypeStruct(shape, F32)] + slab_shapes(shape),
        in_specs=[sspec(), sspec()] + [vspec()] * 6,
        out_specs=[vspec()] * 5,
        scratch_shapes=[VMEM((4 * blocks[0].shape[0],) + blocks[0].shape[1:], F32)],
        name="kappa",
    )(par, tab, *blocks)


def face(ea, eb, ks):
    s = ea + eb
    return s / (0.75 * ks * s + jnp.abs(eb - ea))


def sweep_body(par, planck, e, eold, kap, temp4, eh, kh, enew, ksum, ssum, et, er, kt, kr, wlo):
    groups, rows, lat, _ = e.shape
    rp, tp = par[0], par[1]
    et[1 - tp] = eh[0][...].astype(F32)
    et[tp] = eh[1][...].astype(F32)
    er[1 - rp] = eh[2][...].astype(F32)
    er[rp] = eh[3][...].astype(F32)
    kt[1 - tp] = kh[0][...].astype(F32)
    kt[tp] = kh[1][...].astype(F32)
    kr[1 - rp] = kh[2][...].astype(F32)
    kr[rp] = kh[3][...].astype(F32)
    sub = lax.broadcasted_iota(jnp.int32, e.shape[2:], 0)
    first, last = sub == 0, sub == lat - 1
    ksum[...] = jnp.zeros_like(ksum)
    if ssum is not None:
        ssum[...] = jnp.zeros_like(ssum)

    def one(g, carry):
        share = planck[g]
        wlo[...] = face(e[g, :, 0, :], et[0, g], kap[g, :, 0, :] + kt[0, g])
        here, k = e[g, 0], kap[g, 0]
        below = er[0, g]
        w_below = face(here, below, k + kr[0, g])
        for r in range(rows):
            if r + 1 < rows:
                above, k_above = e[g, r + 1], kap[g, r + 1]
            else:
                above, k_above = er[1, g], kr[1, g]
            w_above = face(here, above, k + k_above)
            row = jnp.broadcast_to(et[1, g, pl.ds(r, 1), :], here.shape)
            krow = jnp.broadcast_to(kt[1, g, pl.ds(r, 1), :], here.shape)
            up = jnp.where(last, row, pltpu.roll(here, lat - 1, 0))
            k_up = jnp.where(last, krow, pltpu.roll(k, lat - 1, 0))
            w_up = face(here, up, k + k_up)
            row = jnp.broadcast_to(et[0, g, pl.ds(r, 1), :], here.shape)
            wrow = jnp.broadcast_to(wlo[pl.ds(r, 1), :], here.shape)
            down = jnp.where(first, row, pltpu.roll(here, 1, 0))
            w_down = jnp.where(first, wrow, pltpu.roll(w_up, 1, 0))
            lanes = here.shape[1]
            east = pltpu.roll(here, lanes - 1, 1)
            west = pltpu.roll(here, 1, 1)
            w_east = face(here, east, k + pltpu.roll(k, lanes - 1, 1))
            w_west = pltpu.roll(w_east, 1, 1)
            wsum = (w_below + w_above) + (w_up + w_down) + (w_east + w_west)
            esum = (w_below * below + w_above * above) + (w_up * up + w_down * down)
            esum = esum + (w_east * east + w_west * west)
            numer = eold[g, r] + k * (share * temp4[r]) + (REACH / 2) * esum
            fresh = numer / (1.0 + k + (REACH / 2) * wsum)
            enew[g, r] = fresh
            ksum[r] += k * fresh
            if ssum is not None:
                ssum[r] += k * share
            below, w_below = here, w_above
            here, k = above, k_above
        return carry

    lax.fori_loop(0, groups, one, 0)


def first_kernel(par, planck, e, kap, temp, *refs):
    eh, kh = refs[0:4], refs[4:8]
    enew, sums, t1, t2, r1, r2 = refs[8:14]
    temp4, et, er, kt, kr, wlo = refs[14:]
    t = temp[...]
    temp4[...] = t * t * t * t
    sweep_body(par, planck, e, e, kap, temp4, eh, kh, enew, sums.at[0], sums.at[1], et, er, kt, kr, wlo)
    write_slabs(par, enew, t1, t2, r1, r2)


def new_temp(told, t, ktot, stot):
    cube = t * t * t
    return (HEAT * told + ktot + 3.0 * stot * (cube * t)) / (HEAT + 4.0 * stot * cube)


def middle_kernel(par, planck, e, eold, kap, told, tprev, ktot, stot, *refs):
    eh, kh = refs[0:4], refs[4:8]
    enew, ksum, tnow, t1, t2, r1, r2 = refs[8:15]
    temp4, et, er, kt, kr, wlo = refs[15:]
    t = new_temp(told[...], tprev[...], ktot[...], stot[...])
    tnow[...] = t
    temp4[...] = t * t * t * t
    sweep_body(par, planck, e, eold, kap, temp4, eh, kh, enew, ksum, None, et, er, kt, kr, wlo)
    write_slabs(par, enew, t1, t2, r1, r2)


def last_kernel(par, planck, e, eold, kap, told, tprev, ktot, stot, *refs):
    eh, kh = refs[0:4], refs[4:8]
    enew, ksum, tnow = refs[8:11]
    temp4, et, er, kt, kr, wlo = refs[11:]
    t = new_temp(told[...], tprev[...], ktot[...], stot[...])
    tnow[...] = t
    temp4[...] = t * t * t * t
    sweep_body(par, planck, e, eold, kap, temp4, eh, kh, enew, ksum, None, et, er, kt, kr, wlo)


def sweep_scratch(shape):
    g, r, t, p = shape
    return [
        VMEM((r, t, p), F32),
        VMEM((2, g, r, p), F32),
        VMEM((2, g, t, p), F32),
        VMEM((2, g, r, p), F32),
        VMEM((2, g, t, p), F32),
        VMEM((r, p), F32),
    ]


def call(kernel, name, outs, args, shape):
    return pl.pallas_call(
        kernel,
        out_shape=outs,
        in_specs=[sspec(), sspec()] + [vspec()] * (len(args) - 2),
        out_specs=[vspec()] * len(outs),
        scratch_shapes=sweep_scratch(shape),
        cost_estimate=pl.CostEstimate(flops=10_000_000, bytes_accessed=3_000_000, transcendentals=0),
        name=name,
    )(*args)


def final_kernel(told, tprev, ktot, stot, out):
    out[...] = new_temp(told[...], tprev[...], ktot[...], stot[...])


def shards(dust, table, planck, energy_old, temp_old):
    groups = planck.shape[0]
    place = lax.axis_index("group")
    par = jnp.stack([lax.axis_index("row") % 2, lax.axis_index("theta") % 2]).astype(jnp.int32)
    shape = energy_old.shape
    full = jax.ShapeDtypeStruct(shape, F32)
    cell = jax.ShapeDtypeStruct(shape[1:], F32)

    eh = swap_halos(pack(par, energy_old))
    a = lax.ppermute(dust, "group", [(0, 1), (1, 0), (2, 3), (3, 2)])
    b = lax.ppermute(dust, "group", [(1, 2), (2, 1)])
    c = lax.ppermute(a, "group", [(1, 2), (2, 1)])
    d = lax.ppermute(b, "group", [(1, 0), (2, 3)])
    e = lax.ppermute(a, "group", [(1, 3), (2, 0)])
    left = place < 2
    sources = jnp.stack([place, place ^ 1, jnp.where(left, 2, 1), jnp.where(left, 3, 0)])
    mine = lax.dynamic_slice_in_dim(table, place * groups, groups, 1)
    tab = mine.reshape(4, -1, groups)[sources].astype(F32).reshape(-1)
    kap, *kslabs = kappa_call(par, tab, (dust, a, b, d, c, e), groups)
    kh = swap_halos(kslabs)

    sums = jax.ShapeDtypeStruct((2,) + shape[1:], F32)
    slabs = slab_shapes(shape)
    energy, part, *es = call(
        first_kernel, "sweep1", [full, sums] + slabs,
        (par, planck, energy_old, kap, temp_old, *eh, *kh), shape,
    )
    eh = swap_halos(es)
    both = group_sum(part)
    ktot, stot = both[0], both[1]
    energy, part, temp, *es = call(
        middle_kernel, "sweep2", [full, cell, cell] + slabs,
        (par, planck, energy, energy_old, kap, temp_old, temp_old, ktot, stot, *eh, *kh), shape,
    )
    eh = swap_halos(es)
    ktot = group_sum(part)
    energy, part, temp = call(
        last_kernel, "sweep3", [full, cell, cell],
        (par, planck, energy, energy_old, kap, temp_old, temp, ktot, stot, *eh, *kh), shape,
    )
    ktot = group_sum(part)
    temp = new_temp(temp_old, temp, ktot, stot)
    return energy, temp


def solution(mesh):
    return jax.shard_map(
        shards,
        mesh=mesh,
        in_specs=(
            P("group", "row", "theta", None),
            P(),
            P("group"),
            P("group", "row", "theta", None),
            P("row", "theta", None),
        ),
        out_specs=(P("group", "row", "theta", None), P("row", "theta", None)),
        check_vma=False,
    )
```

```python
import jax
import jax.numpy as jnp
from jax import lax
from jax.experimental import pallas as pl
from jax.experimental.pallas import tpu as pltpu
from jax.sharding import PartitionSpec as P

ITERS = 3
HEAT = 2.0
REACH = 20.0
SCALE = 2.0 / REACH


BF = jnp.bfloat16
F32 = jnp.float32
VMEM = pltpu.VMEM
SMEM = pltpu.SMEM

BINS = 8
OWN = 12
GROUPS = 24
ROWS = 8
LAT = 8
LANES = 128
TILES = GROUPS * ROWS
CELLS = TILES * LAT


def call(kernel, name, outs, args, smem=0, scratch=(), flops=1_000_000):
    specs = [pl.BlockSpec(memory_space=SMEM)] * smem
    specs += [pl.BlockSpec(memory_space=VMEM)] * (len(args) - smem)
    return pl.pallas_call(
        kernel,
        out_shape=outs,
        in_specs=specs,
        out_specs=[pl.BlockSpec(memory_space=VMEM)] * len(outs),
        scratch_shapes=list(scratch),
        cost_estimate=pl.CostEstimate(flops=flops, bytes_accessed=1_000_000, transcendentals=0),
        compiler_params=pltpu.CompilerParams(vmem_limit_bytes=16 << 20),
        name=name,
    )(*args)


def held(shape, dtype=F32):
    return VMEM(shape, dtype)


def keep(x):
    return pltpu.with_memory_space_constraint(x, VMEM)


def tile(i):
    return pl.ds(pl.multiple_of(i * LAT, LAT), LAT)


def pack_kernel(pos, planck, dust, eold, eown, pair, near, far):
    half = pos[0]
    mine, other = ROWS * half, ROWS * (1 - half)
    for b in range(BINS):
        for r in range(ROWS):
            near[tile(b * ROWS + r), :] = dust[tile(b * 2 * ROWS + mine + r), :]
            away = dust[tile(b * 2 * ROWS + other + r), :]
            far[tile(b * ROWS + r), :] = away
            pair[tile(b * ROWS + r), :] = away
    base = BINS * ROWS
    for g in range(OWN):
        for r in range(ROWS):
            pair[tile(base + g * ROWS + r), :] = eold[tile(g * 2 * ROWS + other + r), :].astype(BF)
            eown[tile(g * ROWS + r), :] = eold[tile(g * 2 * ROWS + mine + r), :]
    base += OWN * ROWS
    row = lax.broadcasted_iota(jnp.int32, (2 * LAT, LANES), 0)
    share = jnp.zeros((2 * LAT, LANES), F32)
    for g in range(OWN):
        share = jnp.where(row == g, planck[g], share)
    for i in range(3):
        piece = share.astype(BF)
        pair[pl.ds((base + 2 * i) * LAT, 2 * LAT), :] = piece
        share = share - piece.astype(F32)


def write_slabs(pos, src, at, t1, t2, r1, r2):
    part, tp = pos[0], pos[1]
    low = src[pl.ds(0, TILES, stride=LAT), :].astype(BF)
    high = src[pl.ds(LAT - 1, TILES, stride=LAT), :].astype(BF)
    rows = pl.ds(at, TILES)

    @pl.when(tp == 0)
    def _():
        t1[rows, :] = high
        t2[rows, :] = low

    @pl.when(tp == 1)
    def _():
        t1[rows, :] = low
        t2[rows, :] = high

    for g in range(0, GROUPS, 2):
        def edge(r):
            a = src[tile(g * ROWS + r), :]
            b = src[tile((g + 1) * ROWS + r), :]
            return jnp.concatenate([a, b], axis=0).astype(BF)

        r1[pl.ds(at + g * LAT, 2 * LAT), :] = edge((ROWS - 1) * (1 - part))
        r2[pl.ds(at + g * LAT, 2 * LAT), :] = edge((ROWS - 1) * part)


def kappa_kernel(pos, tab, planck, dust, eown, pair, near, far, kap, e, share, t1, t2, r1, r2, wide):
    half, place = pos[0], pos[2]
    slot = place % 2
    size = BINS * ROWS * LAT
    for b in range(BINS):
        for r in range(ROWS):
            wide[tile(b * ROWS + r), :] = dust[tile(b * 2 * ROWS + ROWS * half + r), :].astype(F32)
    wide[pl.ds(size, size), :] = pair[pl.ds(0, size), :].astype(F32)
    wide[pl.ds(2 * size, size), :] = near[...].astype(F32)
    wide[pl.ds(3 * size, size), :] = far[...].astype(F32)
    first = (place // 2) * GROUPS

    def one(g, carry):
        acc = [None] * ROWS
        for k in range(4):
            source = jnp.bitwise_xor(place, k)
            for b in range(BINS):
                t = SCALE * tab[(source * BINS + b) * 2 * GROUPS + first + g]
                for r in range(ROWS):
                    term = t * wide[tile((k * BINS + b) * ROWS + r), :]
                    acc[r] = term if acc[r] is None else acc[r] + term
        for r in range(ROWS):
            kap[tile(g * ROWS + r), :] = acc[r]
        return carry

    lax.fori_loop(0, GROUPS, one, 0)
    half_cells = OWN * ROWS * LAT
    e[pl.ds(pl.multiple_of(slot * half_cells, half_cells), half_cells), :] = eown[...]
    e[pl.ds(pl.multiple_of((1 - slot) * half_cells, half_cells), half_cells), :] = pair[pl.ds(size, half_cells), :].astype(F32)
    at = size + half_cells
    pieces = [pair[pl.ds(at + 2 * LAT * i, 2 * LAT), :].astype(F32) for i in range(3)]
    theirs = pieces[0] + pieces[1] + pieces[2]
    row = lax.broadcasted_iota(jnp.int32, (2 * LAT, LANES), 0)
    ours = jnp.zeros((2 * LAT, LANES), F32)
    for g in range(OWN):
        ours = jnp.where(row == g, planck[g], ours)
    share[slot] = ours
    share[1 - slot] = theirs
    write_slabs(pos, e, 0, t1, t2, r1, r2)
    write_slabs(pos, kap, TILES, t1, t2, r1, r2)


def face(ea, eb, c):
    s = ea + eb
    return s / (c * s + jnp.abs(eb - ea))


def unpack_halos(pos, slabs, at, t, r):
    part, tp = pos[0], pos[1]
    rows = pl.ds(at, TILES)
    t[1 - tp] = slabs[0][rows, :].astype(F32)
    t[tp] = slabs[1][rows, :].astype(F32)
    r[1 - part] = slabs[2][rows, :].astype(F32)
    r[part] = slabs[3][rows, :].astype(F32)


COEF = 0.75 / SCALE


def spread(row):
    return jnp.broadcast_to(row, (LAT, LANES))


def sweep_body(e, e01, kap, share, temp4, et, er, coefs, enew, ksum, wlo, first):
    up_c, east_c, above_c, below_c, low_c = coefs
    sub = lax.broadcasted_iota(jnp.int32, (LAT, LANES), 0)
    bottom, top = sub == 0, sub == LAT - 1
    ksum[...] = jnp.zeros_like(ksum)
    if first is not None:
        kt, kr, ssum, e01_out = first
        ssum[...] = jnp.zeros_like(ssum)

    def one(g, carry):
        base = g * ROWS
        part = g // OWN
        row_share = spread(share[part, pl.ds(g - part * OWN, 1), :])
        strip = pl.ds(pl.multiple_of(base * LAT, LAT), ROWS, stride=LAT)
        lows = tile(g)
        if first is not None:
            low_c[lows, :] = COEF * (kap[strip, :] + kt[0, lows, :])
            below_c[lows, :] = COEF * (kap[tile(base), :] + kr[0, lows, :])
        wlo[lows, :] = face(e[strip, :], et[0, lows, :], low_c[lows, :])
        here = e[tile(base), :]
        below = er[0, lows, :]
        w_below = face(here, below, below_c[lows, :])
        for r in range(ROWS):
            i = base + r
            k = kap[tile(i), :]
            if first is not None:
                krow = spread(kt[1, pl.ds(i, 1), :])
                k_up = jnp.where(top, krow, pltpu.roll(k, LAT - 1, 0))
                k_above = kap[tile(i + 1), :] if r + 1 < ROWS else kr[1, lows, :]
                c_up = COEF * (k + k_up)
                c_east = COEF * (k + pltpu.roll(k, LANES - 1, 1))
                c_above = COEF * (k + k_above)
                up_c[tile(i), :] = c_up
                east_c[tile(i), :] = c_east
                above_c[tile(i), :] = c_above
                old = SCALE * here
                e01_out[tile(i), :] = old
                ssum[tile(r), :] += k * row_share
            else:
                c_up, c_east, c_above = up_c[tile(i), :], east_c[tile(i), :], above_c[tile(i), :]
                old = e01[tile(i), :]
            above = e[tile(i + 1), :] if r + 1 < ROWS else er[1, lows, :]
            w_above = face(here, above, c_above)
            up = jnp.where(top, spread(et[1, pl.ds(i, 1), :]), pltpu.roll(here, LAT - 1, 0))
            w_up = face(here, up, c_up)
            down = jnp.where(bottom, spread(et[0, pl.ds(i, 1), :]), pltpu.roll(here, 1, 0))
            w_down = jnp.where(bottom, spread(wlo[pl.ds(i, 1), :]), pltpu.roll(w_up, 1, 0))
            east = pltpu.roll(here, LANES - 1, 1)
            west = pltpu.roll(here, 1, 1)
            w_east = face(here, east, c_east)
            w_west = pltpu.roll(w_east, 1, 1)
            wsum = (w_below + w_above) + (w_up + w_down) + (w_east + w_west)
            esum = (w_below * below + w_above * above) + (w_up * up + w_down * down)
            esum = esum + (w_east * east + w_west * west)
            numer = old + k * (row_share * temp4[tile(r), :]) + esum
            fresh = numer / (SCALE + k + wsum)
            enew[tile(i), :] = fresh
            ksum[tile(r), :] += k * fresh
            below, w_below, here = here, w_above, above
        return carry

    lax.fori_loop(0, GROUPS, one, 0)


def own_rows(pos, ref):
    n = ROWS * LAT
    return ref[pl.ds(pl.multiple_of(pos[0] * n, n), n), :]


def first_kernel(pos, e, kap, share, told, h0, h1, h2, h3, *refs):
    enew, sums, e01, up_c, east_c, above_c, below_c, low_c, t1, t2, r1, r2 = refs[:12]
    temp4, et, er, kt, kr, wlo = refs[12:]
    slabs = (h0, h1, h2, h3)
    unpack_halos(pos, slabs, 0, et, er)
    unpack_halos(pos, slabs, TILES, kt, kr)
    t = own_rows(pos, told)
    temp4[...] = t * t * t * t
    n = ROWS * LAT
    first = (kt, kr, sums.at[pl.ds(n, n)], e01)
    coefs = (up_c, east_c, above_c, below_c, low_c)
    sweep_body(e, None, kap, share, temp4, et, er, coefs, enew, sums.at[pl.ds(0, n)], wlo, first)
    write_slabs(pos, enew, 0, t1, t2, r1, r2)


def terms(told, t, stot):
    cube = t * t * t
    return HEAT * told + 3.0 * stot * (cube * t), HEAT + 4.0 * stot * cube


def middle_kernel(pos, e, e01, kap, share, told, sums, got, up_c, east_c, above_c, below_c, low_c, h0, h1, h2, h3, *refs):
    enew, ksum, tnow, stot, t1, t2, r1, r2 = refs[:8]
    temp4, et, er, wlo = refs[8:]
    unpack_halos(pos, (h0, h1, h2, h3), 0, et, er)
    n = ROWS * LAT
    both = (sums[...] + got[...]) / SCALE
    s = both[n:]
    stot[...] = s
    t = own_rows(pos, told)
    up, down = terms(t, t, s)
    t = (up + both[:n]) / down
    tnow[...] = t
    temp4[...] = t * t * t * t
    coefs = (up_c, east_c, above_c, below_c, low_c)
    sweep_body(e, e01, kap, share, temp4, et, er, coefs, enew, ksum, wlo, None)
    write_slabs(pos, enew, 0, t1, t2, r1, r2)


def last_kernel(pos, e, e01, kap, share, told, tprev, stot, part, got, up_c, east_c, above_c, below_c, low_c, h0, h1, h2, h3, *refs):
    eown, send, ksum = refs[:3]
    temp4, et, er, wlo, enew = refs[3:]
    unpack_halos(pos, (h0, h1, h2, h3), 0, et, er)
    s = stot[...]
    old = own_rows(pos, told)
    up, down = terms(old, tprev[...], s)
    t = (up + (part[...] + got[...]) / SCALE) / down
    temp4[...] = t * t * t * t
    coefs = (up_c, east_c, above_c, below_c, low_c)
    sweep_body(e, e01, kap, share, temp4, et, er, coefs, enew, ksum, wlo, None)
    slot = pos[2] % 2
    n, m = ROWS * LAT, OWN * ROWS * LAT
    eown[...] = enew[pl.ds(pl.multiple_of(slot * m, m), m), :]
    send[pl.ds(0, m), :] = enew[pl.ds(pl.multiple_of((1 - slot) * m, m), m), :]
    up, down = terms(old, t, s)
    send[pl.ds(m, n), :] = ksum[...]
    send[pl.ds(m + n, n), :] = up
    send[pl.ds(m + 2 * n, n), :] = down


def join_kernel(pos, eown, send, pair, near, far, energy, temp):
    half = pos[0]
    n, m = ROWS * LAT, OWN * ROWS * LAT
    for g in range(OWN):
        src = pl.ds(g * n, n)
        energy[pl.ds(pl.multiple_of((2 * g + half) * n, n), n), :] = eown[src, :]
        energy[pl.ds(pl.multiple_of((2 * g + 1 - half) * n, n), n), :] = pair[src, :]
    k, up, down = pl.ds(m, n), pl.ds(m + n, n), pl.ds(m + 2 * n, n)
    temp[pl.ds(pl.multiple_of(half * n, n), n), :] = (send[up, :] + (send[k, :] + near[...]) / SCALE) / send[down, :]
    temp[pl.ds(pl.multiple_of((1 - half) * n, n), n), :] = (pair[up, :] + (pair[k, :] + far[...]) / SCALE) / pair[down, :]


def theta_pairs(count, odd):
    return [p for i in range(odd, count - 1, 2) for p in ((i, i + 1), (i + 1, i))]


def row_pairs(rows, odd):
    def device(chain, position):
        row, part = position // 2, position % 2
        return row * 4 + 2 * chain + (part ^ (row & 1))

    pairs = []
    for chain in range(2):
        for i in range(odd, 2 * rows - 1, 2):
            a, b = device(chain, i), device(chain, i + 1)
            pairs += [(a, b), (b, a)]
    return pairs


def xor(x, k):
    return lax.ppermute(x, "group", [(i, i ^ k) for i in range(4)])


def swap_halos(slabs):
    t1, t2, r1, r2 = slabs
    nt, nr = lax.axis_size("theta"), lax.axis_size("row")
    t2 = lax.ppermute(t2, "theta", theta_pairs(nt, 1))
    t1 = lax.ppermute(t1, "theta", theta_pairs(nt, 0))
    r2 = lax.ppermute(r2, ("row", "group"), row_pairs(nr, 1))
    r1 = lax.ppermute(r1, ("row", "group"), row_pairs(nr, 0))
    return tuple(keep(x) for x in (t1, t2, r1, r2))


def shards(dust, table, planck, energy_old, temp_old):
    place = lax.axis_index("group")
    row = lax.axis_index("row")
    pos = jnp.stack([(place ^ row) & 1, lax.axis_index("theta") & 1, place, row]).astype(jnp.int32)
    dust = dust.reshape(-1, LANES)
    energy_old = energy_old.reshape(-1, LANES)
    told = temp_old.reshape(-1, LANES)
    tab = table.astype(F32).reshape(-1)
    size, half_cells, n = BINS * ROWS * LAT, OWN * ROWS * LAT, ROWS * LAT
    slabs = [held((TILES, LANES), BF)] * 4
    halo = VMEM((2, TILES, LANES), F32)
    scratch = [VMEM((n, LANES), F32), halo, halo]
    wlo = VMEM((TILES, LANES), F32)
    full = held((CELLS, LANES))
    coefs = [full, full, full, held((TILES, LANES)), held((TILES, LANES))]

    eown, pair, near, far = call(
        pack_kernel, "pack",
        [held((half_cells, LANES)), held((size + half_cells + 6 * LAT, LANES), BF), held((size, LANES), BF), held((size, LANES), BF)],
        (pos, planck, dust, energy_old), smem=2,
    )
    pair, near, far = xor(pair, 1), xor(near, 2), xor(far, 3)
    kap, e, share, *both = call(
        kappa_kernel, "kappa",
        [full, full, held((2, 2 * LAT, LANES))] + [held((2 * TILES, LANES), BF)] * 4,
        (pos, tab, planck, dust, keep(eown), keep(pair), keep(near), keep(far)), smem=3,
        scratch=[VMEM((4 * size, LANES), F32)], flops=5_000_000,
    )
    halos = swap_halos(both)
    kap, share = keep(kap), keep(share)
    e, sums, e01, *rest = call(
        first_kernel, "sweep1", [full, held((2 * n, LANES)), full] + coefs + slabs,
        (pos, keep(e), kap, share, told, *halos), smem=1,
        scratch=scratch + [halo, halo, wlo], flops=10_000_000,
    )
    coef = [keep(x) for x in rest[:5]]
    halos = swap_halos(rest[5:])
    got = xor(sums, 2)
    e01 = keep(e01)
    e, part, temp, stot, *rest = call(
        middle_kernel, "sweep2", [full, held((n, LANES)), held((n, LANES)), held((n, LANES))] + slabs,
        (pos, keep(e), e01, kap, share, told, keep(sums), keep(got), *coef, *halos), smem=1,
        scratch=scratch + [wlo], flops=10_000_000,
    )
    halos = swap_halos(rest)
    got = xor(part, 2)
    eown, send, part = call(
        last_kernel, "sweep3", [held((half_cells, LANES)), held((half_cells + 3 * n, LANES)), held((n, LANES))],
        (pos, keep(e), e01, kap, share, told, keep(temp), keep(stot), keep(part), keep(got), *coef, *halos), smem=1,
        scratch=scratch + [wlo, VMEM((CELLS, LANES), F32)], flops=10_000_000,
    )
    pair, near, far = xor(send, 1), xor(part, 2), xor(part, 3)
    energy, temp = call(
        join_kernel, "join",
        [jax.ShapeDtypeStruct((2 * half_cells, LANES), F32), jax.ShapeDtypeStruct((2 * n, LANES), F32)],
        (pos, keep(eown), keep(send), keep(pair), keep(near), keep(far)), smem=1,
    )
    return energy.reshape(OWN, 2 * ROWS, LAT, LANES), temp.reshape(2 * ROWS, LAT, LANES)


def solution(mesh):
    return jax.shard_map(
        shards,
        mesh=mesh,
        in_specs=(
            P("group", "row", "theta", None),
            P(),
            P("group"),
            P("group", "row", "theta", None),
            P("row", "theta", None),
        ),
        out_specs=(P("group", "row", "theta", None), P("row", "theta", None)),
        check_vma=False,
    )
```

```python
import jax
import jax.numpy as jnp
from jax import lax
from jax.experimental import pallas as pl
from jax.experimental.pallas import tpu as pltpu
from jax.sharding import PartitionSpec as P


HEAT = 2.0
REACH = 20.0
SCALE = 2.0 / REACH


BF = jnp.bfloat16
F32 = jnp.float32
VMEM = pltpu.VMEM
SMEM = pltpu.SMEM

BINS = 8
OWN = 12
GROUPS = 24
ROWS = 8
LAT = 8
LANES = 128
TILES = GROUPS * ROWS
CELLS = TILES * LAT


def call(kernel, outs, args, smem=0, scratch=(), flops=1_000_000, space=VMEM):
    specs = [pl.BlockSpec(memory_space=SMEM)] * smem
    specs += [pl.BlockSpec(memory_space=space)] * (len(args) - smem)
    return pl.pallas_call(
        kernel,
        out_shape=outs,
        in_specs=specs,
        out_specs=[pl.BlockSpec(memory_space=VMEM)] * len(outs),
        scratch_shapes=list(scratch),
        cost_estimate=pl.CostEstimate(flops=flops, bytes_accessed=1_000_000, transcendentals=0),
        compiler_params=pltpu.CompilerParams(vmem_limit_bytes=16 << 20),
    )(*args)


def held(shape, dtype=F32):
    return VMEM(shape, dtype)


def keep(x):
    return pltpu.with_memory_space_constraint(x, VMEM)


def tile(i):
    return pl.ds(pl.multiple_of(i * LAT, LAT), LAT)


UNROLL = 4
SIZE = BINS * ROWS * LAT
PART = OWN * ROWS * LAT
N = ROWS * LAT
COEF = 0.75 / SCALE


def pack_kernel(pos, planck, dust, eold, eown, pair, near, far, stage, shares, sems):
    half = pos[0]
    mine = pl.ds(pl.multiple_of(N * half, N), N)
    other = pl.ds(pl.multiple_of(N * (1 - half), N), N)
    copies = [
        pltpu.make_async_copy(dust.at[:, other, :], far, sems.at[0]),
        pltpu.make_async_copy(eold.at[:, other, :], stage, sems.at[1]),
        pltpu.make_async_copy(dust.at[:, mine, :], near, sems.at[2]),
        pltpu.make_async_copy(eold.at[:, mine, :], eown, sems.at[3]),
        pltpu.make_async_copy(planck, shares, sems.at[4]),
    ]
    for copy in copies:
        copy.start()
    copies[0].wait()
    for b in range(BINS):
        pair[pl.ds(b * N, N), :] = far[b]
    copies[1].wait()
    for g in range(OWN):
        pair[pl.ds(SIZE + g * N, N), :] = stage[g].astype(BF)
    copies[4].wait()
    row = lax.broadcasted_iota(jnp.int32, (2 * LAT, LANES), 0)
    share = jnp.zeros((2 * LAT, LANES), F32)
    for g in range(OWN):
        share = jnp.where(row == g, shares[g], share)
    for i in range(3):
        piece = share.astype(BF)
        pair[pl.ds(SIZE + PART + 2 * i * LAT, 2 * LAT), :] = piece
        share = share - piece.astype(F32)
    copies[2].wait()
    copies[3].wait()


def write_slabs(pos, src, at, t1, t2, r1, r2):
    part, tp = pos[0], pos[1]
    low = src[pl.ds(0, TILES, stride=LAT), :].astype(BF)
    high = src[pl.ds(LAT - 1, TILES, stride=LAT), :].astype(BF)
    rows = pl.ds(at, TILES)

    @pl.when(tp == 0)
    def _():
        t1[rows, :] = high
        t2[rows, :] = low

    @pl.when(tp == 1)
    def _():
        t1[rows, :] = low
        t2[rows, :] = high

    for g in range(0, GROUPS, 2):
        def edge(r):
            a = src[tile(g * ROWS + r), :]
            b = src[tile((g + 1) * ROWS + r), :]
            return jnp.concatenate([a, b], axis=0).astype(BF)

        r1[pl.ds(at + g * LAT, 2 * LAT), :] = edge((ROWS - 1) * (1 - part))
        r2[pl.ds(at + g * LAT, 2 * LAT), :] = edge((ROWS - 1) * part)


def gather_bins(tab, wide, place, blocks, g, acc):
    first = (place // 2) * GROUPS
    for j, k in enumerate(blocks):
        source = jnp.bitwise_xor(place, k)
        for b in range(BINS):
            t = SCALE * tab[(source * BINS + b) * 2 * GROUPS + first + g]
            for r in range(ROWS):
                term = t * wide[tile((j * BINS + b) * ROWS + r), :]
                acc[r] = term if acc[r] is None else acc[r] + term
    return acc


def early_kernel(pos, tab, mine, near, far, kap, wide):
    place = pos[2]
    for j, block in enumerate((mine, near, far)):
        for b in range(BINS):
            wide[pl.ds(j * SIZE + b * N, N), :] = block[b].astype(F32)

    def one(g, carry):
        acc = gather_bins(tab, wide, place, (0, 2, 3), g, [None] * ROWS)
        for r in range(ROWS):
            kap[tile(g * ROWS + r), :] = acc[r]
        return carry

    lax.fori_loop(0, GROUPS, one, 0, unroll=2)


def late_kernel(pos, tab, planck, part, eown, pair, kap, e, share, t1, t2, r1, r2, wide):
    place = pos[2]
    slot = place % 2
    wide[...] = pair[pl.ds(0, SIZE), :].astype(F32)

    def one(g, carry):
        acc = [part[tile(g * ROWS + r), :] for r in range(ROWS)]
        acc = gather_bins(tab, wide, place, (1,), g, acc)
        for r in range(ROWS):
            kap[tile(g * ROWS + r), :] = acc[r]
        return carry

    lax.fori_loop(0, GROUPS, one, 0, unroll=2)
    theirs = pl.multiple_of((1 - slot) * PART, PART)
    mine = pl.multiple_of(slot * PART, PART)
    for g in range(OWN):
        e[pl.ds(mine + g * N, N), :] = eown[g]
    e[pl.ds(theirs, PART), :] = pair[pl.ds(SIZE, PART), :].astype(F32)
    at = SIZE + PART
    pieces = [pair[pl.ds(at + 2 * LAT * i, 2 * LAT), :].astype(F32) for i in range(3)]
    row = lax.broadcasted_iota(jnp.int32, (2 * LAT, LANES), 0)
    ours = jnp.zeros((2 * LAT, LANES), F32)
    for g in range(OWN):
        ours = jnp.where(row == g, planck[g], ours)
    share[slot] = ours
    share[1 - slot] = pieces[0] + pieces[1] + pieces[2]
    write_slabs(pos, e, 0, t1, t2, r1, r2)
    write_slabs(pos, kap, TILES, t1, t2, r1, r2)


def face(ea, eb, c):
    d = eb - ea
    w = 1.0 / (c + jnp.abs(d) / (ea + eb))
    return w, w * d


def spread(row):
    return jnp.broadcast_to(row, (LAT, LANES))


def share_of(share, g):
    part = g // OWN
    return spread(share[part, pl.ds(g - part * OWN, 1), :])


def inner_body(e, coefs, flux, weight, prepare):
    top = lax.broadcasted_iota(jnp.int32, (LAT, LANES), 0) == LAT - 1

    def one(g, carry):
        base = g * ROWS
        tiles = [e[tile(base + r), :] for r in range(ROWS)]
        coef = prepare(g, base, tiles) if prepare else [[c[tile(base + r), :] for c in coefs] for r in range(ROWS)]
        ws, fs = [], []
        for r in range(ROWS):
            here = tiles[r]
            c_up, c_east, c_above = coef[r]
            w_up, f_up = face(here, pltpu.roll(here, LAT - 1, 0), c_up)
            w_up, f_up = jnp.where(top, 0.0, w_up), jnp.where(top, 0.0, f_up)
            w_east, f_east = face(here, pltpu.roll(here, LANES - 1, 1), c_east)
            w = (w_up + pltpu.roll(w_up, 1, 0)) + (w_east + pltpu.roll(w_east, 1, 1))
            f = (f_up - pltpu.roll(f_up, 1, 0)) + (f_east - pltpu.roll(f_east, 1, 1))
            if r > 0:
                w, f = w + w_below, f - f_below
            if r + 1 < ROWS:
                w_below, f_below = face(here, tiles[r + 1], c_above)
                w, f = w + w_below, f + f_below
            ws.append(w)
            fs.append(f)
        for r in range(ROWS):
            weight[tile(base + r), :] = ws[r]
            flux[tile(base + r), :] = fs[r]
        return carry

    lax.fori_loop(0, GROUPS, one, 0, unroll=UNROLL)


def inner_first(pos, e, kap, share, flux, weight, up_c, east_c, above_c, e01, ssum):
    ssum[...] = jnp.zeros_like(ssum)

    def prepare(g, base, tiles):
        ks = [kap[tile(base + r), :] for r in range(ROWS)]
        sums = [ssum[tile(r), :] for r in range(ROWS)]
        share_row = share_of(share, g)
        out = []
        for r in range(ROWS):
            k = ks[r]
            c_up, c_east = COEF * (k + pltpu.roll(k, LAT - 1, 0)), COEF * (k + pltpu.roll(k, LANES - 1, 1))
            out.append((c_up, c_east, COEF * (k + ks[r + 1]) if r + 1 < ROWS else None))
        for r in range(ROWS):
            i = base + r
            up_c[tile(i), :], east_c[tile(i), :] = out[r][:2]
            if r + 1 < ROWS:
                above_c[tile(i), :] = out[r][2]
            e01[tile(i), :] = SCALE * tiles[r]
            ssum[tile(r), :] = sums[r] + ks[r] * share_row
        return out

    inner_body(e, None, flux, weight, prepare)


def inner_next(pos, e, up_c, east_c, above_c, flux, weight):
    inner_body(e, (up_c, east_c, above_c), flux, weight, None)


def unpack_halos(pos, slabs, at, halo):
    part, tp = pos[0], pos[1]
    rows = pl.ds(at, TILES)
    halo[1 - tp] = slabs[0][rows, :].astype(F32)
    halo[tp] = slabs[1][rows, :].astype(F32)
    halo[3 - part] = slabs[2][rows, :].astype(F32)
    halo[2 + part] = slabs[3][rows, :].astype(F32)


def outer_body(e, e01, kap, share, temp4, halo, edge, flux, weight, enew, ksum, numer, denom):
    def one(g, carry):
        base = g * ROWS
        row_share = share_of(share, g)
        refs = (e, kap, weight, flux, e01)
        rows = [[x[tile(base + r), :] for x in refs] + [temp4[tile(r), :]] for r in range(ROWS)]
        ends = {at: (halo[j, tile(g), :], edge[j, tile(g), :]) for j, at in ((2, 0), (3, ROWS - 1))}
        out = []
        for r in range(ROWS):
            here, k, w, f, old, t4 = rows[r]
            if r in ends:
                w_out, f_out = face(here, *ends[r])
                w, f = w + w_out, f + f_out
            out.append((old + k * (row_share * t4) + (here * w + f), SCALE + k + w))
        for r in range(ROWS):
            numer[tile(base + r), :], denom[tile(base + r), :] = out[r]
        return carry

    lax.fori_loop(0, GROUPS, one, 0, unroll=UNROLL)
    for j, at in ((0, 0), (1, LAT - 1)):
        strip = pl.ds(at, TILES, stride=LAT)
        out = halo[j]
        w, _ = face(e[strip, :], out, edge[j])
        numer[strip, :] = numer[strip, :] + w * out
        denom[strip, :] = denom[strip, :] + w

    def two(g, sums):
        at = [tile(g * ROWS + r) for r in range(ROWS)]
        fresh = [numer[i, :] / denom[i, :] for i in at]
        sums = tuple(sums[r] + kap[at[r], :] * fresh[r] for r in range(ROWS))
        for r in range(ROWS):
            enew[at[r], :] = fresh[r]
        return sums

    sums = lax.fori_loop(0, GROUPS, two, (jnp.zeros((LAT, LANES), F32),) * ROWS, unroll=UNROLL)
    for r in range(ROWS):
        ksum[tile(r), :] = sums[r]


def own_rows(pos, ref):
    return ref[pl.ds(pl.multiple_of(pos[0] * N, N), N), :]


def terms(told, t, stot):
    cube = t * t * t
    return HEAT * told + 3.0 * stot * (cube * t), HEAT + 4.0 * stot * cube


def outer_first(pos, e, e01, kap, share, told, ssum, flux, weight, h0, h1, h2, h3, *refs):
    enew, sums, edge, t1, t2, r1, r2 = refs[:7]
    temp4, halo, numer, denom = refs[7:]
    slabs = (h0, h1, h2, h3)
    unpack_halos(pos, slabs, TILES, halo)
    for j, at in ((0, 0), (1, LAT - 1)):
        edge[j] = COEF * (kap[pl.ds(at, TILES, stride=LAT), :] + halo[j])
    for g in range(GROUPS):
        for j, at in ((2, 0), (3, ROWS - 1)):
            edge[j, tile(g), :] = COEF * (kap[tile(g * ROWS + at), :] + halo[j, tile(g), :])
    unpack_halos(pos, slabs, 0, halo)
    t = own_rows(pos, told)
    temp4[...] = t * t * t * t
    outer_body(e, e01, kap, share, temp4, halo, edge, flux, weight, enew, sums.at[pl.ds(0, N)], numer, denom)
    sums[pl.ds(N, N), :] = ssum[...]
    write_slabs(pos, enew, 0, t1, t2, r1, r2)


def outer_middle(pos, e, e01, kap, share, told, sums, got, edge, flux, weight, h0, h1, h2, h3, *refs):
    enew, ksum, tnow, stot, t1, t2, r1, r2 = refs[:8]
    temp4, halo, numer, denom = refs[8:]
    unpack_halos(pos, (h0, h1, h2, h3), 0, halo)
    both = (sums[...] + got[...]) / SCALE
    s = both[N:]
    stot[...] = s
    t = own_rows(pos, told)
    up, down = terms(t, t, s)
    t = (up + both[:N]) / down
    tnow[...] = t
    temp4[...] = t * t * t * t
    outer_body(e, e01, kap, share, temp4, halo, edge, flux, weight, enew, ksum, numer, denom)
    write_slabs(pos, enew, 0, t1, t2, r1, r2)


def outer_last(pos, e, e01, kap, share, told, tprev, stot, part, got, edge, flux, weight, h0, h1, h2, h3, *refs):
    eown, send, ksum = refs[:3]
    temp4, halo, numer, denom, enew = refs[3:]
    unpack_halos(pos, (h0, h1, h2, h3), 0, halo)
    s = stot[...]
    old = own_rows(pos, told)
    up, down = terms(old, tprev[...], s)
    t = (up + (part[...] + got[...]) / SCALE) / down
    temp4[...] = t * t * t * t
    outer_body(e, e01, kap, share, temp4, halo, edge, flux, weight, enew, ksum, numer, denom)
    slot = pos[2] % 2
    eown[...] = enew[pl.ds(pl.multiple_of(slot * PART, PART), PART), :]
    send[pl.ds(0, PART), :] = enew[pl.ds(pl.multiple_of((1 - slot) * PART, PART), PART), :]
    up, down = terms(old, t, s)
    send[pl.ds(PART, N), :] = ksum[...]
    send[pl.ds(PART + N, N), :] = up
    send[pl.ds(PART + 2 * N, N), :] = down


def join_kernel(pos, eown, send, pair, near, far, energy, temp):
    half = pos[0]
    for g in range(OWN):
        src = pl.ds(g * N, N)
        energy[pl.ds(pl.multiple_of((2 * g + half) * N, N), N), :] = eown[src, :]
        energy[pl.ds(pl.multiple_of((2 * g + 1 - half) * N, N), N), :] = pair[src, :]
    k, up, down = pl.ds(PART, N), pl.ds(PART + N, N), pl.ds(PART + 2 * N, N)
    temp[pl.ds(pl.multiple_of(half * N, N), N), :] = (send[up, :] + (send[k, :] + near[...]) / SCALE) / send[down, :]
    temp[pl.ds(pl.multiple_of((1 - half) * N, N), N), :] = (pair[up, :] + (pair[k, :] + far[...]) / SCALE) / pair[down, :]


def theta_pairs(count, odd):
    return [p for i in range(odd, count - 1, 2) for p in ((i, i + 1), (i + 1, i))]


def row_pairs(rows, odd):
    def device(chain, position):
        row, part = position // 2, position % 2
        return row * 4 + 2 * chain + (part ^ (row & 1))

    pairs = []
    for chain in range(2):
        for i in range(odd, 2 * rows - 1, 2):
            a, b = device(chain, i), device(chain, i + 1)
            pairs += [(a, b), (b, a)]
    return pairs


def xor(x, k):
    return lax.ppermute(x, "group", [(i, i ^ k) for i in range(4)])


def swap_halos(slabs, part=None):
    t1, t2, r1, r2 = slabs
    nt, nr = lax.axis_size("theta"), lax.axis_size("row")
    t2 = lax.ppermute(t2, "theta", theta_pairs(nt, 1))
    part = part if part is None else keep(xor(part, 2))
    t1 = lax.ppermute(t1, "theta", theta_pairs(nt, 0))
    r2 = lax.ppermute(r2, ("row", "group"), row_pairs(nr, 1))
    r1 = lax.ppermute(r1, ("row", "group"), row_pairs(nr, 0))
    return tuple(keep(x) for x in (t1, t2, r1, r2)), part


def shards(dust, table, planck, energy_old, temp_old):
    place = lax.axis_index("group")
    row = lax.axis_index("row")
    pos = jnp.stack([(place ^ row) & 1, lax.axis_index("theta") & 1, place, row]).astype(jnp.int32)
    dust = dust.reshape(BINS, 2 * N, LANES)
    energy_old = energy_old.reshape(OWN, 2 * N, LANES)
    told = temp_old.reshape(-1, LANES)
    tab = table.astype(F32).reshape(-1)
    slabs = [held((TILES, LANES), BF)] * 4
    scratch = [VMEM((N, LANES), F32), VMEM((4, TILES, LANES), F32), VMEM((CELLS, LANES), F32), VMEM((CELLS, LANES), F32)]
    full = held((CELLS, LANES))
    sheet = held((N, LANES))
    block = held((BINS, N, LANES), BF)

    eown, pair, mine, far = call(
        pack_kernel,
        [held((OWN, N, LANES)), held((SIZE + PART + 6 * LAT, LANES), BF), block, block],
        (pos, *(pltpu.with_memory_space_constraint(x, pltpu.HBM) for x in (planck, dust, energy_old))), smem=1, space=pl.ANY,
        scratch=[VMEM((OWN, N, LANES), F32), SMEM(planck.shape, F32), pltpu.SemaphoreType.DMA((5,))],
    )
    far = xor(far, 3)
    near = xor(mine, 2)
    pair = xor(pair, 1)
    early, = call(
        early_kernel, [full], (pos, tab, keep(mine), keep(near), keep(far)), smem=2,
        scratch=[VMEM((3 * SIZE, LANES), F32)], flops=20_000_000,
    )
    kap, e, share, *both = call(
        late_kernel,
        [full, full, held((2, 2 * LAT, LANES))] + [held((2 * TILES, LANES), BF)] * 4,
        (pos, tab, planck, keep(early), keep(eown), keep(pair)), smem=3,
        scratch=[VMEM((SIZE, LANES), F32)], flops=5_000_000,
    )
    kap, share, e = keep(kap), keep(share), keep(e)
    halos, _ = swap_halos(both)
    flux, weight, *coefs, e01, ssum = call(
        inner_first, [full] * 6 + [sheet], (pos, e, kap, share), smem=1, flops=20_000_000,
    )
    coefs = [keep(x) for x in coefs]
    e01 = keep(e01)
    e, sums, edge, *rest = call(
        outer_first, [full, held((2 * N, LANES)), held((4, TILES, LANES))] + slabs,
        (pos, e, e01, kap, share, told, keep(ssum), keep(flux), keep(weight), *halos), smem=1,
        scratch=scratch, flops=5_000_000,
    )
    e, edge, sums = keep(e), keep(edge), keep(sums)
    halos, got = swap_halos(rest, sums)
    flux, weight = call(inner_next, [full] * 2, (pos, e, *coefs), smem=1, flops=20_000_000)
    e, part, temp, stot, *rest = call(
        outer_middle, [full, sheet, sheet, sheet] + slabs,
        (pos, e, e01, kap, share, told, sums, got, edge, keep(flux), keep(weight), *halos), smem=1,
        scratch=scratch, flops=5_000_000,
    )
    e, part = keep(e), keep(part)
    halos, got = swap_halos(rest, part)
    flux, weight = call(inner_next, [full] * 2, (pos, e, *coefs), smem=1, flops=20_000_000)
    eown, send, part = call(
        outer_last, [held((PART, LANES)), held((PART + 3 * N, LANES)), sheet],
        (pos, e, e01, kap, share, told, keep(temp), keep(stot), part, got, edge, keep(flux), keep(weight), *halos), smem=1,
        scratch=scratch + [VMEM((CELLS, LANES), F32)], flops=5_000_000,
    )
    pair = xor(send, 1)
    far = xor(part, 3)
    near = xor(part, 2)
    energy, temp = call(
        join_kernel,
        [jax.ShapeDtypeStruct((2 * PART, LANES), F32), jax.ShapeDtypeStruct((2 * N, LANES), F32)],
        (pos, keep(eown), keep(send), keep(pair), keep(near), keep(far)), smem=1,
    )
    return energy.reshape(OWN, 2 * ROWS, LAT, LANES), temp.reshape(2 * ROWS, LAT, LANES)


def solution(mesh):
    return jax.shard_map(
        shards,
        mesh=mesh,
        in_specs=(
            P("group", "row", "theta", None),
            P(),
            P("group"),
            P("group", "row", "theta", None),
            P("row", "theta", None),
        ),
        out_specs=(P("group", "row", "theta", None), P("row", "theta", None)),
        check_vma=False,
    )
```

```python
import jax
import jax.numpy as jnp
from jax import lax
from jax.experimental import pallas as pl
from jax.experimental.pallas import tpu as pltpu
from jax.sharding import PartitionSpec as P


HEAT = 2.0
REACH = 20.0
SCALE = 2.0 / REACH


BF = jnp.bfloat16
F32 = jnp.float32
VMEM = pltpu.VMEM
SMEM = pltpu.SMEM

BINS = 8
OWN = 12
GROUPS = 24
ROWS = 8
LAT = 8
LANES = 128
TILES = GROUPS * ROWS
CELLS = TILES * LAT


def call(kernel, outs, args, smem=0, scratch=(), flops=1_000_000, space=VMEM):
    specs = [pl.BlockSpec(memory_space=SMEM)] * smem
    specs += [pl.BlockSpec(memory_space=space)] * (len(args) - smem)
    return pl.pallas_call(
        kernel,
        out_shape=outs,
        in_specs=specs,
        out_specs=[pl.BlockSpec(memory_space=VMEM)] * len(outs),
        scratch_shapes=list(scratch),
        cost_estimate=pl.CostEstimate(flops=flops, bytes_accessed=1_000_000, transcendentals=0),
        compiler_params=pltpu.CompilerParams(vmem_limit_bytes=16 << 20),
    )(*args)


def held(shape, dtype=F32):
    return VMEM(shape, dtype)


def keep(x):
    return pltpu.with_memory_space_constraint(x, VMEM)


def tile(i):
    return pl.ds(pl.multiple_of(i * LAT, LAT), LAT)


UNROLL = 4
SIZE = BINS * ROWS * LAT
PART = OWN * ROWS * LAT
N = ROWS * LAT
COEF = 0.75 / SCALE


def pack_kernel(pos, planck, dust, eold, eown, pair, near, far, stage, shares, sems):
    half = pos[0]
    mine = pl.ds(pl.multiple_of(N * half, N), N)
    other = pl.ds(pl.multiple_of(N * (1 - half), N), N)
    copies = [
        pltpu.make_async_copy(dust.at[:, other, :], far, sems.at[0]),
        pltpu.make_async_copy(eold.at[:, other, :], stage, sems.at[1]),
        pltpu.make_async_copy(dust.at[:, mine, :], near, sems.at[2]),
        pltpu.make_async_copy(eold.at[:, mine, :], eown, sems.at[3]),
        pltpu.make_async_copy(planck, shares, sems.at[4]),
    ]
    for copy in copies:
        copy.start()
    copies[0].wait()
    for b in range(BINS):
        pair[pl.ds(b * N, N), :] = far[b]
    copies[1].wait()
    for g in range(OWN):
        pair[pl.ds(SIZE + g * N, N), :] = stage[g].astype(BF)
    copies[4].wait()
    row = lax.broadcasted_iota(jnp.int32, (2 * LAT, LANES), 0)
    share = jnp.zeros((2 * LAT, LANES), F32)
    for g in range(OWN):
        share = jnp.where(row == g, shares[g], share)
    for i in range(3):
        piece = share.astype(BF)
        pair[pl.ds(SIZE + PART + 2 * i * LAT, 2 * LAT), :] = piece
        share = share - piece.astype(F32)
    copies[2].wait()
    copies[3].wait()


def write_slabs(pos, src, at, t1, t2, r1, r2):
    part, tp = pos[0], pos[1]
    low = src[pl.ds(0, TILES, stride=LAT), :].astype(BF)
    high = src[pl.ds(LAT - 1, TILES, stride=LAT), :].astype(BF)
    rows = pl.ds(at, TILES)

    @pl.when(tp == 0)
    def _():
        t1[rows, :] = high
        t2[rows, :] = low

    @pl.when(tp == 1)
    def _():
        t1[rows, :] = low
        t2[rows, :] = high

    for g in range(0, GROUPS, 2):
        def edge(r):
            a = src[tile(g * ROWS + r), :]
            b = src[tile((g + 1) * ROWS + r), :]
            return jnp.concatenate([a, b], axis=0).astype(BF)

        r1[pl.ds(at + g * LAT, 2 * LAT), :] = edge((ROWS - 1) * (1 - part))
        r2[pl.ds(at + g * LAT, 2 * LAT), :] = edge((ROWS - 1) * part)


def gather_bins(tab, wide, place, blocks, g, acc):
    first = (place // 2) * GROUPS
    for j, k in enumerate(blocks):
        source = jnp.bitwise_xor(place, k)
        for b in range(BINS):
            t = SCALE * tab[(source * BINS + b) * 2 * GROUPS + first + g]
            for r in range(ROWS):
                term = t * wide[tile((j * BINS + b) * ROWS + r), :]
                acc[r] = term if acc[r] is None else acc[r] + term
    return acc


def early_kernel(pos, tab, mine, near, far, kap, wide):
    place = pos[2]
    for j, block in enumerate((mine, near, far)):
        for b in range(BINS):
            wide[pl.ds(j * SIZE + b * N, N), :] = block[b].astype(F32)

    def one(g, carry):
        acc = gather_bins(tab, wide, place, (0, 2, 3), g, [None] * ROWS)
        for r in range(ROWS):
            kap[tile(g * ROWS + r), :] = acc[r]
        return carry

    lax.fori_loop(0, GROUPS, one, 0, unroll=2)


def late_kernel(pos, tab, planck, part, eown, pair, kap, e, share, t1, t2, r1, r2, wide):
    place = pos[2]
    slot = place % 2
    wide[...] = pair[pl.ds(0, SIZE), :].astype(F32)

    def one(g, carry):
        acc = [part[tile(g * ROWS + r), :] for r in range(ROWS)]
        acc = gather_bins(tab, wide, place, (1,), g, acc)
        for r in range(ROWS):
            kap[tile(g * ROWS + r), :] = acc[r]
        return carry

    lax.fori_loop(0, GROUPS, one, 0, unroll=2)
    theirs = pl.multiple_of((1 - slot) * PART, PART)
    mine = pl.multiple_of(slot * PART, PART)
    for g in range(OWN):
        e[pl.ds(mine + g * N, N), :] = eown[g]
    e[pl.ds(theirs, PART), :] = pair[pl.ds(SIZE, PART), :].astype(F32)
    at = SIZE + PART
    pieces = [pair[pl.ds(at + 2 * LAT * i, 2 * LAT), :].astype(F32) for i in range(3)]
    row = lax.broadcasted_iota(jnp.int32, (2 * LAT, LANES), 0)
    ours = jnp.zeros((2 * LAT, LANES), F32)
    for g in range(OWN):
        ours = jnp.where(row == g, planck[g], ours)
    share[slot] = ours
    share[1 - slot] = pieces[0] + pieces[1] + pieces[2]
    write_slabs(pos, e, 0, t1, t2, r1, r2)
    write_slabs(pos, kap, TILES, t1, t2, r1, r2)


def face(ea, eb, c):
    d = eb - ea
    w = 1.0 / (c + jnp.abs(d) / (ea + eb))
    return w, w * d


def spread(row):
    return jnp.broadcast_to(row, (LAT, LANES))


def share_of(share, g):
    part = g // OWN
    return spread(share[part, pl.ds(g - part * OWN, 1), :])


def inner_body(e, coefs, flux, weight, prepare):
    top = lax.broadcasted_iota(jnp.int32, (LAT, LANES), 0) == LAT - 1

    def one(g, carry):
        base = g * ROWS
        tiles = [e[tile(base + r), :] for r in range(ROWS)]
        coef = prepare(g, base, tiles) if prepare else [[c[tile(base + r), :] for c in coefs] for r in range(ROWS)]
        ws, fs = [], []
        for r in range(ROWS):
            here = tiles[r]
            c_up, c_east, c_above = coef[r]
            w_up, f_up = face(here, pltpu.roll(here, LAT - 1, 0), c_up)
            w_up, f_up = jnp.where(top, 0.0, w_up), jnp.where(top, 0.0, f_up)
            w_east, f_east = face(here, pltpu.roll(here, LANES - 1, 1), c_east)
            w = (w_up + pltpu.roll(w_up, 1, 0)) + (w_east + pltpu.roll(w_east, 1, 1))
            f = (f_up - pltpu.roll(f_up, 1, 0)) + (f_east - pltpu.roll(f_east, 1, 1))
            if r > 0:
                w, f = w + w_below, f - f_below
            if r + 1 < ROWS:
                w_below, f_below = face(here, tiles[r + 1], c_above)
                w, f = w + w_below, f + f_below
            ws.append(w)
            fs.append(f)
        for r in range(ROWS):
            weight[tile(base + r), :] = ws[r]
            flux[tile(base + r), :] = fs[r]
        return carry

    lax.fori_loop(0, GROUPS, one, 0, unroll=UNROLL)


def inner_first(pos, e, kap, share, flux, weight, up_c, east_c, above_c, e01, ssum):
    ssum[...] = jnp.zeros_like(ssum)

    def prepare(g, base, tiles):
        ks = [kap[tile(base + r), :] for r in range(ROWS)]
        sums = [ssum[tile(r), :] for r in range(ROWS)]
        share_row = share_of(share, g)
        out = []
        for r in range(ROWS):
            k = ks[r]
            c_up, c_east = COEF * (k + pltpu.roll(k, LAT - 1, 0)), COEF * (k + pltpu.roll(k, LANES - 1, 1))
            out.append((c_up, c_east, COEF * (k + ks[r + 1]) if r + 1 < ROWS else None))
        for r in range(ROWS):
            i = base + r
            up_c[tile(i), :], east_c[tile(i), :] = out[r][:2]
            if r + 1 < ROWS:
                above_c[tile(i), :] = out[r][2]
            e01[tile(i), :] = SCALE * tiles[r]
            ssum[tile(r), :] = sums[r] + ks[r] * share_row
        return out

    inner_body(e, None, flux, weight, prepare)


def inner_next(pos, e, up_c, east_c, above_c, flux, weight):
    inner_body(e, (up_c, east_c, above_c), flux, weight, None)


def unpack_halos(pos, slabs, at, halo):
    part, tp = pos[0], pos[1]
    rows = pl.ds(at, TILES)
    halo[1 - tp] = slabs[0][rows, :].astype(F32)
    halo[tp] = slabs[1][rows, :].astype(F32)
    halo[3 - part] = slabs[2][rows, :].astype(F32)
    halo[2 + part] = slabs[3][rows, :].astype(F32)


def outer_body(e, e01, kap, share, temp4, halo, edge, flux, weight, enew, ksum, numer, denom):
    def one(g, carry):
        base = g * ROWS
        row_share = share_of(share, g)
        refs = (e, kap, weight, flux, e01)
        rows = [[x[tile(base + r), :] for x in refs] + [temp4[tile(r), :]] for r in range(ROWS)]
        ends = {at: (halo[j, tile(g), :], edge[j, tile(g), :]) for j, at in ((2, 0), (3, ROWS - 1))}
        strips = [pl.ds(base * LAT + at, ROWS, stride=LAT) for at in (0, LAT - 1)]
        strips = [(strip, e[strip, :]) for strip in strips]
        out = []
        for r in range(ROWS):
            here, k, w, f, old, t4 = rows[r]
            if r in ends:
                w_out, f_out = face(here, *ends[r])
                w, f = w + w_out, f + f_out
            out.append((old + k * (row_share * t4) + (here * w + f), SCALE + k + w))
        for r in range(ROWS):
            numer[tile(base + r), :], denom[tile(base + r), :] = out[r]
        for j, (strip, past) in enumerate(strips):
            w, _ = face(past, halo[j, tile(g), :], edge[j, tile(g), :])
            numer[strip, :] = numer[strip, :] + w * halo[j, tile(g), :]
            denom[strip, :] = denom[strip, :] + w
        return carry

    lax.fori_loop(0, GROUPS, one, 0, unroll=8)

    def two(g, sums):
        at = [tile(g * ROWS + r) for r in range(ROWS)]
        fresh = [numer[i, :] / denom[i, :] for i in at]
        sums = tuple(sums[r] + kap[at[r], :] * fresh[r] for r in range(ROWS))
        for r in range(ROWS):
            enew[at[r], :] = fresh[r]
        return sums

    sums = lax.fori_loop(0, GROUPS, two, (jnp.zeros((LAT, LANES), F32),) * ROWS, unroll=8)
    for r in range(ROWS):
        ksum[tile(r), :] = sums[r]


def own_rows(pos, ref):
    return ref[pl.ds(pl.multiple_of(pos[0] * N, N), N), :]


def terms(told, t, stot):
    cube = t * t * t
    return HEAT * told + 3.0 * stot * (cube * t), HEAT + 4.0 * stot * cube


def outer_first(pos, e, e01, kap, share, told, ssum, flux, weight, h0, h1, h2, h3, *refs):
    enew, sums, edge, t1, t2, r1, r2 = refs[:7]
    temp4, halo, numer, denom = refs[7:]
    slabs = (h0, h1, h2, h3)
    unpack_halos(pos, slabs, TILES, halo)
    for j, at in ((0, 0), (1, LAT - 1)):
        edge[j] = COEF * (kap[pl.ds(at, TILES, stride=LAT), :] + halo[j])
    for g in range(GROUPS):
        for j, at in ((2, 0), (3, ROWS - 1)):
            edge[j, tile(g), :] = COEF * (kap[tile(g * ROWS + at), :] + halo[j, tile(g), :])
    unpack_halos(pos, slabs, 0, halo)
    t = own_rows(pos, told)
    temp4[...] = t * t * t * t
    outer_body(e, e01, kap, share, temp4, halo, edge, flux, weight, enew, sums.at[pl.ds(0, N)], numer, denom)
    sums[pl.ds(N, N), :] = ssum[...]
    write_slabs(pos, enew, 0, t1, t2, r1, r2)


def outer_middle(pos, e, e01, kap, share, told, sums, got, edge, flux, weight, h0, h1, h2, h3, *refs):
    enew, ksum, tnow, stot, t1, t2, r1, r2 = refs[:8]
    temp4, halo, numer, denom = refs[8:]
    unpack_halos(pos, (h0, h1, h2, h3), 0, halo)
    both = (sums[...] + got[...]) / SCALE
    s = both[N:]
    stot[...] = s
    t = own_rows(pos, told)
    up, down = terms(t, t, s)
    t = (up + both[:N]) / down
    tnow[...] = t
    temp4[...] = t * t * t * t
    outer_body(e, e01, kap, share, temp4, halo, edge, flux, weight, enew, ksum, numer, denom)
    write_slabs(pos, enew, 0, t1, t2, r1, r2)


def outer_last(pos, e, e01, kap, share, told, tprev, stot, part, got, edge, flux, weight, h0, h1, h2, h3, *refs):
    eown, send, ksum, up, down = refs[:5]
    temp4, halo, numer, denom, enew = refs[5:]
    unpack_halos(pos, (h0, h1, h2, h3), 0, halo)
    s = stot[...]
    old = own_rows(pos, told)
    above, below = terms(old, tprev[...], s)
    t = (above + (part[...] + got[...]) / SCALE) / below
    temp4[...] = t * t * t * t
    outer_body(e, e01, kap, share, temp4, halo, edge, flux, weight, enew, ksum, numer, denom)
    slot = pos[2] % 2
    for g in range(OWN):
        eown[g] = enew[pl.ds(pl.multiple_of((slot * OWN + g) * N, N), N), :]
        send[g] = enew[pl.ds(pl.multiple_of(((1 - slot) * OWN + g) * N, N), N), :]
    up[...], down[...] = terms(old, t, s)


def finish_kernel(ksum, got, up, down, temp):
    temp[...] = (up[...] + (ksum[...] + got[...]) / SCALE) / down[...]


def half_rows(half):
    return pl.ds(pl.multiple_of(N * half, N), N)


def own_kernel(pos, eown, energy, sem):
    copy = pltpu.make_async_copy(eown, energy.at[:, half_rows(pos[0]), :], sem)
    copy.start()
    copy.wait()


def join_kernel(pos, pair, mine, other, held_energy, energy, temp, sem):
    half = pos[0]
    copy = pltpu.make_async_copy(pair, energy.at[:, half_rows(1 - half), :], sem)
    copy.start()
    temp[half_rows(half), :] = mine[...]
    temp[half_rows(1 - half), :] = other[...]
    copy.wait()


def theta_pairs(count, odd):
    return [p for i in range(odd, count - 1, 2) for p in ((i, i + 1), (i + 1, i))]


def row_pairs(rows, odd):
    def device(chain, position):
        row, part = position // 2, position % 2
        return row * 4 + 2 * chain + (part ^ (row & 1))

    pairs = []
    for chain in range(2):
        for i in range(odd, 2 * rows - 1, 2):
            a, b = device(chain, i), device(chain, i + 1)
            pairs += [(a, b), (b, a)]
    return pairs


def xor(x, k):
    return lax.ppermute(x, "group", [(i, i ^ k) for i in range(4)])


def swap_halos(slabs, part=None):
    t1, t2, r1, r2 = slabs
    nt, nr = lax.axis_size("theta"), lax.axis_size("row")
    t2 = lax.ppermute(t2, "theta", theta_pairs(nt, 1))
    part = part if part is None else keep(xor(part, 2))
    t1 = lax.ppermute(t1, "theta", theta_pairs(nt, 0))
    r2 = lax.ppermute(r2, ("row", "group"), row_pairs(nr, 1))
    r1 = lax.ppermute(r1, ("row", "group"), row_pairs(nr, 0))
    return tuple(keep(x) for x in (t1, t2, r1, r2)), part


def shards(dust, table, planck, energy_old, temp_old):
    place = lax.axis_index("group")
    row = lax.axis_index("row")
    pos = jnp.stack([(place ^ row) & 1, lax.axis_index("theta") & 1, place, row]).astype(jnp.int32)
    dust = dust.reshape(BINS, 2 * N, LANES)
    energy_old = energy_old.reshape(OWN, 2 * N, LANES)
    told = temp_old.reshape(-1, LANES)
    tab = table.astype(F32).reshape(-1)
    slabs = [held((TILES, LANES), BF)] * 4
    scratch = [VMEM((N, LANES), F32), VMEM((4, TILES, LANES), F32), VMEM((CELLS, LANES), F32), VMEM((CELLS, LANES), F32)]
    full = held((CELLS, LANES))
    sheet = held((N, LANES))
    block = held((BINS, N, LANES), BF)

    eown, pair, mine, far = call(
        pack_kernel,
        [held((OWN, N, LANES)), held((SIZE + PART + 6 * LAT, LANES), BF), block, block],
        (pos, *(pltpu.with_memory_space_constraint(x, pltpu.HBM) for x in (planck, dust, energy_old))), smem=1, space=pl.ANY,
        scratch=[VMEM((OWN, N, LANES), F32), SMEM(planck.shape, F32), pltpu.SemaphoreType.DMA((5,))],
    )
    far = xor(far, 3)
    near = xor(mine, 2)
    pair = xor(pair, 1)
    early, = call(
        early_kernel, [full], (pos, tab, keep(mine), keep(near), keep(far)), smem=2,
        scratch=[VMEM((3 * SIZE, LANES), F32)], flops=20_000_000,
    )
    kap, e, share, *both = call(
        late_kernel,
        [full, full, held((2, 2 * LAT, LANES))] + [held((2 * TILES, LANES), BF)] * 4,
        (pos, tab, planck, keep(early), keep(eown), keep(pair)), smem=3,
        scratch=[VMEM((SIZE, LANES), F32)], flops=5_000_000,
    )
    kap, share, e = keep(kap), keep(share), keep(e)
    halos, _ = swap_halos(both)
    flux, weight, *coefs, e01, ssum = call(
        inner_first, [full] * 6 + [sheet], (pos, e, kap, share), smem=1, flops=20_000_000,
    )
    coefs = [keep(x) for x in coefs]
    e01 = keep(e01)
    e, sums, edge, *rest = call(
        outer_first, [full, held((2 * N, LANES)), held((4, TILES, LANES))] + slabs,
        (pos, e, e01, kap, share, told, keep(ssum), keep(flux), keep(weight), *halos), smem=1,
        scratch=scratch, flops=5_000_000,
    )
    e, edge, sums = keep(e), keep(edge), keep(sums)
    halos, got = swap_halos(rest, sums)
    flux, weight = call(inner_next, [full] * 2, (pos, e, *coefs), smem=1, flops=20_000_000)
    e, part, temp, stot, *rest = call(
        outer_middle, [full, sheet, sheet, sheet] + slabs,
        (pos, e, e01, kap, share, told, sums, got, edge, keep(flux), keep(weight), *halos), smem=1,
        scratch=scratch, flops=5_000_000,
    )
    e, part = keep(e), keep(part)
    halos, got = swap_halos(rest, part)
    flux, weight = call(inner_next, [full] * 2, (pos, e, *coefs), smem=1, flops=20_000_000)
    eown, send, part, up, down = call(
        outer_last, [held((OWN, N, LANES)), held((OWN, N, LANES)), sheet, sheet, sheet],
        (pos, e, e01, kap, share, told, keep(temp), keep(stot), part, got, edge, keep(flux), keep(weight), *halos), smem=1,
        scratch=scratch + [VMEM((CELLS, LANES), F32)], flops=5_000_000,
    )
    whole = pltpu.HBM((OWN, 2 * N, LANES), F32)
    pair = xor(send, 1)
    got = xor(part, 2)
    mine, = call(finish_kernel, [sheet], [keep(x) for x in (part, got, up, down)])
    other = xor(mine, 1)
    energy = pl.pallas_call(
        own_kernel,
        out_shape=whole,
        in_specs=[pl.BlockSpec(memory_space=SMEM), pl.BlockSpec(memory_space=VMEM)],
        out_specs=pl.BlockSpec(memory_space=pl.ANY),
        scratch_shapes=[pltpu.SemaphoreType.DMA],
        compiler_params=pltpu.CompilerParams(vmem_limit_bytes=16 << 20),
        name="own",
    )(pos, keep(eown))
    energy, temp = pl.pallas_call(
        join_kernel,
        out_shape=[whole, jax.ShapeDtypeStruct((2 * N, LANES), F32)],
        in_specs=[pl.BlockSpec(memory_space=SMEM)] + [pl.BlockSpec(memory_space=VMEM)] * 3 + [pl.BlockSpec(memory_space=pl.ANY)],
        out_specs=[pl.BlockSpec(memory_space=pl.ANY), pl.BlockSpec(memory_space=VMEM)],
        scratch_shapes=[pltpu.SemaphoreType.DMA],
        input_output_aliases={4: 0},
        compiler_params=pltpu.CompilerParams(vmem_limit_bytes=16 << 20),
        name="join",
    )(pos, keep(pair), keep(mine), keep(other), energy)
    return energy.reshape(OWN, 2 * ROWS, LAT, LANES), temp.reshape(2 * ROWS, LAT, LANES)


def solution(mesh):
    return jax.shard_map(
        shards,
        mesh=mesh,
        in_specs=(
            P("group", "row", "theta", None),
            P(),
            P("group"),
            P("group", "row", "theta", None),
            P("row", "theta", None),
        ),
        out_specs=(P("group", "row", "theta", None), P("row", "theta", None)),
        check_vma=False,
    )
```

```python
import jax
import jax.numpy as jnp
from jax import lax
from jax.experimental import pallas as pl
from jax.experimental.pallas import tpu as pltpu
from jax.sharding import PartitionSpec as P


HEAT = 2.0
REACH = 20.0
SCALE = 2.0 / REACH


BF = jnp.bfloat16
F32 = jnp.float32
VMEM = pltpu.VMEM
SMEM = pltpu.SMEM

BINS = 8
OWN = 12
GROUPS = 24
ROWS = 8
LAT = 8
LANES = 128
TILES = GROUPS * ROWS
CELLS = TILES * LAT


def call(kernel, outs, args, smem=0, scratch=(), flops=1_000_000, space=VMEM):
    specs = [pl.BlockSpec(memory_space=SMEM)] * smem
    specs += [pl.BlockSpec(memory_space=space)] * (len(args) - smem)
    return pl.pallas_call(
        kernel,
        out_shape=outs,
        in_specs=specs,
        out_specs=[pl.BlockSpec(memory_space=VMEM)] * len(outs),
        scratch_shapes=list(scratch),
        cost_estimate=pl.CostEstimate(flops=flops, bytes_accessed=1_000_000, transcendentals=0),
        compiler_params=pltpu.CompilerParams(vmem_limit_bytes=16 << 20),
    )(*args)


def held(shape, dtype=F32):
    return VMEM(shape, dtype)


def keep(x):
    return pltpu.with_memory_space_constraint(x, VMEM)


def tile(i):
    return pl.ds(pl.multiple_of(i * LAT, LAT), LAT)


UNROLL = 4
SIZE = BINS * ROWS * LAT
PART = OWN * ROWS * LAT
N = ROWS * LAT
COEF = 0.75 / SCALE


def half_rows(half):
    return pl.ds(pl.multiple_of(N * half, N), N)


def pack_kernel(pos, planck, dust, eold, eown, pair, near, far, stage, shares, sems):
    half = pos[0]
    mine, other = half_rows(half), half_rows(1 - half)
    give = [pltpu.make_async_copy(eold.at[g, other, :], stage.at[g], sems.at[g]) for g in range(OWN)]
    away = [pltpu.make_async_copy(dust.at[b, other, :], far.at[b], sems.at[OWN + b]) for b in range(BINS)]
    shared = pltpu.make_async_copy(planck, shares, sems.at[OWN + BINS])
    rest = [
        pltpu.make_async_copy(dust.at[:, mine, :], near, sems.at[OWN + BINS + 1]),
        pltpu.make_async_copy(eold.at[:, mine, :], eown, sems.at[OWN + BINS + 2]),
    ]
    for copy in [shared] + away + give + rest:
        copy.start()
    shared.wait()
    row = lax.broadcasted_iota(jnp.int32, (2 * LAT, LANES), 0)
    share = jnp.zeros((2 * LAT, LANES), F32)
    for g in range(OWN):
        share = jnp.where(row == g, shares[g], share)
    for i in range(3):
        piece = share.astype(BF)
        pair[pl.ds(SIZE + PART + 2 * i * LAT, 2 * LAT), :] = piece
        share = share - piece.astype(F32)
    for b in range(BINS):
        away[b].wait()
        pair[pl.ds(b * N, N), :] = far[b]
    for g in range(OWN):
        give[g].wait()
        pair[pl.ds(SIZE + g * N, N), :] = stage[g].astype(BF)
    for copy in rest:
        copy.wait()


def write_slabs(pos, src, at, t1, t2, r1, r2):
    part, tp = pos[0], pos[1]
    low = src[pl.ds(0, TILES, stride=LAT), :].astype(BF)
    high = src[pl.ds(LAT - 1, TILES, stride=LAT), :].astype(BF)
    rows = pl.ds(at, TILES)

    @pl.when(tp == 0)
    def _():
        t1[rows, :] = high
        t2[rows, :] = low

    @pl.when(tp == 1)
    def _():
        t1[rows, :] = low
        t2[rows, :] = high

    for g in range(0, GROUPS, 2):
        def edge(r):
            a = src[tile(g * ROWS + r), :]
            b = src[tile((g + 1) * ROWS + r), :]
            return jnp.concatenate([a, b], axis=0).astype(BF)

        r1[pl.ds(at + g * LAT, 2 * LAT), :] = edge((ROWS - 1) * (1 - part))
        r2[pl.ds(at + g * LAT, 2 * LAT), :] = edge((ROWS - 1) * part)


def gather_bins(tab, wide, place, blocks, g, acc):
    first = (place // 2) * GROUPS
    for j, k in enumerate(blocks):
        source = jnp.bitwise_xor(place, k)
        for b in range(BINS):
            t = SCALE * tab[(source * BINS + b) * 2 * GROUPS + first + g]
            for r in range(ROWS):
                term = t * wide[tile((j * BINS + b) * ROWS + r), :]
                acc[r] = term if acc[r] is None else acc[r] + term
    return acc


def early_kernel(pos, tab, planck, mine, pair, near, eown, kap, e, share, wide):
    place = pos[2]
    slot = place % 2
    for b in range(BINS):
        wide[pl.ds(b * N, N), :] = mine[b].astype(F32)
        wide[pl.ds(SIZE + b * N, N), :] = pair[pl.ds(b * N, N), :].astype(F32)
        wide[pl.ds(2 * SIZE + b * N, N), :] = near[b].astype(F32)

    def one(g, carry):
        acc = gather_bins(tab, wide, place, (0, 1, 2), g, [None] * ROWS)
        for r in range(ROWS):
            kap[tile(g * ROWS + r), :] = acc[r]
        return carry

    lax.fori_loop(0, GROUPS, one, 0, unroll=2)
    for g in range(OWN):
        e[half_rows(slot * OWN + g), :] = eown[g]
        e[half_rows((1 - slot) * OWN + g), :] = pair[pl.ds(SIZE + g * N, N), :].astype(F32)
    at = SIZE + PART
    pieces = [pair[pl.ds(at + 2 * LAT * i, 2 * LAT), :].astype(F32) for i in range(3)]
    row = lax.broadcasted_iota(jnp.int32, (2 * LAT, LANES), 0)
    ours = jnp.zeros((2 * LAT, LANES), F32)
    for g in range(OWN):
        ours = jnp.where(row == g, planck[g], ours)
    share[slot] = ours
    share[1 - slot] = pieces[0] + pieces[1] + pieces[2]


def late_kernel(pos, tab, part, far, e, kap, t1, t2, r1, r2, wide):
    place = pos[2]
    for b in range(BINS):
        wide[pl.ds(b * N, N), :] = far[b].astype(F32)

    def one(g, carry):
        acc = [part[tile(g * ROWS + r), :] for r in range(ROWS)]
        acc = gather_bins(tab, wide, place, (3,), g, acc)
        for r in range(ROWS):
            kap[tile(g * ROWS + r), :] = acc[r]
        return carry

    lax.fori_loop(0, GROUPS, one, 0, unroll=4)
    write_slabs(pos, e, 0, t1, t2, r1, r2)
    write_slabs(pos, kap, TILES, t1, t2, r1, r2)


def face(ea, eb, c):
    d = eb - ea
    w = 1.0 / (c + jnp.abs(d) / (ea + eb))
    return w, w * d


def spread(row):
    return jnp.broadcast_to(row, (LAT, LANES))


def share_of(share, g):
    part = g // OWN
    return spread(share[part, pl.ds(g - part * OWN, 1), :])


def inner_body(e, coefs, flux, weight, prepare):
    top = lax.broadcasted_iota(jnp.int32, (LAT, LANES), 0) == LAT - 1

    def one(g, carry):
        base = g * ROWS
        tiles = [e[tile(base + r), :] for r in range(ROWS)]
        coef = prepare(g, base, tiles) if prepare else [[c[tile(base + r), :] for c in coefs] for r in range(ROWS)]
        ws, fs = [], []
        for r in range(ROWS):
            here = tiles[r]
            c_up, c_east, c_above = coef[r]
            w_up, f_up = face(here, pltpu.roll(here, LAT - 1, 0), c_up)
            w_up, f_up = jnp.where(top, 0.0, w_up), jnp.where(top, 0.0, f_up)
            w_east, f_east = face(here, pltpu.roll(here, LANES - 1, 1), c_east)
            w = (w_up + pltpu.roll(w_up, 1, 0)) + (w_east + pltpu.roll(w_east, 1, 1))
            f = (f_up - pltpu.roll(f_up, 1, 0)) + (f_east - pltpu.roll(f_east, 1, 1))
            if r > 0:
                w, f = w + w_below, f - f_below
            if r + 1 < ROWS:
                w_below, f_below = face(here, tiles[r + 1], c_above)
                w, f = w + w_below, f + f_below
            ws.append(w)
            fs.append(f)
        for r in range(ROWS):
            weight[tile(base + r), :] = ws[r]
            flux[tile(base + r), :] = fs[r]
        return carry

    lax.fori_loop(0, GROUPS, one, 0, unroll=UNROLL)


def inner_first(pos, e, kap, share, flux, weight, up_c, east_c, above_c, e01, ssum):
    ssum[...] = jnp.zeros_like(ssum)

    def prepare(g, base, tiles):
        ks = [kap[tile(base + r), :] for r in range(ROWS)]
        sums = [ssum[tile(r), :] for r in range(ROWS)]
        share_row = share_of(share, g)
        out = []
        for r in range(ROWS):
            k = ks[r]
            c_up, c_east = COEF * (k + pltpu.roll(k, LAT - 1, 0)), COEF * (k + pltpu.roll(k, LANES - 1, 1))
            out.append((c_up, c_east, COEF * (k + ks[r + 1]) if r + 1 < ROWS else None))
        for r in range(ROWS):
            i = base + r
            up_c[tile(i), :], east_c[tile(i), :] = out[r][:2]
            if r + 1 < ROWS:
                above_c[tile(i), :] = out[r][2]
            e01[tile(i), :] = SCALE * tiles[r]
            ssum[tile(r), :] = sums[r] + ks[r] * share_row
        return out

    inner_body(e, None, flux, weight, prepare)


def inner_next(pos, e, up_c, east_c, above_c, flux, weight):
    inner_body(e, (up_c, east_c, above_c), flux, weight, None)


def unpack_halos(pos, slabs, at, halo):
    part, tp = pos[0], pos[1]
    rows = pl.ds(at, TILES)
    halo[1 - tp] = slabs[0][rows, :].astype(F32)
    halo[tp] = slabs[1][rows, :].astype(F32)
    halo[3 - part] = slabs[2][rows, :].astype(F32)
    halo[2 + part] = slabs[3][rows, :].astype(F32)


def outer_body(e, e01, kap, share, temp4, halo, edge, flux, weight, enew, ksum, numer, denom):
    def one(g, carry):
        base = g * ROWS
        row_share = share_of(share, g)
        refs = (e, kap, weight, flux, e01)
        rows = [[x[tile(base + r), :] for x in refs] + [temp4[tile(r), :]] for r in range(ROWS)]
        ends = {at: (halo[j, tile(g), :], edge[j, tile(g), :]) for j, at in ((2, 0), (3, ROWS - 1))}
        strips = [pl.ds(base * LAT + at, ROWS, stride=LAT) for at in (0, LAT - 1)]
        strips = [(strip, e[strip, :]) for strip in strips]
        out = []
        for r in range(ROWS):
            here, k, w, f, old, t4 = rows[r]
            if r in ends:
                w_out, f_out = face(here, *ends[r])
                w, f = w + w_out, f + f_out
            out.append((old + k * (row_share * t4) + (here * w + f), SCALE + k + w))
        for r in range(ROWS):
            numer[tile(base + r), :], denom[tile(base + r), :] = out[r]
        for j, (strip, past) in enumerate(strips):
            w, _ = face(past, halo[j, tile(g), :], edge[j, tile(g), :])
            numer[strip, :] = numer[strip, :] + w * halo[j, tile(g), :]
            denom[strip, :] = denom[strip, :] + w
        return carry

    lax.fori_loop(0, GROUPS, one, 0, unroll=8)

    def two(g, sums):
        at = [tile(g * ROWS + r) for r in range(ROWS)]
        fresh = [numer[i, :] / denom[i, :] for i in at]
        sums = tuple(sums[r] + kap[at[r], :] * fresh[r] for r in range(ROWS))
        for r in range(ROWS):
            enew[at[r], :] = fresh[r]
        return sums

    sums = lax.fori_loop(0, GROUPS, two, (jnp.zeros((LAT, LANES), F32),) * ROWS, unroll=8)
    for r in range(ROWS):
        ksum[tile(r), :] = sums[r]


def own_rows(pos, ref):
    return ref[pl.ds(pl.multiple_of(pos[0] * N, N), N), :]


def terms(told, t, stot):
    cube = t * t * t
    return HEAT * told + 3.0 * stot * (cube * t), HEAT + 4.0 * stot * cube


def outer_first(pos, e, e01, kap, share, told, ssum, flux, weight, h0, h1, h2, h3, *refs):
    enew, sums, edge, t1, t2, r1, r2 = refs[:7]
    temp4, halo, numer, denom = refs[7:]
    slabs = (h0, h1, h2, h3)
    unpack_halos(pos, slabs, TILES, halo)
    for j, at in ((0, 0), (1, LAT - 1)):
        edge[j] = COEF * (kap[pl.ds(at, TILES, stride=LAT), :] + halo[j])
    for g in range(GROUPS):
        for j, at in ((2, 0), (3, ROWS - 1)):
            edge[j, tile(g), :] = COEF * (kap[tile(g * ROWS + at), :] + halo[j, tile(g), :])
    unpack_halos(pos, slabs, 0, halo)
    t = own_rows(pos, told)
    temp4[...] = t * t * t * t
    outer_body(e, e01, kap, share, temp4, halo, edge, flux, weight, enew, sums.at[pl.ds(0, N)], numer, denom)
    sums[pl.ds(N, N), :] = ssum[...]
    write_slabs(pos, enew, 0, t1, t2, r1, r2)


def outer_middle(pos, e, e01, kap, share, told, sums, got, edge, flux, weight, h0, h1, h2, h3, *refs):
    enew, ksum, tnow, stot, t1, t2, r1, r2 = refs[:8]
    temp4, halo, numer, denom = refs[8:]
    unpack_halos(pos, (h0, h1, h2, h3), 0, halo)
    both = (sums[...] + got[...]) / SCALE
    s = both[N:]
    stot[...] = s
    t = own_rows(pos, told)
    up, down = terms(t, t, s)
    t = (up + both[:N]) / down
    tnow[...] = t
    temp4[...] = t * t * t * t
    outer_body(e, e01, kap, share, temp4, halo, edge, flux, weight, enew, ksum, numer, denom)
    write_slabs(pos, enew, 0, t1, t2, r1, r2)


def outer_last(pos, e, e01, kap, share, told, tprev, stot, part, got, edge, flux, weight, h0, h1, h2, h3, *refs):
    eown, send, ksum, up, down = refs[:5]
    temp4, halo, numer, denom, enew = refs[5:]
    unpack_halos(pos, (h0, h1, h2, h3), 0, halo)
    s = stot[...]
    old = own_rows(pos, told)
    above, below = terms(old, tprev[...], s)
    t = (above + (part[...] + got[...]) / SCALE) / below
    temp4[...] = t * t * t * t
    outer_body(e, e01, kap, share, temp4, halo, edge, flux, weight, enew, ksum, numer, denom)
    slot = pos[2] % 2
    for g in range(OWN):
        eown[g] = enew[pl.ds(pl.multiple_of((slot * OWN + g) * N, N), N), :]
        send[g] = enew[pl.ds(pl.multiple_of(((1 - slot) * OWN + g) * N, N), N), :]
    up[...], down[...] = terms(old, t, s)


def finish_kernel(ksum, got, up, down, temp):
    temp[...] = (up[...] + (ksum[...] + got[...]) / SCALE) / down[...]


def put(src, energy, half, sems):
    copies = [pltpu.make_async_copy(src.at[g], energy.at[g, half_rows(half), :], sems.at[g]) for g in range(OWN)]
    for copy in copies:
        copy.start()
    return copies


def own_kernel(pos, eown, energy, sems):
    for copy in put(eown, energy, pos[0], sems):
        copy.wait()


def join_kernel(pos, pair, mine, other, held_energy, energy, temp, sems):
    half = pos[0]
    copies = put(pair, energy, 1 - half, sems)
    temp[half_rows(half), :] = mine[...]
    temp[half_rows(1 - half), :] = other[...]
    for copy in copies:
        copy.wait()


def theta_pairs(count, odd):
    return [p for i in range(odd, count - 1, 2) for p in ((i, i + 1), (i + 1, i))]


def row_pairs(rows, odd):
    def device(chain, position):
        row, part = position // 2, position % 2
        return row * 4 + 2 * chain + (part ^ (row & 1))

    pairs = []
    for chain in range(2):
        for i in range(odd, 2 * rows - 1, 2):
            a, b = device(chain, i), device(chain, i + 1)
            pairs += [(a, b), (b, a)]
    return pairs


def xor(x, k):
    return lax.ppermute(x, "group", [(i, i ^ k) for i in range(4)])


def swap_halos(slabs, part=None):
    t1, t2, r1, r2 = slabs
    nt, nr = lax.axis_size("theta"), lax.axis_size("row")
    t2 = lax.ppermute(t2, "theta", theta_pairs(nt, 1))
    part = part if part is None else keep(xor(part, 2))
    t1 = lax.ppermute(t1, "theta", theta_pairs(nt, 0))
    r2 = lax.ppermute(r2, ("row", "group"), row_pairs(nr, 1))
    r1 = lax.ppermute(r1, ("row", "group"), row_pairs(nr, 0))
    return tuple(keep(x) for x in (t1, t2, r1, r2)), part


def shards(dust, table, planck, energy_old, temp_old):
    place = lax.axis_index("group")
    row = lax.axis_index("row")
    pos = jnp.stack([(place ^ row) & 1, lax.axis_index("theta") & 1, place, row]).astype(jnp.int32)
    dust = dust.reshape(BINS, 2 * N, LANES)
    energy_old = energy_old.reshape(OWN, 2 * N, LANES)
    told = temp_old.reshape(-1, LANES)
    tab = table.astype(F32).reshape(-1)
    slabs = [held((TILES, LANES), BF)] * 4
    scratch = [VMEM((N, LANES), F32), VMEM((4, TILES, LANES), F32), VMEM((CELLS, LANES), F32), VMEM((CELLS, LANES), F32)]
    full = held((CELLS, LANES))
    sheet = held((N, LANES))
    block = held((BINS, N, LANES), BF)

    eown, pair, mine, far = call(
        pack_kernel,
        [held((OWN, N, LANES)), held((SIZE + PART + 6 * LAT, LANES), BF), block, block],
        (pos, *(pltpu.with_memory_space_constraint(x, pltpu.HBM) for x in (planck, dust, energy_old))), smem=1, space=pl.ANY,
        scratch=[VMEM((OWN, N, LANES), F32), SMEM(planck.shape, F32), pltpu.SemaphoreType.DMA((OWN + BINS + 3,))],
    )
    pair = xor(pair, 1)
    near = xor(mine, 2)
    far = xor(far, 3)
    early, e, share = call(
        early_kernel, [full, full, held((2, 2 * LAT, LANES))],
        (pos, tab, planck, keep(mine), keep(pair), keep(near), keep(eown)), smem=3,
        scratch=[VMEM((3 * SIZE, LANES), F32)], flops=20_000_000,
    )
    e = keep(e)
    kap, *both = call(
        late_kernel,
        [full] + [held((2 * TILES, LANES), BF)] * 4,
        (pos, tab, keep(early), keep(far), e), smem=2,
        scratch=[VMEM((SIZE, LANES), F32)], flops=5_000_000,
    )
    kap, share = keep(kap), keep(share)
    halos, _ = swap_halos(both)
    flux, weight, *coefs, e01, ssum = call(
        inner_first, [full] * 6 + [sheet], (pos, e, kap, share), smem=1, flops=20_000_000,
    )
    coefs = [keep(x) for x in coefs]
    e01 = keep(e01)
    e, sums, edge, *rest = call(
        outer_first, [full, held((2 * N, LANES)), held((4, TILES, LANES))] + slabs,
        (pos, e, e01, kap, share, told, keep(ssum), keep(flux), keep(weight), *halos), smem=1,
        scratch=scratch, flops=5_000_000,
    )
    e, edge, sums = keep(e), keep(edge), keep(sums)
    halos, got = swap_halos(rest, sums)
    flux, weight = call(inner_next, [full] * 2, (pos, e, *coefs), smem=1, flops=20_000_000)
    e, part, temp, stot, *rest = call(
        outer_middle, [full, sheet, sheet, sheet] + slabs,
        (pos, e, e01, kap, share, told, sums, got, edge, keep(flux), keep(weight), *halos), smem=1,
        scratch=scratch, flops=5_000_000,
    )
    e, part = keep(e), keep(part)
    halos, got = swap_halos(rest, part)
    flux, weight = call(inner_next, [full] * 2, (pos, e, *coefs), smem=1, flops=20_000_000)
    eown, send, part, up, down = call(
        outer_last, [held((OWN, N, LANES)), held((OWN, N, LANES)), sheet, sheet, sheet],
        (pos, e, e01, kap, share, told, keep(temp), keep(stot), part, got, edge, keep(flux), keep(weight), *halos), smem=1,
        scratch=scratch + [VMEM((CELLS, LANES), F32)], flops=5_000_000,
    )
    whole = pltpu.HBM((OWN, 2 * N, LANES), F32)
    got = xor(part, 2)
    pair = xor(send, 1)
    mine, = call(finish_kernel, [sheet], [keep(x) for x in (part, got, up, down)])
    other = xor(mine, 1)
    energy = pl.pallas_call(
        own_kernel,
        out_shape=whole,
        in_specs=[pl.BlockSpec(memory_space=SMEM), pl.BlockSpec(memory_space=VMEM)],
        out_specs=pl.BlockSpec(memory_space=pl.ANY),
        scratch_shapes=[pltpu.SemaphoreType.DMA((OWN,))],
        compiler_params=pltpu.CompilerParams(vmem_limit_bytes=16 << 20),
        name="own",
    )(pos, keep(eown))
    energy, temp = pl.pallas_call(
        join_kernel,
        out_shape=[whole, jax.ShapeDtypeStruct((2 * N, LANES), F32)],
        in_specs=[pl.BlockSpec(memory_space=SMEM)] + [pl.BlockSpec(memory_space=VMEM)] * 3 + [pl.BlockSpec(memory_space=pl.ANY)],
        out_specs=[pl.BlockSpec(memory_space=pl.ANY), pl.BlockSpec(memory_space=VMEM)],
        scratch_shapes=[pltpu.SemaphoreType.DMA((OWN,))],
        input_output_aliases={4: 0},
        compiler_params=pltpu.CompilerParams(vmem_limit_bytes=16 << 20),
        name="join",
    )(pos, keep(pair), keep(mine), keep(other), energy)
    return energy.reshape(OWN, 2 * ROWS, LAT, LANES), temp.reshape(2 * ROWS, LAT, LANES)


def solution(mesh):
    return jax.shard_map(
        shards,
        mesh=mesh,
        in_specs=(
            P("group", "row", "theta", None),
            P(),
            P("group"),
            P("group", "row", "theta", None),
            P("row", "theta", None),
        ),
        out_specs=(P("group", "row", "theta", None), P("row", "theta", None)),
        check_vma=False,
    )
```

```python
import jax
import jax.numpy as jnp
from jax import lax
from jax.experimental import pallas as pl
from jax.experimental.pallas import tpu as pltpu
from jax.sharding import PartitionSpec as P


HEAT = 2.0
REACH = 20.0
SCALE = 2.0 / REACH


BF = jnp.bfloat16
F32 = jnp.float32
VMEM = pltpu.VMEM
SMEM = pltpu.SMEM

BINS = 8
OWN = 12
GROUPS = 24
ROWS = 8
LAT = 8
LANES = 128
TILES = GROUPS * ROWS
CELLS = TILES * LAT


def call(kernel, outs, args, smem=0, scratch=(), flops=1_000_000, space=VMEM):
    specs = [pl.BlockSpec(memory_space=SMEM)] * smem
    specs += [pl.BlockSpec(memory_space=space)] * (len(args) - smem)
    return pl.pallas_call(
        kernel,
        out_shape=outs,
        in_specs=specs,
        out_specs=[pl.BlockSpec(memory_space=VMEM)] * len(outs),
        scratch_shapes=list(scratch),
        cost_estimate=pl.CostEstimate(flops=flops, bytes_accessed=1_000_000, transcendentals=0),
        compiler_params=pltpu.CompilerParams(vmem_limit_bytes=16 << 20),
    )(*args)


def held(shape, dtype=F32):
    return VMEM(shape, dtype)


def keep(x):
    return pltpu.with_memory_space_constraint(x, VMEM)


def tile(i):
    return pl.ds(pl.multiple_of(i * LAT, LAT), LAT)


UNROLL = 4
SIZE = BINS * ROWS * LAT
PART = OWN * ROWS * LAT
N = ROWS * LAT
COEF = 0.75 / SCALE


def half_rows(half):
    return pl.ds(pl.multiple_of(N * half, N), N)


def pack_kernel(pos, planck, dust, eold, eown, pair, near, far, stage, shares, sems):
    half = pos[0]
    mine = pl.ds(pl.multiple_of(N * half, N), N)
    other = pl.ds(pl.multiple_of(N * (1 - half), N), N)
    copies = [
        pltpu.make_async_copy(dust.at[:, other, :], far, sems.at[0]),
        pltpu.make_async_copy(eold.at[:, other, :], stage, sems.at[1]),
        pltpu.make_async_copy(dust.at[:, mine, :], near, sems.at[2]),
        pltpu.make_async_copy(eold.at[:, mine, :], eown, sems.at[3]),
        pltpu.make_async_copy(planck, shares, sems.at[4]),
    ]
    for copy in copies:
        copy.start()
    copies[0].wait()
    for b in range(BINS):
        pair[pl.ds(b * N, N), :] = far[b]
    copies[1].wait()
    for g in range(OWN):
        pair[pl.ds(SIZE + g * N, N), :] = stage[g].astype(BF)
    copies[4].wait()
    row = lax.broadcasted_iota(jnp.int32, (2 * LAT, LANES), 0)
    share = jnp.zeros((2 * LAT, LANES), F32)
    for g in range(OWN):
        share = jnp.where(row == g, shares[g], share)
    for i in range(3):
        piece = share.astype(BF)
        pair[pl.ds(SIZE + PART + 2 * i * LAT, 2 * LAT), :] = piece
        share = share - piece.astype(F32)
    copies[2].wait()
    copies[3].wait()


def write_slabs(pos, src, at, t1, t2, r1, r2):
    part, tp = pos[0], pos[1]
    low = src[pl.ds(0, TILES, stride=LAT), :].astype(BF)
    high = src[pl.ds(LAT - 1, TILES, stride=LAT), :].astype(BF)
    rows = pl.ds(at, TILES)

    @pl.when(tp == 0)
    def _():
        t1[rows, :] = high
        t2[rows, :] = low

    @pl.when(tp == 1)
    def _():
        t1[rows, :] = low
        t2[rows, :] = high

    for g in range(0, GROUPS, 2):
        def edge(r):
            a = src[tile(g * ROWS + r), :]
            b = src[tile((g + 1) * ROWS + r), :]
            return jnp.concatenate([a, b], axis=0).astype(BF)

        r1[pl.ds(at + g * LAT, 2 * LAT), :] = edge((ROWS - 1) * (1 - part))
        r2[pl.ds(at + g * LAT, 2 * LAT), :] = edge((ROWS - 1) * part)


def gather_bins(tab, wide, place, blocks, g, acc):
    first = (place // 2) * GROUPS
    for j, k in enumerate(blocks):
        source = jnp.bitwise_xor(place, k)
        for b in range(BINS):
            t = SCALE * tab[(source * BINS + b) * 2 * GROUPS + first + g]
            for r in range(ROWS):
                term = t * wide[tile((j * BINS + b) * ROWS + r), :]
                acc[r] = term if acc[r] is None else acc[r] + term
    return acc


def early_kernel(pos, tab, planck, mine, pair, far, eown, kap, e, share, wide):
    place = pos[2]
    slot = place % 2
    for b in range(BINS):
        wide[pl.ds(b * N, N), :] = mine[b].astype(F32)
        wide[pl.ds(SIZE + b * N, N), :] = pair[pl.ds(b * N, N), :].astype(F32)
        wide[pl.ds(2 * SIZE + b * N, N), :] = far[b].astype(F32)

    def one(g, carry):
        acc = gather_bins(tab, wide, place, (0, 1, 3), g, [None] * ROWS)
        for r in range(ROWS):
            kap[tile(g * ROWS + r), :] = acc[r]
        return carry

    lax.fori_loop(0, GROUPS, one, 0, unroll=2)
    for g in range(OWN):
        e[half_rows(slot * OWN + g), :] = eown[g]
        e[half_rows((1 - slot) * OWN + g), :] = pair[pl.ds(SIZE + g * N, N), :].astype(F32)
    at = SIZE + PART
    pieces = [pair[pl.ds(at + 2 * LAT * i, 2 * LAT), :].astype(F32) for i in range(3)]
    row = lax.broadcasted_iota(jnp.int32, (2 * LAT, LANES), 0)
    ours = jnp.zeros((2 * LAT, LANES), F32)
    for g in range(OWN):
        ours = jnp.where(row == g, planck[g], ours)
    share[slot] = ours
    share[1 - slot] = pieces[0] + pieces[1] + pieces[2]


def late_kernel(pos, tab, part, near, e, kap, t1, t2, r1, r2, wide):
    place = pos[2]
    for b in range(BINS):
        wide[pl.ds(b * N, N), :] = near[b].astype(F32)

    def one(g, carry):
        acc = [part[tile(g * ROWS + r), :] for r in range(ROWS)]
        acc = gather_bins(tab, wide, place, (2,), g, acc)
        for r in range(ROWS):
            kap[tile(g * ROWS + r), :] = acc[r]
        return carry

    lax.fori_loop(0, GROUPS, one, 0, unroll=4)
    write_slabs(pos, e, 0, t1, t2, r1, r2)
    write_slabs(pos, kap, TILES, t1, t2, r1, r2)


def face(ea, eb, c):
    d = eb - ea
    w = 1.0 / (c + jnp.abs(d) / (ea + eb))
    return w, w * d


def spread(row):
    return jnp.broadcast_to(row, (LAT, LANES))


def share_of(share, g):
    part = g // OWN
    return spread(share[part, pl.ds(g - part * OWN, 1), :])


def inner_body(e, coefs, flux, weight, prepare):
    def one(g, carry):
        base = g * ROWS
        tiles = [e[tile(base + r), :] for r in range(ROWS)]
        coef = prepare(g, base, tiles) if prepare else [[c[tile(base + r), :] for c in coefs] for r in range(ROWS)]
        ws, fs = [], []
        for r in range(ROWS):
            here = tiles[r]
            c_up, c_east, c_above = coef[r]
            w_up, f_up = face(here, pltpu.roll(here, LAT - 1, 0), c_up)
            w_east, f_east = face(here, pltpu.roll(here, LANES - 1, 1), c_east)
            w = (w_up + pltpu.roll(w_up, 1, 0)) + (w_east + pltpu.roll(w_east, 1, 1))
            f = (f_up - pltpu.roll(f_up, 1, 0)) + (f_east - pltpu.roll(f_east, 1, 1))
            if r > 0:
                w, f = w + w_below, f - f_below
            if r + 1 < ROWS:
                w_below, f_below = face(here, tiles[r + 1], c_above)
                w, f = w + w_below, f + f_below
            ws.append(w)
            fs.append(f)
        for r in range(ROWS):
            weight[tile(base + r), :] = ws[r]
            flux[tile(base + r), :] = fs[r]
        return carry

    lax.fori_loop(0, GROUPS, one, 0, unroll=UNROLL)


def inner_first(pos, e, kap, share, flux, weight, up_c, east_c, above_c, e01, ssum):
    ssum[...] = jnp.zeros_like(ssum)
    top = lax.broadcasted_iota(jnp.int32, (LAT, LANES), 0) == LAT - 1

    def prepare(g, base, tiles):
        ks = [kap[tile(base + r), :] for r in range(ROWS)]
        sums = [ssum[tile(r), :] for r in range(ROWS)]
        share_row = share_of(share, g)
        out = []
        for r in range(ROWS):
            k = ks[r]
            c_up = jnp.where(top, jnp.inf, COEF * (k + pltpu.roll(k, LAT - 1, 0)))
            c_east = COEF * (k + pltpu.roll(k, LANES - 1, 1))
            out.append((c_up, c_east, COEF * (k + ks[r + 1]) if r + 1 < ROWS else None))
        for r in range(ROWS):
            i = base + r
            up_c[tile(i), :], east_c[tile(i), :] = out[r][:2]
            if r + 1 < ROWS:
                above_c[tile(i), :] = out[r][2]
            e01[tile(i), :] = SCALE * tiles[r]
            ssum[tile(r), :] = sums[r] + ks[r] * share_row
        return out

    inner_body(e, None, flux, weight, prepare)


def inner_next(pos, e, up_c, east_c, above_c, flux, weight):
    inner_body(e, (up_c, east_c, above_c), flux, weight, None)


def unpack_halos(pos, slabs, at, halo):
    part, tp = pos[0], pos[1]
    rows = pl.ds(at, TILES)
    halo[1 - tp] = slabs[0][rows, :].astype(F32)
    halo[tp] = slabs[1][rows, :].astype(F32)
    halo[3 - part] = slabs[2][rows, :].astype(F32)
    halo[2 + part] = slabs[3][rows, :].astype(F32)


def outer_body(e, e01, kap, share, temp4, halo, edge, flux, weight, enew, ksum, numer, denom):
    def one(g, carry):
        base = g * ROWS
        row_share = share_of(share, g)
        refs = (e, kap, weight, flux, e01)
        rows = [[x[tile(base + r), :] for x in refs] + [temp4[tile(r), :]] for r in range(ROWS)]
        ends = {at: (halo[j, tile(g), :], edge[j, tile(g), :]) for j, at in ((2, 0), (3, ROWS - 1))}
        strips = [pl.ds(base * LAT + at, ROWS, stride=LAT) for at in (0, LAT - 1)]
        strips = [(strip, e[strip, :]) for strip in strips]
        out = []
        for r in range(ROWS):
            here, k, w, f, old, t4 = rows[r]
            if r in ends:
                w_out, f_out = face(here, *ends[r])
                w, f = w + w_out, f + f_out
            out.append((old + k * (row_share * t4) + (here * w + f), SCALE + k + w))
        for r in range(ROWS):
            numer[tile(base + r), :], denom[tile(base + r), :] = out[r]
        for j, (strip, past) in enumerate(strips):
            w, _ = face(past, halo[j, tile(g), :], edge[j, tile(g), :])
            numer[strip, :] = numer[strip, :] + w * halo[j, tile(g), :]
            denom[strip, :] = denom[strip, :] + w
        return carry

    lax.fori_loop(0, GROUPS, one, 0, unroll=8)

    def two(g, sums):
        at = [tile(g * ROWS + r) for r in range(ROWS)]
        fresh = [numer[i, :] / denom[i, :] for i in at]
        sums = tuple(sums[r] + kap[at[r], :] * fresh[r] for r in range(ROWS))
        for r in range(ROWS):
            enew[at[r], :] = fresh[r]
        return sums

    sums = lax.fori_loop(0, GROUPS, two, (jnp.zeros((LAT, LANES), F32),) * ROWS, unroll=8)
    for r in range(ROWS):
        ksum[tile(r), :] = sums[r]


def own_rows(pos, ref):
    return ref[pl.ds(pl.multiple_of(pos[0] * N, N), N), :]


def terms(told, t, stot):
    cube = t * t * t
    return HEAT * told + 3.0 * stot * (cube * t), HEAT + 4.0 * stot * cube


def outer_first(pos, e, e01, kap, share, told, ssum, flux, weight, h0, h1, h2, h3, *refs):
    enew, sums, edge, t1, t2, r1, r2 = refs[:7]
    temp4, halo, numer, denom = refs[7:]
    slabs = (h0, h1, h2, h3)
    unpack_halos(pos, slabs, TILES, halo)
    for j, at in ((0, 0), (1, LAT - 1)):
        edge[j] = COEF * (kap[pl.ds(at, TILES, stride=LAT), :] + halo[j])
    for g in range(GROUPS):
        for j, at in ((2, 0), (3, ROWS - 1)):
            edge[j, tile(g), :] = COEF * (kap[tile(g * ROWS + at), :] + halo[j, tile(g), :])
    unpack_halos(pos, slabs, 0, halo)
    t = own_rows(pos, told)
    temp4[...] = t * t * t * t
    outer_body(e, e01, kap, share, temp4, halo, edge, flux, weight, enew, sums.at[pl.ds(0, N)], numer, denom)
    sums[pl.ds(N, N), :] = ssum[...]
    write_slabs(pos, enew, 0, t1, t2, r1, r2)


def outer_middle(pos, e, e01, kap, share, told, sums, got, edge, flux, weight, h0, h1, h2, h3, *refs):
    enew, ksum, tnow, stot, t1, t2, r1, r2 = refs[:8]
    temp4, halo, numer, denom = refs[8:]
    unpack_halos(pos, (h0, h1, h2, h3), 0, halo)
    both = (sums[...] + got[...]) / SCALE
    s = both[N:]
    stot[...] = s
    t = own_rows(pos, told)
    up, down = terms(t, t, s)
    t = (up + both[:N]) / down
    tnow[...] = t
    temp4[...] = t * t * t * t
    outer_body(e, e01, kap, share, temp4, halo, edge, flux, weight, enew, ksum, numer, denom)
    write_slabs(pos, enew, 0, t1, t2, r1, r2)


def outer_last(pos, e, e01, kap, share, told, tprev, stot, part, got, edge, flux, weight, h0, h1, h2, h3, *refs):
    eown, send, ksum = refs[:3]
    temp4, halo, numer, denom, enew = refs[3:]
    unpack_halos(pos, (h0, h1, h2, h3), 0, halo)
    s = stot[...]
    old = own_rows(pos, told)
    above, below = terms(old, tprev[...], s)
    t = (above + (part[...] + got[...]) / SCALE) / below
    temp4[...] = t * t * t * t
    outer_body(e, e01, kap, share, temp4, halo, edge, flux, weight, enew, ksum, numer, denom)
    slot = pos[2] % 2
    eown[...] = enew[pl.ds(pl.multiple_of(slot * PART, PART), PART), :]
    send[pl.ds(0, PART), :] = enew[pl.ds(pl.multiple_of((1 - slot) * PART, PART), PART), :]
    up, down = terms(old, t, s)
    send[pl.ds(PART, N), :] = ksum[...]
    send[pl.ds(PART + N, N), :] = up
    send[pl.ds(PART + 2 * N, N), :] = down


def join_kernel(pos, eown, send, pair, near, far, energy, temp):
    half = pos[0]
    for g in range(OWN):
        src = pl.ds(g * N, N)
        energy[pl.ds(pl.multiple_of((2 * g + half) * N, N), N), :] = eown[src, :]
        energy[pl.ds(pl.multiple_of((2 * g + 1 - half) * N, N), N), :] = pair[src, :]
    k, up, down = pl.ds(PART, N), pl.ds(PART + N, N), pl.ds(PART + 2 * N, N)
    temp[pl.ds(pl.multiple_of(half * N, N), N), :] = (send[up, :] + (send[k, :] + near[...]) / SCALE) / send[down, :]
    temp[pl.ds(pl.multiple_of((1 - half) * N, N), N), :] = (pair[up, :] + (pair[k, :] + far[...]) / SCALE) / pair[down, :]


def theta_pairs(count, odd):
    return [p for i in range(odd, count - 1, 2) for p in ((i, i + 1), (i + 1, i))]


def row_pairs(rows, odd):
    def device(chain, position):
        row, part = position // 2, position % 2
        return row * 4 + 2 * chain + (part ^ (row & 1))

    pairs = []
    for chain in range(2):
        for i in range(odd, 2 * rows - 1, 2):
            a, b = device(chain, i), device(chain, i + 1)
            pairs += [(a, b), (b, a)]
    return pairs


def xor(x, k):
    return lax.ppermute(x, "group", [(i, i ^ k) for i in range(4)])


def swap_halos(slabs, part=None):
    t1, t2, r1, r2 = slabs
    nt, nr = lax.axis_size("theta"), lax.axis_size("row")
    t2 = lax.ppermute(t2, "theta", theta_pairs(nt, 1))
    part = part if part is None else keep(xor(part, 2))
    t1 = lax.ppermute(t1, "theta", theta_pairs(nt, 0))
    r2 = lax.ppermute(r2, ("row", "group"), row_pairs(nr, 1))
    r1 = lax.ppermute(r1, ("row", "group"), row_pairs(nr, 0))
    return tuple(keep(x) for x in (t1, t2, r1, r2)), part


def shards(dust, table, planck, energy_old, temp_old):
    place = lax.axis_index("group")
    row = lax.axis_index("row")
    pos = jnp.stack([(place ^ row) & 1, lax.axis_index("theta") & 1, place, row]).astype(jnp.int32)
    dust = dust.reshape(BINS, 2 * N, LANES)
    energy_old = energy_old.reshape(OWN, 2 * N, LANES)
    told = temp_old.reshape(-1, LANES)
    tab = table.astype(F32).reshape(-1)
    slabs = [held((TILES, LANES), BF)] * 4
    scratch = [VMEM((N, LANES), F32), VMEM((4, TILES, LANES), F32), VMEM((CELLS, LANES), F32), VMEM((CELLS, LANES), F32)]
    full = held((CELLS, LANES))
    sheet = held((N, LANES))
    block = held((BINS, N, LANES), BF)

    eown, pair, mine, far = call(
        pack_kernel,
        [held((OWN, N, LANES)), held((SIZE + PART + 6 * LAT, LANES), BF), block, block],
        (pos, *(pltpu.with_memory_space_constraint(x, pltpu.HBM) for x in (planck, dust, energy_old))), smem=1, space=pl.ANY,
        scratch=[VMEM((OWN, N, LANES), F32), SMEM(planck.shape, F32), pltpu.SemaphoreType.DMA((5,))],
    )
    pair = xor(pair, 1)
    near = xor(mine, 2)
    far = xor(far, 3)
    early, e, share = call(
        early_kernel, [full, full, held((2, 2 * LAT, LANES))],
        (pos, tab, planck, keep(mine), keep(pair), keep(far), keep(eown)), smem=3,
        scratch=[VMEM((3 * SIZE, LANES), F32)], flops=20_000_000,
    )
    e = keep(e)
    kap, *both = call(
        late_kernel,
        [full] + [held((2 * TILES, LANES), BF)] * 4,
        (pos, tab, keep(early), keep(near), e), smem=2,
        scratch=[VMEM((SIZE, LANES), F32)], flops=5_000_000,
    )
    kap, share = keep(kap), keep(share)
    halos, _ = swap_halos(both)
    flux, weight, *coefs, e01, ssum = call(
        inner_first, [full] * 6 + [sheet], (pos, e, kap, share), smem=1, flops=20_000_000,
    )
    coefs = [keep(x) for x in coefs]
    e01 = keep(e01)
    e, sums, edge, *rest = call(
        outer_first, [full, held((2 * N, LANES)), held((4, TILES, LANES))] + slabs,
        (pos, e, e01, kap, share, told, keep(ssum), keep(flux), keep(weight), *halos), smem=1,
        scratch=scratch, flops=5_000_000,
    )
    e, edge, sums = keep(e), keep(edge), keep(sums)
    halos, got = swap_halos(rest, sums)
    flux, weight = call(inner_next, [full] * 2, (pos, e, *coefs), smem=1, flops=20_000_000)
    e, part, temp, stot, *rest = call(
        outer_middle, [full, sheet, sheet, sheet] + slabs,
        (pos, e, e01, kap, share, told, sums, got, edge, keep(flux), keep(weight), *halos), smem=1,
        scratch=scratch, flops=5_000_000,
    )
    e, part = keep(e), keep(part)
    halos, got = swap_halos(rest, part)
    flux, weight = call(inner_next, [full] * 2, (pos, e, *coefs), smem=1, flops=20_000_000)
    eown, send, part = call(
        outer_last, [held((PART, LANES)), held((PART + 3 * N, LANES)), sheet],
        (pos, e, e01, kap, share, told, keep(temp), keep(stot), part, got, edge, keep(flux), keep(weight), *halos), smem=1,
        scratch=scratch + [VMEM((CELLS, LANES), F32)], flops=5_000_000,
    )
    pair = xor(send, 1)
    far = xor(part, 3)
    near = xor(part, 2)
    energy, temp = call(
        join_kernel,
        [jax.ShapeDtypeStruct((2 * PART, LANES), F32), jax.ShapeDtypeStruct((2 * N, LANES), F32)],
        (pos, keep(eown), keep(send), keep(pair), keep(near), keep(far)), smem=1,
    )
    return energy.reshape(OWN, 2 * ROWS, LAT, LANES), temp.reshape(2 * ROWS, LAT, LANES)


def solution(mesh):
    return jax.shard_map(
        shards,
        mesh=mesh,
        in_specs=(
            P("group", "row", "theta", None),
            P(),
            P("group"),
            P("group", "row", "theta", None),
            P("row", "theta", None),
        ),
        out_specs=(P("group", "row", "theta", None), P("row", "theta", None)),
        check_vma=False,
    )
```

```python
import jax
import jax.numpy as jnp
from jax import lax
from jax.experimental import pallas as pl
from jax.experimental.pallas import tpu as pltpu
from jax.sharding import PartitionSpec as P


HEAT = 2.0
REACH = 20.0
SCALE = 2.0 / REACH


BF = jnp.bfloat16
F32 = jnp.float32
VMEM = pltpu.VMEM
SMEM = pltpu.SMEM

BINS = 8
OWN = 12
GROUPS = 24
ROWS = 8
LAT = 8
LANES = 128
TILES = GROUPS * ROWS
CELLS = TILES * LAT


def call(kernel, outs, args, smem=0, scratch=(), flops=1_000_000, space=VMEM, aliases=()):
    specs = [pl.BlockSpec(memory_space=SMEM)] * smem
    specs += [pl.BlockSpec(memory_space=space)] * (len(args) - smem)
    return pl.pallas_call(
        kernel,
        out_shape=outs,
        in_specs=specs,
        out_specs=[pl.BlockSpec(memory_space=VMEM)] * len(outs),
        scratch_shapes=list(scratch),
        input_output_aliases=dict(aliases),
        cost_estimate=pl.CostEstimate(flops=flops, bytes_accessed=1_000_000, transcendentals=0),
        compiler_params=pltpu.CompilerParams(vmem_limit_bytes=16 << 20),
    )(*args)


def held(shape, dtype=F32):
    return VMEM(shape, dtype)


def keep(x):
    return pltpu.with_memory_space_constraint(x, VMEM)


def tile(i):
    return pl.ds(pl.multiple_of(i * LAT, LAT), LAT)


UNROLL = 4
SIZE = BINS * ROWS * LAT
PART = OWN * ROWS * LAT
N = ROWS * LAT
COEF = 0.75 / SCALE


def half_rows(half):
    return pl.ds(pl.multiple_of(N * half, N), N)


def pack_kernel(pos, planck, dust, eold, eown, pair, near, far, stage, shares, sems):
    half = pos[0]
    mine = pl.ds(pl.multiple_of(N * half, N), N)
    other = pl.ds(pl.multiple_of(N * (1 - half), N), N)
    copies = [
        pltpu.make_async_copy(dust.at[:, other, :], far, sems.at[0]),
        pltpu.make_async_copy(eold.at[:, other, :], stage, sems.at[1]),
        pltpu.make_async_copy(dust.at[:, mine, :], near, sems.at[2]),
        pltpu.make_async_copy(eold.at[:, mine, :], eown, sems.at[3]),
        pltpu.make_async_copy(planck, shares, sems.at[4]),
    ]
    for copy in copies:
        copy.start()
    copies[0].wait()
    for b in range(BINS):
        pair[pl.ds(b * N, N), :] = far[b]
    copies[1].wait()
    for g in range(OWN):
        pair[pl.ds(SIZE + g * N, N), :] = stage[g].astype(BF)
    copies[4].wait()
    row = lax.broadcasted_iota(jnp.int32, (2 * LAT, LANES), 0)
    share = jnp.zeros((2 * LAT, LANES), F32)
    for g in range(OWN):
        share = jnp.where(row == g, shares[g], share)
    for i in range(3):
        piece = share.astype(BF)
        pair[pl.ds(SIZE + PART + 2 * i * LAT, 2 * LAT), :] = piece
        share = share - piece.astype(F32)
    copies[2].wait()
    copies[3].wait()


def write_slabs(pos, src, at, t1, t2, r1, r2):
    part, tp = pos[0], pos[1]
    low = src[pl.ds(0, TILES, stride=LAT), :].astype(BF)
    high = src[pl.ds(LAT - 1, TILES, stride=LAT), :].astype(BF)
    rows = pl.ds(at, TILES)

    @pl.when(tp == 0)
    def _():
        t1[rows, :] = high
        t2[rows, :] = low

    @pl.when(tp == 1)
    def _():
        t1[rows, :] = low
        t2[rows, :] = high

    for g in range(0, GROUPS, 2):
        def edge(r):
            a = src[tile(g * ROWS + r), :]
            b = src[tile((g + 1) * ROWS + r), :]
            return jnp.concatenate([a, b], axis=0).astype(BF)

        r1[pl.ds(at + g * LAT, 2 * LAT), :] = edge((ROWS - 1) * (1 - part))
        r2[pl.ds(at + g * LAT, 2 * LAT), :] = edge((ROWS - 1) * part)


def gather_bins(tab, wide, place, blocks, g, acc):
    first = (place // 2) * GROUPS
    for j, k in enumerate(blocks):
        source = jnp.bitwise_xor(place, k)
        for b in range(BINS):
            t = SCALE * tab[(source * BINS + b) * 2 * GROUPS + first + g]
            for r in range(ROWS):
                term = t * wide[tile((j * BINS + b) * ROWS + r), :]
                acc[r] = term if acc[r] is None else acc[r] + term
    return acc


def early_kernel(pos, tab, planck, mine, pair, near, eown, kap, e, share, wide):
    place = pos[2]
    slot = place % 2
    for b in range(BINS):
        wide[pl.ds(b * N, N), :] = mine[b].astype(F32)
        wide[pl.ds(SIZE + b * N, N), :] = pair[pl.ds(b * N, N), :].astype(F32)
        wide[pl.ds(2 * SIZE + b * N, N), :] = near[b].astype(F32)

    def one(g, carry):
        acc = gather_bins(tab, wide, place, (0, 1, 2), g, [None] * ROWS)
        for r in range(ROWS):
            kap[tile(g * ROWS + r), :] = acc[r]
        return carry

    lax.fori_loop(0, GROUPS, one, 0, unroll=2)
    for g in range(OWN):
        e[half_rows(slot * OWN + g), :] = eown[g]
        e[half_rows((1 - slot) * OWN + g), :] = pair[pl.ds(SIZE + g * N, N), :].astype(F32)
    at = SIZE + PART
    pieces = [pair[pl.ds(at + 2 * LAT * i, 2 * LAT), :].astype(F32) for i in range(3)]
    row = lax.broadcasted_iota(jnp.int32, (2 * LAT, LANES), 0)
    ours = jnp.zeros((2 * LAT, LANES), F32)
    for g in range(OWN):
        ours = jnp.where(row == g, planck[g], ours)
    share[slot] = ours
    share[1 - slot] = pieces[0] + pieces[1] + pieces[2]


def late_kernel(pos, tab, part, far, e, kap, t1, t2, r1, r2, wide):
    place = pos[2]
    for b in range(BINS):
        wide[pl.ds(b * N, N), :] = far[b].astype(F32)

    def one(g, carry):
        acc = [part[tile(g * ROWS + r), :] for r in range(ROWS)]
        acc = gather_bins(tab, wide, place, (3,), g, acc)
        for r in range(ROWS):
            kap[tile(g * ROWS + r), :] = acc[r]
        return carry

    lax.fori_loop(0, GROUPS, one, 0, unroll=4)
    write_slabs(pos, e, 0, t1, t2, r1, r2)
    write_slabs(pos, kap, TILES, t1, t2, r1, r2)


def face(ea, eb, c):
    d = eb - ea
    w = 1.0 / (c + jnp.abs(d) / (ea + eb))
    return w, w * d


def spread(row):
    return jnp.broadcast_to(row, (LAT, LANES))


def share_of(share, g):
    part = g // OWN
    return spread(share[part, pl.ds(g - part * OWN, 1), :])


def inner_body(e, kap, numer, denom, prepare):
    def one(g, carry):
        base = g * ROWS
        tiles = [e[tile(base + r), :] for r in range(ROWS)]
        ks = [kap[tile(base + r), :] for r in range(ROWS)]
        coef, olds = prepare(g, base, tiles, ks)
        out = []
        for r in range(ROWS):
            here = tiles[r]
            c_up, c_east, c_above = coef[r]
            w_up, f_up = face(here, pltpu.roll(here, LAT - 1, 0), c_up)
            w_east, f_east = face(here, pltpu.roll(here, LANES - 1, 1), c_east)
            w = (w_up + pltpu.roll(w_up, 1, 0)) + (w_east + pltpu.roll(w_east, 1, 1))
            f = (f_up - pltpu.roll(f_up, 1, 0)) + (f_east - pltpu.roll(f_east, 1, 1))
            if r > 0:
                w, f = w + w_below, f - f_below
            if r + 1 < ROWS:
                w_below, f_below = face(here, tiles[r + 1], c_above)
                w, f = w + w_below, f + f_below
            out.append((olds[r] + (here * w + f), SCALE + ks[r] + w))
        for r in range(ROWS):
            numer[tile(base + r), :], denom[tile(base + r), :] = out[r]
        return carry

    lax.fori_loop(0, GROUPS, one, 0, unroll=UNROLL)


def inner_first(pos, e, kap, share, numer, denom, up_c, east_c, above_c, e01, ssum):
    ssum[...] = jnp.zeros_like(ssum)
    top = lax.broadcasted_iota(jnp.int32, (LAT, LANES), 0) == LAT - 1

    def prepare(g, base, tiles, ks):
        sums = [ssum[tile(r), :] for r in range(ROWS)]
        share_row = share_of(share, g)
        olds = [SCALE * x for x in tiles]
        out = []
        for r in range(ROWS):
            k = ks[r]
            c_up = jnp.where(top, jnp.inf, COEF * (k + pltpu.roll(k, LAT - 1, 0)))
            c_east = COEF * (k + pltpu.roll(k, LANES - 1, 1))
            out.append((c_up, c_east, COEF * (k + ks[r + 1]) if r + 1 < ROWS else None))
        for r in range(ROWS):
            i = base + r
            up_c[tile(i), :], east_c[tile(i), :] = out[r][:2]
            if r + 1 < ROWS:
                above_c[tile(i), :] = out[r][2]
            e01[tile(i), :] = olds[r]
            ssum[tile(r), :] = sums[r] + ks[r] * share_row
        return out, olds

    inner_body(e, kap, numer, denom, prepare)


def inner_next(pos, e, kap, e01, up_c, east_c, above_c, numer, denom):
    def prepare(g, base, tiles, ks):
        at = [tile(base + r) for r in range(ROWS)]
        return [(up_c[i, :], east_c[i, :], above_c[i, :]) for i in at], [e01[i, :] for i in at]

    inner_body(e, kap, numer, denom, prepare)


def unpack_halos(pos, slabs, at, halo):
    part, tp = pos[0], pos[1]
    rows = pl.ds(at, TILES)
    halo[1 - tp] = slabs[0][rows, :].astype(F32)
    halo[tp] = slabs[1][rows, :].astype(F32)
    halo[3 - part] = slabs[2][rows, :].astype(F32)
    halo[2 + part] = slabs[3][rows, :].astype(F32)


def outer_body(e, kap, share, temp4, halo, edge, numer, denom, enew, ksum):
    def close(g, carry):
        lows = tile(g)
        base = g * ROWS * LAT
        places = [pl.ds(base, ROWS, stride=LAT), pl.ds(base + LAT - 1, ROWS, stride=LAT)]
        places += [tile(g * ROWS), tile(g * ROWS + ROWS - 1)]
        pasts = [e[i, :] for i in places]
        outs = [halo[j, lows, :] for j in range(4)]
        ws = [face(pasts[j], outs[j], edge[j, lows, :])[0] for j in range(4)]
        for j, i in enumerate(places):
            numer[i, :] = numer[i, :] + ws[j] * outs[j]
            denom[i, :] = denom[i, :] + ws[j]
        return carry

    lax.fori_loop(0, GROUPS, close, 0, unroll=8)

    def finish(g, sums):
        row_share = share_of(share, g)
        at = [tile(g * ROWS + r) for r in range(ROWS)]
        ks = [kap[i, :] for i in at]
        fresh = [(numer[at[r], :] + ks[r] * (row_share * temp4[tile(r), :])) / denom[at[r], :] for r in range(ROWS)]
        sums = tuple(sums[r] + ks[r] * fresh[r] for r in range(ROWS))
        for r in range(ROWS):
            enew[at[r], :] = fresh[r]
        return sums

    sums = lax.fori_loop(0, GROUPS, finish, (jnp.zeros((LAT, LANES), F32),) * ROWS, unroll=8)
    for r in range(ROWS):
        ksum[tile(r), :] = sums[r]


def own_rows(pos, ref):
    return ref[pl.ds(pl.multiple_of(pos[0] * N, N), N), :]


def terms(told, t, stot):
    cube = t * t * t
    return HEAT * told + 3.0 * stot * (cube * t), HEAT + 4.0 * stot * cube


def outer_first(pos, e, kap, share, told, ssum, numer_in, denom_in, h0, h1, h2, h3, *refs):
    enew, sums, edge, t1, t2, r1, r2, numer, denom = refs[:9]
    temp4, halo = refs[9:]
    slabs = (h0, h1, h2, h3)
    unpack_halos(pos, slabs, TILES, halo)
    for j, at in ((0, 0), (1, LAT - 1)):
        edge[j] = COEF * (kap[pl.ds(at, TILES, stride=LAT), :] + halo[j])
    for g in range(GROUPS):
        for j, at in ((2, 0), (3, ROWS - 1)):
            edge[j, tile(g), :] = COEF * (kap[tile(g * ROWS + at), :] + halo[j, tile(g), :])
    unpack_halos(pos, slabs, 0, halo)
    t = own_rows(pos, told)
    temp4[...] = t * t * t * t
    outer_body(e, kap, share, temp4, halo, edge, numer, denom, enew, sums.at[pl.ds(0, N)])
    sums[pl.ds(N, N), :] = ssum[...]
    write_slabs(pos, enew, 0, t1, t2, r1, r2)


def outer_middle(pos, e, kap, share, told, sums, got, edge, numer_in, denom_in, h0, h1, h2, h3, *refs):
    enew, ksum, tnow, stot, t1, t2, r1, r2, numer, denom = refs[:10]
    temp4, halo = refs[10:]
    unpack_halos(pos, (h0, h1, h2, h3), 0, halo)
    both = (sums[...] + got[...]) / SCALE
    s = both[N:]
    stot[...] = s
    t = own_rows(pos, told)
    up, down = terms(t, t, s)
    t = (up + both[:N]) / down
    tnow[...] = t
    temp4[...] = t * t * t * t
    outer_body(e, kap, share, temp4, halo, edge, numer, denom, enew, ksum)
    write_slabs(pos, enew, 0, t1, t2, r1, r2)


def outer_last(pos, e, kap, share, told, tprev, stot, part, got, edge, numer_in, denom_in, h0, h1, h2, h3, *refs):
    eown, send, ksum, numer, denom = refs[:5]
    temp4, halo, enew = refs[5:]
    unpack_halos(pos, (h0, h1, h2, h3), 0, halo)
    s = stot[...]
    old = own_rows(pos, told)
    above, below = terms(old, tprev[...], s)
    t = (above + (part[...] + got[...]) / SCALE) / below
    temp4[...] = t * t * t * t
    outer_body(e, kap, share, temp4, halo, edge, numer, denom, enew, ksum)
    slot = pos[2] % 2
    eown[...] = enew[pl.ds(pl.multiple_of(slot * PART, PART), PART), :]
    send[pl.ds(0, PART), :] = enew[pl.ds(pl.multiple_of((1 - slot) * PART, PART), PART), :]
    up, down = terms(old, t, s)
    send[pl.ds(PART, N), :] = ksum[...]
    send[pl.ds(PART + N, N), :] = up
    send[pl.ds(PART + 2 * N, N), :] = down


def join_kernel(pos, eown, send, pair, near, far, energy, temp):
    half = pos[0]
    for g in range(OWN):
        src = pl.ds(g * N, N)
        energy[pl.ds(pl.multiple_of((2 * g + half) * N, N), N), :] = eown[src, :]
        energy[pl.ds(pl.multiple_of((2 * g + 1 - half) * N, N), N), :] = pair[src, :]
    k, up, down = pl.ds(PART, N), pl.ds(PART + N, N), pl.ds(PART + 2 * N, N)
    temp[pl.ds(pl.multiple_of(half * N, N), N), :] = (send[up, :] + (send[k, :] + near[...]) / SCALE) / send[down, :]
    temp[pl.ds(pl.multiple_of((1 - half) * N, N), N), :] = (pair[up, :] + (pair[k, :] + far[...]) / SCALE) / pair[down, :]


def theta_pairs(count, odd):
    return [p for i in range(odd, count - 1, 2) for p in ((i, i + 1), (i + 1, i))]


def row_pairs(rows, odd):
    def device(chain, position):
        row, part = position // 2, position % 2
        return row * 4 + 2 * chain + (part ^ (row & 1))

    pairs = []
    for chain in range(2):
        for i in range(odd, 2 * rows - 1, 2):
            a, b = device(chain, i), device(chain, i + 1)
            pairs += [(a, b), (b, a)]
    return pairs


def xor(x, k):
    return lax.ppermute(x, "group", [(i, i ^ k) for i in range(4)])


def swap_halos(slabs, part=None):
    t1, t2, r1, r2 = slabs
    nt, nr = lax.axis_size("theta"), lax.axis_size("row")
    t2 = lax.ppermute(t2, "theta", theta_pairs(nt, 1))
    part = part if part is None else keep(xor(part, 2))
    t1 = lax.ppermute(t1, "theta", theta_pairs(nt, 0))
    r2 = lax.ppermute(r2, ("row", "group"), row_pairs(nr, 1))
    r1 = lax.ppermute(r1, ("row", "group"), row_pairs(nr, 0))
    return tuple(keep(x) for x in (t1, t2, r1, r2)), part


def shards(dust, table, planck, energy_old, temp_old):
    place = lax.axis_index("group")
    row = lax.axis_index("row")
    pos = jnp.stack([(place ^ row) & 1, lax.axis_index("theta") & 1, place, row]).astype(jnp.int32)
    dust = dust.reshape(BINS, 2 * N, LANES)
    energy_old = energy_old.reshape(OWN, 2 * N, LANES)
    told = temp_old.reshape(-1, LANES)
    tab = table.astype(F32).reshape(-1)
    slabs = [held((TILES, LANES), BF)] * 4
    scratch = [VMEM((N, LANES), F32), VMEM((4, TILES, LANES), F32)]
    full = held((CELLS, LANES))
    sheet = held((N, LANES))
    block = held((BINS, N, LANES), BF)

    eown, pair, mine, far = call(
        pack_kernel,
        [held((OWN, N, LANES)), held((SIZE + PART + 6 * LAT, LANES), BF), block, block],
        (pos, *(pltpu.with_memory_space_constraint(x, pltpu.HBM) for x in (planck, dust, energy_old))), smem=1, space=pl.ANY,
        scratch=[VMEM((OWN, N, LANES), F32), SMEM(planck.shape, F32), pltpu.SemaphoreType.DMA((5,))],
    )
    pair = xor(pair, 1)
    near = xor(mine, 2)
    far = xor(far, 3)
    early, e, share = call(
        early_kernel, [full, full, held((2, 2 * LAT, LANES))],
        (pos, tab, planck, keep(mine), keep(pair), keep(near), keep(eown)), smem=3,
        scratch=[VMEM((3 * SIZE, LANES), F32)], flops=20_000_000,
    )
    e = keep(e)
    kap, *both = call(
        late_kernel,
        [full] + [held((2 * TILES, LANES), BF)] * 4,
        (pos, tab, keep(early), keep(far), e), smem=2,
        scratch=[VMEM((SIZE, LANES), F32)], flops=5_000_000,
    )
    kap, share = keep(kap), keep(share)
    halos, _ = swap_halos(both)
    numer, denom, *coefs, e01, ssum = call(
        inner_first, [full] * 6 + [sheet], (pos, e, kap, share), smem=1, flops=20_000_000,
    )
    coefs = [keep(x) for x in coefs]
    e01 = keep(e01)
    e, sums, edge, *rest = call(
        outer_first, [full, held((2 * N, LANES)), held((4, TILES, LANES))] + slabs + [full, full],
        (pos, e, kap, share, told, keep(ssum), keep(numer), keep(denom), *halos), smem=1,
        scratch=scratch, flops=5_000_000, aliases=((6, 7), (7, 8)),
    )
    rest = rest[:4]
    e, edge, sums = keep(e), keep(edge), keep(sums)
    halos, got = swap_halos(rest, sums)
    numer, denom = call(inner_next, [full] * 2, (pos, e, kap, e01, *coefs), smem=1, flops=20_000_000)
    e, part, temp, stot, *rest = call(
        outer_middle, [full, sheet, sheet, sheet] + slabs + [full, full],
        (pos, e, kap, share, told, sums, got, edge, keep(numer), keep(denom), *halos), smem=1,
        scratch=scratch, flops=5_000_000, aliases=((8, 8), (9, 9)),
    )
    rest = rest[:4]
    e, part = keep(e), keep(part)
    halos, got = swap_halos(rest, part)
    numer, denom = call(inner_next, [full] * 2, (pos, e, kap, e01, *coefs), smem=1, flops=20_000_000)
    eown, send, part, _, _ = call(
        outer_last, [held((PART, LANES)), held((PART + 3 * N, LANES)), sheet, full, full],
        (pos, e, kap, share, told, keep(temp), keep(stot), part, got, edge, keep(numer), keep(denom), *halos), smem=1,
        scratch=scratch + [VMEM((CELLS, LANES), F32)], flops=5_000_000, aliases=((10, 3), (11, 4)),
    )
    pair = xor(send, 1)
    far = xor(part, 3)
    near = xor(part, 2)
    energy, temp = call(
        join_kernel,
        [jax.ShapeDtypeStruct((2 * PART, LANES), F32), jax.ShapeDtypeStruct((2 * N, LANES), F32)],
        (pos, keep(eown), keep(send), keep(pair), keep(near), keep(far)), smem=1,
    )
    return energy.reshape(OWN, 2 * ROWS, LAT, LANES), temp.reshape(2 * ROWS, LAT, LANES)


def solution(mesh):
    return jax.shard_map(
        shards,
        mesh=mesh,
        in_specs=(
            P("group", "row", "theta", None),
            P(),
            P("group"),
            P("group", "row", "theta", None),
            P("row", "theta", None),
        ),
        out_specs=(P("group", "row", "theta", None), P("row", "theta", None)),
        check_vma=False,
    )
```

```python
import jax
import jax.numpy as jnp
from jax import lax
from jax.experimental import pallas as pl
from jax.experimental.pallas import tpu as pltpu
from jax.sharding import PartitionSpec as P


HEAT = 2.0
REACH = 20.0
SCALE = 2.0 / REACH


BF = jnp.bfloat16
F32 = jnp.float32
VMEM = pltpu.VMEM
SMEM = pltpu.SMEM

BINS = 8
OWN = 12
GROUPS = 24
ROWS = 8
LAT = 8
LANES = 128
TILES = GROUPS * ROWS
CELLS = TILES * LAT


def call(kernel, outs, args, smem=0, scratch=(), flops=1_000_000, space=VMEM, aliases=()):
    specs = [pl.BlockSpec(memory_space=SMEM)] * smem
    specs += [pl.BlockSpec(memory_space=space)] * (len(args) - smem)
    return pl.pallas_call(
        kernel,
        out_shape=outs,
        in_specs=specs,
        out_specs=[pl.BlockSpec(memory_space=VMEM)] * len(outs),
        scratch_shapes=list(scratch),
        input_output_aliases=dict(aliases),
        cost_estimate=pl.CostEstimate(flops=flops, bytes_accessed=1_000_000, transcendentals=0),
        compiler_params=pltpu.CompilerParams(vmem_limit_bytes=16 << 20),
    )(*args)


def held(shape, dtype=F32):
    return VMEM(shape, dtype)


def keep(x):
    return pltpu.with_memory_space_constraint(x, VMEM)


def tile(i):
    return pl.ds(pl.multiple_of(i * LAT, LAT), LAT)


UNROLL = 4
AHEAD = 4
SIZE = BINS * ROWS * LAT
PART = OWN * ROWS * LAT
N = ROWS * LAT
COEF = 0.75 / SCALE


def half_rows(half):
    return pl.ds(pl.multiple_of(N * half, N), N)


def pack_kernel(pos, planck, dust, eold, eown, pair, near, far, stage, shares, sems):
    half = pos[0]
    mine = pl.ds(pl.multiple_of(N * half, N), N)
    other = pl.ds(pl.multiple_of(N * (1 - half), N), N)
    copies = [
        pltpu.make_async_copy(dust.at[:, other, :], far, sems.at[0]),
        pltpu.make_async_copy(eold.at[:, other, :], stage, sems.at[1]),
        pltpu.make_async_copy(dust.at[:, mine, :], near, sems.at[2]),
        pltpu.make_async_copy(eold.at[:, mine, :], eown, sems.at[3]),
        pltpu.make_async_copy(planck, shares, sems.at[4]),
    ]
    for copy in copies:
        copy.start()
    copies[0].wait()
    for b in range(BINS):
        pair[pl.ds(b * N, N), :] = far[b]
    copies[1].wait()
    for g in range(OWN):
        pair[pl.ds(SIZE + g * N, N), :] = stage[g].astype(BF)
    copies[4].wait()
    row = lax.broadcasted_iota(jnp.int32, (2 * LAT, LANES), 0)
    share = jnp.zeros((2 * LAT, LANES), F32)
    for g in range(OWN):
        share = jnp.where(row == g, shares[g], share)
    for i in range(3):
        piece = share.astype(BF)
        pair[pl.ds(SIZE + PART + 2 * i * LAT, 2 * LAT), :] = piece
        share = share - piece.astype(F32)
    copies[2].wait()
    copies[3].wait()


def write_slabs(pos, src, at, t1, t2, r1, r2):
    part, tp = pos[0], pos[1]
    low = src[pl.ds(0, TILES, stride=LAT), :].astype(BF)
    high = src[pl.ds(LAT - 1, TILES, stride=LAT), :].astype(BF)
    rows = pl.ds(at, TILES)

    @pl.when(tp == 0)
    def _():
        t1[rows, :] = high
        t2[rows, :] = low

    @pl.when(tp == 1)
    def _():
        t1[rows, :] = low
        t2[rows, :] = high

    for g in range(0, GROUPS, 2):
        def edge(r):
            a = src[tile(g * ROWS + r), :]
            b = src[tile((g + 1) * ROWS + r), :]
            return jnp.concatenate([a, b], axis=0).astype(BF)

        r1[pl.ds(at + g * LAT, 2 * LAT), :] = edge((ROWS - 1) * (1 - part))
        r2[pl.ds(at + g * LAT, 2 * LAT), :] = edge((ROWS - 1) * part)


def gather_bins(tab, wide, place, blocks, g, acc):
    first = (place // 2) * GROUPS
    for j, k in enumerate(blocks):
        source = jnp.bitwise_xor(place, k)
        for b in range(BINS):
            t = SCALE * tab[(source * BINS + b) * 2 * GROUPS + first + g]
            for r in range(ROWS):
                term = t * wide[tile((j * BINS + b) * ROWS + r), :]
                acc[r] = term if acc[r] is None else acc[r] + term
    return acc


def early_kernel(pos, tab, planck, mine, pair, near, eown, kap, e, share, wide):
    place = pos[2]
    slot = place % 2
    for b in range(BINS):
        wide[pl.ds(b * N, N), :] = mine[b].astype(F32)
        wide[pl.ds(SIZE + b * N, N), :] = pair[pl.ds(b * N, N), :].astype(F32)
        wide[pl.ds(2 * SIZE + b * N, N), :] = near[b].astype(F32)

    def one(g, carry):
        acc = gather_bins(tab, wide, place, (0, 1, 2), g, [None] * ROWS)
        for r in range(ROWS):
            kap[tile(g * ROWS + r), :] = acc[r]
        return carry

    lax.fori_loop(0, GROUPS, one, 0, unroll=2)
    for g in range(OWN):
        e[half_rows(slot * OWN + g), :] = eown[g]
        e[half_rows((1 - slot) * OWN + g), :] = pair[pl.ds(SIZE + g * N, N), :].astype(F32)
    at = SIZE + PART
    pieces = [pair[pl.ds(at + 2 * LAT * i, 2 * LAT), :].astype(F32) for i in range(3)]
    row = lax.broadcasted_iota(jnp.int32, (2 * LAT, LANES), 0)
    ours = jnp.zeros((2 * LAT, LANES), F32)
    for g in range(OWN):
        ours = jnp.where(row == g, planck[g], ours)
    share[slot] = ours
    share[1 - slot] = pieces[0] + pieces[1] + pieces[2]


def late_kernel(pos, tab, part, far, e, kap, t1, t2, r1, r2, wide):
    place = pos[2]
    for b in range(BINS):
        wide[pl.ds(b * N, N), :] = far[b].astype(F32)

    def one(g, carry):
        acc = [part[tile(g * ROWS + r), :] for r in range(ROWS)]
        acc = gather_bins(tab, wide, place, (3,), g, acc)
        for r in range(ROWS):
            kap[tile(g * ROWS + r), :] = acc[r]
        return carry

    lax.fori_loop(0, GROUPS, one, 0, unroll=4)
    write_slabs(pos, e, 0, t1, t2, r1, r2)
    write_slabs(pos, kap, TILES, t1, t2, r1, r2)


def face(ea, eb, c):
    d = eb - ea
    w = 1.0 / (c + jnp.abs(d) / (ea + eb))
    return w, w * d


def spread(row):
    return jnp.broadcast_to(row, (LAT, LANES))


def share_of(share, g):
    part = g // OWN
    return spread(share[part, pl.ds(g - part * OWN, 1), :])


def inner_body(e, kap, numer, denom, prepare):
    def one(g, carry):
        base = g * ROWS
        tiles = [e[tile(base + r), :] for r in range(ROWS)]
        ks = [kap[tile(base + r), :] for r in range(ROWS)]
        coef, olds = prepare(g, base, tiles, ks)
        out = []
        for r in range(ROWS):
            here = tiles[r]
            c_up, c_east, c_above = coef[r]
            w_up, f_up = face(here, pltpu.roll(here, LAT - 1, 0), c_up)
            w_east, f_east = face(here, pltpu.roll(here, LANES - 1, 1), c_east)
            w = (w_up + pltpu.roll(w_up, 1, 0)) + (w_east + pltpu.roll(w_east, 1, 1))
            f = (f_up - pltpu.roll(f_up, 1, 0)) + (f_east - pltpu.roll(f_east, 1, 1))
            if r > 0:
                w, f = w + w_below, f - f_below
            if r + 1 < ROWS:
                w_below, f_below = face(here, tiles[r + 1], c_above)
                w, f = w + w_below, f + f_below
            out.append((olds[r] + (here * w + f), SCALE + ks[r] + w))
        for r in range(ROWS):
            numer[tile(base + r), :], denom[tile(base + r), :] = out[r]
        return carry

    lax.fori_loop(0, GROUPS, one, 0, unroll=UNROLL)


def inner_first(pos, e, kap, share, numer, denom, up_c, east_c, above_c, e01, ssum):
    ssum[...] = jnp.zeros_like(ssum)
    top = lax.broadcasted_iota(jnp.int32, (LAT, LANES), 0) == LAT - 1

    def prepare(g, base, tiles, ks):
        sums = [ssum[tile(r), :] for r in range(ROWS)]
        share_row = share_of(share, g)
        olds = [SCALE * x for x in tiles]
        out = []
        for r in range(ROWS):
            k = ks[r]
            c_up = jnp.where(top, jnp.inf, COEF * (k + pltpu.roll(k, LAT - 1, 0)))
            c_east = COEF * (k + pltpu.roll(k, LANES - 1, 1))
            out.append((c_up, c_east, COEF * (k + ks[r + 1]) if r + 1 < ROWS else None))
        for r in range(ROWS):
            i = base + r
            up_c[tile(i), :], east_c[tile(i), :] = out[r][:2]
            if r + 1 < ROWS:
                above_c[tile(i), :] = out[r][2]
            e01[tile(i), :] = olds[r]
            ssum[tile(r), :] = sums[r] + ks[r] * share_row
        return out, olds

    inner_body(e, kap, numer, denom, prepare)


def inner_next(pos, e, kap, e01, up_c, east_c, above_c, numer, denom):
    def prepare(g, base, tiles, ks):
        at = [tile(base + r) for r in range(ROWS)]
        return [(up_c[i, :], east_c[i, :], above_c[i, :]) for i in at], [e01[i, :] for i in at]

    inner_body(e, kap, numer, denom, prepare)


def unpack_halos(pos, slabs, at, halo):
    part, tp = pos[0], pos[1]
    rows = pl.ds(at, TILES)
    halo[1 - tp] = slabs[0][rows, :].astype(F32)
    halo[tp] = slabs[1][rows, :].astype(F32)
    halo[3 - part] = slabs[2][rows, :].astype(F32)
    halo[2 + part] = slabs[3][rows, :].astype(F32)


def outer_body(e, kap, share, temp4, halo, edge, numer, denom, enew, ksum):
    def close(g, carry):
        lows = tile(g)
        base = g * ROWS * LAT
        places = [pl.ds(base, ROWS, stride=LAT), pl.ds(base + LAT - 1, ROWS, stride=LAT)]
        places += [tile(g * ROWS), tile(g * ROWS + ROWS - 1)]
        pasts = [e[i, :] for i in places]
        outs = [halo[j, lows, :] for j in range(4)]
        ws = [face(pasts[j], outs[j], edge[j, lows, :])[0] for j in range(4)]
        for j, i in enumerate(places):
            numer[i, :] = numer[i, :] + ws[j] * outs[j]
            denom[i, :] = denom[i, :] + ws[j]
        return carry

    lax.fori_loop(0, GROUPS, close, 0, unroll=8)

    def finish(g, sums):
        row_share = share_of(share, g)
        at = [tile(g * ROWS + r) for r in range(ROWS)]
        ks = [kap[i, :] for i in at]
        fresh = [(numer[at[r], :] + ks[r] * (row_share * temp4[tile(r), :])) / denom[at[r], :] for r in range(ROWS)]
        sums = tuple(sums[r] + ks[r] * fresh[r] for r in range(ROWS))
        for r in range(ROWS):
            enew[at[r], :] = fresh[r]
        return sums

    sums = lax.fori_loop(0, GROUPS, finish, (jnp.zeros((LAT, LANES), F32),) * ROWS, unroll=8)
    for r in range(ROWS):
        ksum[tile(r), :] = sums[r]


def own_rows(pos, ref):
    return ref[pl.ds(pl.multiple_of(pos[0] * N, N), N), :]


def terms(told, t, stot):
    cube = t * t * t
    return HEAT * told + 3.0 * stot * (cube * t), HEAT + 4.0 * stot * cube


def outer_first(pos, e, kap, share, told, ssum, numer_in, denom_in, h0, h1, h2, h3, *refs):
    enew, sums, edge, t1, t2, r1, r2, numer, denom = refs[:9]
    temp4, halo = refs[9:]
    slabs = (h0, h1, h2, h3)
    unpack_halos(pos, slabs, TILES, halo)
    for j, at in ((0, 0), (1, LAT - 1)):
        edge[j] = COEF * (kap[pl.ds(at, TILES, stride=LAT), :] + halo[j])
    for g in range(GROUPS):
        for j, at in ((2, 0), (3, ROWS - 1)):
            edge[j, tile(g), :] = COEF * (kap[tile(g * ROWS + at), :] + halo[j, tile(g), :])
    unpack_halos(pos, slabs, 0, halo)
    t = own_rows(pos, told)
    temp4[...] = t * t * t * t
    outer_body(e, kap, share, temp4, halo, edge, numer, denom, enew, sums.at[pl.ds(0, N)])
    sums[pl.ds(N, N), :] = ssum[...]
    write_slabs(pos, enew, 0, t1, t2, r1, r2)


def outer_middle(pos, e, kap, share, told, sums, got, edge, numer_in, denom_in, h0, h1, h2, h3, *refs):
    enew, ksum, tnow, stot, t1, t2, r1, r2, numer, denom = refs[:10]
    temp4, halo = refs[10:]
    unpack_halos(pos, (h0, h1, h2, h3), 0, halo)
    both = (sums[...] + got[...]) / SCALE
    s = both[N:]
    stot[...] = s
    t = own_rows(pos, told)
    up, down = terms(t, t, s)
    t = (up + both[:N]) / down
    tnow[...] = t
    temp4[...] = t * t * t * t
    outer_body(e, kap, share, temp4, halo, edge, numer, denom, enew, ksum)
    write_slabs(pos, enew, 0, t1, t2, r1, r2)


def outer_last(pos, e, kap, share, told, tprev, stot, part, got, edge, numer_in, denom_in, h0, h1, h2, h3, *refs):
    eown, ahead, behind, ksum, up, down, numer, denom = refs[:8]
    temp4, halo, enew = refs[8:]
    unpack_halos(pos, (h0, h1, h2, h3), 0, halo)
    s = stot[...]
    old = own_rows(pos, told)
    above, below = terms(old, tprev[...], s)
    t = (above + (part[...] + got[...]) / SCALE) / below
    temp4[...] = t * t * t * t
    outer_body(e, kap, share, temp4, halo, edge, numer, denom, enew, ksum)
    slot = pos[2] % 2
    eown[...] = enew[pl.ds(pl.multiple_of(slot * PART, PART), PART), :]
    theirs = pl.multiple_of((1 - slot) * PART, PART)
    ahead[...] = enew[pl.ds(theirs, AHEAD * N), :]
    behind[...] = enew[pl.ds(pl.multiple_of(theirs + AHEAD * N, N), PART - AHEAD * N), :]
    up[...], down[...] = terms(old, t, s)


def finish_kernel(ksum, got, up, down, temp):
    temp[...] = (up[...] + (ksum[...] + got[...]) / SCALE) / down[...]


def join_kernel(pos, eown, ahead, behind, mine, other, energy, temp):
    half = pos[0]
    for g in range(OWN):
        energy[half_rows(2 * g + half), :] = eown[pl.ds(g * N, N), :]
        src, at = (ahead, g) if g < AHEAD else (behind, g - AHEAD)
        energy[half_rows(2 * g + 1 - half), :] = src[pl.ds(at * N, N), :]
    temp[half_rows(half), :] = mine[...]
    temp[half_rows(1 - half), :] = other[...]


def theta_pairs(count, odd):
    return [p for i in range(odd, count - 1, 2) for p in ((i, i + 1), (i + 1, i))]


def row_pairs(rows, odd):
    def device(chain, position):
        row, part = position // 2, position % 2
        return row * 4 + 2 * chain + (part ^ (row & 1))

    pairs = []
    for chain in range(2):
        for i in range(odd, 2 * rows - 1, 2):
            a, b = device(chain, i), device(chain, i + 1)
            pairs += [(a, b), (b, a)]
    return pairs


def xor(x, k):
    return lax.ppermute(x, "group", [(i, i ^ k) for i in range(4)])


def swap_halos(slabs, part=None):
    t1, t2, r1, r2 = slabs
    nt, nr = lax.axis_size("theta"), lax.axis_size("row")
    t2 = lax.ppermute(t2, "theta", theta_pairs(nt, 1))
    part = part if part is None else keep(xor(part, 2))
    t1 = lax.ppermute(t1, "theta", theta_pairs(nt, 0))
    r2 = lax.ppermute(r2, ("row", "group"), row_pairs(nr, 1))
    r1 = lax.ppermute(r1, ("row", "group"), row_pairs(nr, 0))
    return tuple(keep(x) for x in (t1, t2, r1, r2)), part


def shards(dust, table, planck, energy_old, temp_old):
    place = lax.axis_index("group")
    row = lax.axis_index("row")
    pos = jnp.stack([(place ^ row) & 1, lax.axis_index("theta") & 1, place, row]).astype(jnp.int32)
    dust = dust.reshape(BINS, 2 * N, LANES)
    energy_old = energy_old.reshape(OWN, 2 * N, LANES)
    told = temp_old.reshape(-1, LANES)
    tab = table.astype(F32).reshape(-1)
    slabs = [held((TILES, LANES), BF)] * 4
    scratch = [VMEM((N, LANES), F32), VMEM((4, TILES, LANES), F32)]
    full = held((CELLS, LANES))
    sheet = held((N, LANES))
    block = held((BINS, N, LANES), BF)

    eown, pair, mine, far = call(
        pack_kernel,
        [held((OWN, N, LANES)), held((SIZE + PART + 6 * LAT, LANES), BF), block, block],
        (pos, *(pltpu.with_memory_space_constraint(x, pltpu.HBM) for x in (planck, dust, energy_old))), smem=1, space=pl.ANY,
        scratch=[VMEM((OWN, N, LANES), F32), SMEM(planck.shape, F32), pltpu.SemaphoreType.DMA((5,))],
    )
    pair = xor(pair, 1)
    near = xor(mine, 2)
    far = xor(far, 3)
    early, e, share = call(
        early_kernel, [full, full, held((2, 2 * LAT, LANES))],
        (pos, tab, planck, keep(mine), keep(pair), keep(near), keep(eown)), smem=3,
        scratch=[VMEM((3 * SIZE, LANES), F32)], flops=20_000_000,
    )
    e = keep(e)
    kap, *both = call(
        late_kernel,
        [full] + [held((2 * TILES, LANES), BF)] * 4,
        (pos, tab, keep(early), keep(far), e), smem=2,
        scratch=[VMEM((SIZE, LANES), F32)], flops=5_000_000,
    )
    kap, share = keep(kap), keep(share)
    halos, _ = swap_halos(both)
    numer, denom, *coefs, e01, ssum = call(
        inner_first, [full] * 6 + [sheet], (pos, e, kap, share), smem=1, flops=20_000_000,
    )
    coefs = [keep(x) for x in coefs]
    e01 = keep(e01)
    e, sums, edge, *rest = call(
        outer_first, [full, held((2 * N, LANES)), held((4, TILES, LANES))] + slabs + [full, full],
        (pos, e, kap, share, told, keep(ssum), keep(numer), keep(denom), *halos), smem=1,
        scratch=scratch, flops=5_000_000, aliases=((6, 7), (7, 8)),
    )
    rest = rest[:4]
    e, edge, sums = keep(e), keep(edge), keep(sums)
    halos, got = swap_halos(rest, sums)
    numer, denom = call(inner_next, [full] * 2, (pos, e, kap, e01, *coefs), smem=1, flops=20_000_000)
    e, part, temp, stot, *rest = call(
        outer_middle, [full, sheet, sheet, sheet] + slabs + [full, full],
        (pos, e, kap, share, told, sums, got, edge, keep(numer), keep(denom), *halos), smem=1,
        scratch=scratch, flops=5_000_000, aliases=((8, 8), (9, 9)),
    )
    rest = rest[:4]
    e, part = keep(e), keep(part)
    halos, got = swap_halos(rest, part)
    numer, denom = call(inner_next, [full] * 2, (pos, e, kap, e01, *coefs), smem=1, flops=20_000_000)
    eown, ahead, behind, part, up, down, _, _ = call(
        outer_last,
        [held((PART, LANES)), held((AHEAD * N, LANES)), held((PART - AHEAD * N, LANES)), sheet, sheet, sheet, full, full],
        (pos, e, kap, share, told, keep(temp), keep(stot), part, got, edge, keep(numer), keep(denom), *halos), smem=1,
        scratch=scratch + [VMEM((CELLS, LANES), F32)], flops=5_000_000, aliases=((10, 6), (11, 7)),
    )
    ahead = xor(ahead, 1)
    got = xor(part, 2)
    behind = xor(behind, 1)
    mine, = call(finish_kernel, [sheet], [keep(x) for x in (part, got, up, down)])
    other = xor(mine, 1)
    energy, temp = call(
        join_kernel,
        [jax.ShapeDtypeStruct((2 * PART, LANES), F32), jax.ShapeDtypeStruct((2 * N, LANES), F32)],
        (pos, *(keep(x) for x in (eown, ahead, behind, mine, other))), smem=1,
    )
    return energy.reshape(OWN, 2 * ROWS, LAT, LANES), temp.reshape(2 * ROWS, LAT, LANES)


def solution(mesh):
    return jax.shard_map(
        shards,
        mesh=mesh,
        in_specs=(
            P("group", "row", "theta", None),
            P(),
            P("group"),
            P("group", "row", "theta", None),
            P("row", "theta", None),
        ),
        out_specs=(P("group", "row", "theta", None), P("row", "theta", None)),
        check_vma=False,
    )
```

```python
import jax
import jax.numpy as jnp
from jax import lax
from jax.experimental import pallas as pl
from jax.experimental.pallas import tpu as pltpu
from jax.sharding import PartitionSpec as P


HEAT = 2.0
REACH = 20.0
SCALE = 2.0 / REACH


BF = jnp.bfloat16
F32 = jnp.float32
VMEM = pltpu.VMEM
SMEM = pltpu.SMEM

BINS = 8
OWN = 12
GROUPS = 24
ROWS = 8
LAT = 8
LANES = 128
TILES = GROUPS * ROWS
CELLS = TILES * LAT


def call(kernel, outs, args, smem=0, scratch=(), flops=1_000_000, space=VMEM, aliases=(), hbm=0):
    specs = [pl.BlockSpec(memory_space=SMEM)] * smem
    specs += [pl.BlockSpec(memory_space=space)] * (len(args) - smem - hbm)
    specs += [pl.BlockSpec(memory_space=pl.ANY)] * hbm
    return pl.pallas_call(
        kernel,
        out_shape=outs,
        in_specs=specs,
        out_specs=[pl.BlockSpec(memory_space=VMEM)] * len(outs),
        scratch_shapes=list(scratch),
        input_output_aliases=dict(aliases),
        cost_estimate=pl.CostEstimate(flops=flops, bytes_accessed=1_000_000, transcendentals=0),
        compiler_params=pltpu.CompilerParams(vmem_limit_bytes=16 << 20),
    )(*args)


def held(shape, dtype=F32):
    return VMEM(shape, dtype)


def keep(x):
    return pltpu.with_memory_space_constraint(x, VMEM)


def tile(i):
    return pl.ds(pl.multiple_of(i * LAT, LAT), LAT)


UNROLL = 4
AHEAD = 2
SIZE = BINS * ROWS * LAT
PART = OWN * ROWS * LAT
N = ROWS * LAT
COEF = 0.75 / SCALE


def half_rows(half):
    return pl.ds(pl.multiple_of(N * half, N), N)


def pack_kernel(pos, planck, dust, eold, pair, near, far, stage, shares, sems):
    half = pos[0]
    mine = pl.ds(pl.multiple_of(N * half, N), N)
    other = pl.ds(pl.multiple_of(N * (1 - half), N), N)
    copies = [
        pltpu.make_async_copy(dust.at[:, other, :], far, sems.at[0]),
        pltpu.make_async_copy(eold.at[:, other, :], stage, sems.at[1]),
        pltpu.make_async_copy(dust.at[:, mine, :], near, sems.at[2]),
        pltpu.make_async_copy(planck, shares, sems.at[3]),
    ]
    for copy in copies:
        copy.start()
    copies[0].wait()
    for b in range(BINS):
        pair[pl.ds(b * N, N), :] = far[b]
    copies[1].wait()
    for g in range(OWN):
        pair[pl.ds(SIZE + g * N, N), :] = stage[g].astype(BF)
    copies[3].wait()
    row = lax.broadcasted_iota(jnp.int32, (2 * LAT, LANES), 0)
    share = jnp.zeros((2 * LAT, LANES), F32)
    for g in range(OWN):
        share = jnp.where(row == g, shares[g], share)
    for i in range(3):
        piece = share.astype(BF)
        pair[pl.ds(SIZE + PART + 2 * i * LAT, 2 * LAT), :] = piece
        share = share - piece.astype(F32)
    copies[2].wait()


def write_slabs(pos, src, at, t1, t2, r1, r2):
    part, tp = pos[0], pos[1]
    low = src[pl.ds(0, TILES, stride=LAT), :].astype(BF)
    high = src[pl.ds(LAT - 1, TILES, stride=LAT), :].astype(BF)
    rows = pl.ds(at, TILES)

    @pl.when(tp == 0)
    def _():
        t1[rows, :] = high
        t2[rows, :] = low

    @pl.when(tp == 1)
    def _():
        t1[rows, :] = low
        t2[rows, :] = high

    for g in range(0, GROUPS, 2):
        def edge(r):
            a = src[tile(g * ROWS + r), :]
            b = src[tile((g + 1) * ROWS + r), :]
            return jnp.concatenate([a, b], axis=0).astype(BF)

        r1[pl.ds(at + g * LAT, 2 * LAT), :] = edge((ROWS - 1) * (1 - part))
        r2[pl.ds(at + g * LAT, 2 * LAT), :] = edge((ROWS - 1) * part)


def widen(wide, tile_of, source):
    for b in range(BINS):
        for r in range(ROWS):
            wide[tile(r * 4 * BINS + source * BINS + b), :] = tile_of(b, r).astype(F32)


def early_kernel(pos, planck, mine, pair, near, eold, wide, e, share, sems):
    place = pos[2]
    slot = place % 2
    copies = [
        pltpu.make_async_copy(eold.at[g, half_rows(pos[0]), :], e.at[half_rows(slot * OWN + g), :], sems.at[g])
        for g in range(OWN)
    ]
    for copy in copies:
        copy.start()
    widen(wide, lambda b, r: mine[b, tile(r), :], place)
    widen(wide, lambda b, r: near[b, tile(r), :], jnp.bitwise_xor(place, 2))
    widen(wide, lambda b, r: pair[tile(b * ROWS + r), :], jnp.bitwise_xor(place, 1))
    for g in range(OWN):
        e[half_rows((1 - slot) * OWN + g), :] = pair[pl.ds(SIZE + g * N, N), :].astype(F32)
    at = SIZE + PART
    pieces = [pair[pl.ds(at + 2 * LAT * i, 2 * LAT), :].astype(F32) for i in range(3)]
    row = lax.broadcasted_iota(jnp.int32, (2 * LAT, LANES), 0)
    ours = jnp.zeros((2 * LAT, LANES), F32)
    for g in range(OWN):
        ours = jnp.where(row == g, planck[g], ours)
    share[slot] = ours
    share[1 - slot] = pieces[0] + pieces[1] + pieces[2]
    for copy in copies:
        copy.wait()


def late_kernel(pos, columns, wide_in, far, e, kap, t1, t2, r1, r2, wide, turned):
    place = pos[2]
    widen(wide, lambda b, r: far[b, tile(r), :], jnp.bitwise_xor(place, 3))
    lhs = columns[pl.ds(pl.multiple_of((place // 2) * GROUPS, LAT), GROUPS), :].astype(BF)

    def one(r, carry):
        bins = 4 * BINS
        rhs = [wide[pl.ds(r * bins * LAT + t, bins, stride=LAT), :] for t in range(LAT)]
        rhs = jnp.concatenate(rhs, axis=1).astype(BF)
        out = SCALE * jnp.dot(lhs, rhs, preferred_element_type=F32)
        for t in range(LAT):
            turned[pl.ds(r * GROUPS * LAT + t, GROUPS, stride=LAT), :] = out[:, t * LANES : (t + 1) * LANES]
        for g in range(GROUPS):
            kap[tile(g * ROWS + r), :] = turned[tile(r * GROUPS + g), :]
        return carry

    lax.fori_loop(0, ROWS, one, 0, unroll=2)
    write_slabs(pos, e, 0, t1, t2, r1, r2)
    write_slabs(pos, kap, TILES, t1, t2, r1, r2)


def face(ea, eb, c):
    d = eb - ea
    w = 1.0 / (c + jnp.abs(d) / (ea + eb))
    return w, w * d


def spread(row):
    return jnp.broadcast_to(row, (LAT, LANES))


def share_of(share, g):
    part = g // OWN
    return spread(share[part, pl.ds(g - part * OWN, 1), :])


def inner_body(e, kap, numer, denom, prepare):
    def one(g, carry):
        base = g * ROWS
        tiles = [e[tile(base + r), :] for r in range(ROWS)]
        ks = [kap[tile(base + r), :] for r in range(ROWS)]
        coef, olds = prepare(g, base, tiles, ks)
        out = []
        for r in range(ROWS):
            here = tiles[r]
            c_up, c_east, c_above = coef[r]
            w_up, f_up = face(here, pltpu.roll(here, LAT - 1, 0), c_up)
            w_east, f_east = face(here, pltpu.roll(here, LANES - 1, 1), c_east)
            w = (w_up + pltpu.roll(w_up, 1, 0)) + (w_east + pltpu.roll(w_east, 1, 1))
            f = (f_up - pltpu.roll(f_up, 1, 0)) + (f_east - pltpu.roll(f_east, 1, 1))
            if r > 0:
                w, f = w + w_below, f - f_below
            if r + 1 < ROWS:
                w_below, f_below = face(here, tiles[r + 1], c_above)
                w, f = w + w_below, f + f_below
            out.append((olds[r] + (here * w + f), SCALE + ks[r] + w))
        for r in range(ROWS):
            numer[tile(base + r), :], denom[tile(base + r), :] = out[r]
        return carry

    lax.fori_loop(0, GROUPS, one, 0, unroll=UNROLL)


def inner_first(pos, e, kap, share, numer, denom, up_c, east_c, above_c, e01, ssum):
    ssum[...] = jnp.zeros_like(ssum)
    top = lax.broadcasted_iota(jnp.int32, (LAT, LANES), 0) == LAT - 1

    def prepare(g, base, tiles, ks):
        sums = [ssum[tile(r), :] for r in range(ROWS)]
        share_row = share_of(share, g)
        olds = [SCALE * x for x in tiles]
        out = []
        for r in range(ROWS):
            k = ks[r]
            c_up = jnp.where(top, jnp.inf, COEF * (k + pltpu.roll(k, LAT - 1, 0)))
            c_east = COEF * (k + pltpu.roll(k, LANES - 1, 1))
            out.append((c_up, c_east, COEF * (k + ks[r + 1]) if r + 1 < ROWS else None))
        for r in range(ROWS):
            i = base + r
            up_c[tile(i), :], east_c[tile(i), :] = out[r][:2]
            if r + 1 < ROWS:
                above_c[tile(i), :] = out[r][2]
            e01[tile(i), :] = olds[r]
            ssum[tile(r), :] = sums[r] + ks[r] * share_row
        return out, olds

    inner_body(e, kap, numer, denom, prepare)


def inner_next(pos, e, kap, e01, up_c, east_c, above_c, numer, denom):
    def prepare(g, base, tiles, ks):
        at = [tile(base + r) for r in range(ROWS)]
        return [(up_c[i, :], east_c[i, :], above_c[i, :]) for i in at], [e01[i, :] for i in at]

    inner_body(e, kap, numer, denom, prepare)


def unpack_halos(pos, slabs, at, halo):
    part, tp = pos[0], pos[1]
    rows = pl.ds(at, TILES)
    halo[1 - tp] = slabs[0][rows, :].astype(F32)
    halo[tp] = slabs[1][rows, :].astype(F32)
    halo[3 - part] = slabs[2][rows, :].astype(F32)
    halo[2 + part] = slabs[3][rows, :].astype(F32)


def outer_body(e, kap, share, temp4, halo, edge, numer, denom, enew, ksum):
    def close(g, carry):
        lows = tile(g)
        base = g * ROWS * LAT
        places = [pl.ds(base, ROWS, stride=LAT), pl.ds(base + LAT - 1, ROWS, stride=LAT)]
        places += [tile(g * ROWS), tile(g * ROWS + ROWS - 1)]
        pasts = [e[i, :] for i in places]
        outs = [halo[j, lows, :] for j in range(4)]
        ws = [face(pasts[j], outs[j], edge[j, lows, :])[0] for j in range(4)]
        for j, i in enumerate(places):
            numer[i, :] = numer[i, :] + ws[j] * outs[j]
            denom[i, :] = denom[i, :] + ws[j]
        return carry

    lax.fori_loop(0, GROUPS, close, 0, unroll=8)

    def finish(g, sums):
        row_share = share_of(share, g)
        at = [tile(g * ROWS + r) for r in range(ROWS)]
        ks = [kap[i, :] for i in at]
        fresh = [(numer[at[r], :] + ks[r] * (row_share * temp4[tile(r), :])) / denom[at[r], :] for r in range(ROWS)]
        sums = tuple(sums[r] + ks[r] * fresh[r] for r in range(ROWS))
        for r in range(ROWS):
            enew[at[r], :] = fresh[r]
        return sums

    sums = lax.fori_loop(0, GROUPS, finish, (jnp.zeros((LAT, LANES), F32),) * ROWS, unroll=8)
    for r in range(ROWS):
        ksum[tile(r), :] = sums[r]


def own_rows(pos, ref):
    return ref[pl.ds(pl.multiple_of(pos[0] * N, N), N), :]


def terms(told, t, stot):
    cube = t * t * t
    return HEAT * told + 3.0 * stot * (cube * t), HEAT + 4.0 * stot * cube


def outer_first(pos, e, kap, share, told, ssum, numer_in, denom_in, h0, h1, h2, h3, *refs):
    enew, sums, edge, t1, t2, r1, r2, numer, denom = refs[:9]
    temp4, halo = refs[9:]
    slabs = (h0, h1, h2, h3)
    unpack_halos(pos, slabs, TILES, halo)
    for j, at in ((0, 0), (1, LAT - 1)):
        edge[j] = COEF * (kap[pl.ds(at, TILES, stride=LAT), :] + halo[j])
    for g in range(GROUPS):
        for j, at in ((2, 0), (3, ROWS - 1)):
            edge[j, tile(g), :] = COEF * (kap[tile(g * ROWS + at), :] + halo[j, tile(g), :])
    unpack_halos(pos, slabs, 0, halo)
    t = own_rows(pos, told)
    temp4[...] = t * t * t * t
    outer_body(e, kap, share, temp4, halo, edge, numer, denom, enew, sums.at[pl.ds(0, N)])
    sums[pl.ds(N, N), :] = ssum[...]
    write_slabs(pos, enew, 0, t1, t2, r1, r2)


def outer_middle(pos, e, kap, share, told, sums, got, edge, numer_in, denom_in, h0, h1, h2, h3, *refs):
    enew, ksum, tnow, stot, t1, t2, r1, r2, numer, denom = refs[:10]
    temp4, halo = refs[10:]
    unpack_halos(pos, (h0, h1, h2, h3), 0, halo)
    both = (sums[...] + got[...]) / SCALE
    s = both[N:]
    stot[...] = s
    t = own_rows(pos, told)
    up, down = terms(t, t, s)
    t = (up + both[:N]) / down
    tnow[...] = t
    temp4[...] = t * t * t * t
    outer_body(e, kap, share, temp4, halo, edge, numer, denom, enew, ksum)
    write_slabs(pos, enew, 0, t1, t2, r1, r2)


def outer_last(pos, e, kap, share, told, tprev, stot, part, got, edge, numer_in, denom_in, h0, h1, h2, h3, *refs):
    eown, ahead, behind, ksum, up, down, numer, denom = refs[:8]
    temp4, halo, enew = refs[8:]
    unpack_halos(pos, (h0, h1, h2, h3), 0, halo)
    s = stot[...]
    old = own_rows(pos, told)
    above, below = terms(old, tprev[...], s)
    t = (above + (part[...] + got[...]) / SCALE) / below
    temp4[...] = t * t * t * t
    outer_body(e, kap, share, temp4, halo, edge, numer, denom, enew, ksum)
    slot = pos[2] % 2
    eown[...] = enew[pl.ds(pl.multiple_of(slot * PART, PART), PART), :]
    theirs = pl.multiple_of((1 - slot) * PART, PART)
    ahead[...] = enew[pl.ds(theirs, AHEAD * N), :]
    behind[...] = enew[pl.ds(pl.multiple_of(theirs + AHEAD * N, N), PART - AHEAD * N), :]
    up[...], down[...] = terms(old, t, s)


def finish_kernel(ksum, got, up, down, temp):
    temp[...] = (up[...] + (ksum[...] + got[...]) / SCALE) / down[...]


def join_kernel(pos, eown, ahead, behind, mine, other, energy, temp):
    half = pos[0]
    for g in range(OWN):
        energy[half_rows(2 * g + half), :] = eown[pl.ds(g * N, N), :]
        src, at = (ahead, g) if g < AHEAD else (behind, g - AHEAD)
        energy[half_rows(2 * g + 1 - half), :] = src[pl.ds(at * N, N), :]
    temp[half_rows(half), :] = mine[...]
    temp[half_rows(1 - half), :] = other[...]


def theta_pairs(count, odd):
    return [p for i in range(odd, count - 1, 2) for p in ((i, i + 1), (i + 1, i))]


def row_pairs(rows, odd):
    def device(chain, position):
        row, part = position // 2, position % 2
        return row * 4 + 2 * chain + (part ^ (row & 1))

    pairs = []
    for chain in range(2):
        for i in range(odd, 2 * rows - 1, 2):
            a, b = device(chain, i), device(chain, i + 1)
            pairs += [(a, b), (b, a)]
    return pairs


def xor(x, k):
    return lax.ppermute(x, "group", [(i, i ^ k) for i in range(4)])


def swap_halos(slabs, part=None):
    t1, t2, r1, r2 = slabs
    nt, nr = lax.axis_size("theta"), lax.axis_size("row")
    t2 = lax.ppermute(t2, "theta", theta_pairs(nt, 1))
    part = part if part is None else keep(xor(part, 2))
    t1 = lax.ppermute(t1, "theta", theta_pairs(nt, 0))
    r2 = lax.ppermute(r2, ("row", "group"), row_pairs(nr, 1))
    r1 = lax.ppermute(r1, ("row", "group"), row_pairs(nr, 0))
    return tuple(keep(x) for x in (t1, t2, r1, r2)), part


def shards(dust, table, planck, energy_old, temp_old):
    place = lax.axis_index("group")
    row = lax.axis_index("row")
    pos = jnp.stack([(place ^ row) & 1, lax.axis_index("theta") & 1, place, row]).astype(jnp.int32)
    dust = dust.reshape(BINS, 2 * N, LANES)
    energy_old = energy_old.reshape(OWN, 2 * N, LANES)
    told = temp_old.reshape(-1, LANES)
    columns = table.astype(F32).T
    slabs = [held((TILES, LANES), BF)] * 4
    scratch = [VMEM((N, LANES), F32), VMEM((4, TILES, LANES), F32)]
    full = held((CELLS, LANES))
    sheet = held((N, LANES))
    block = held((BINS, N, LANES), BF)

    pair, mine, far = call(
        pack_kernel,
        [held((SIZE + PART + 6 * LAT, LANES), BF), block, block],
        (pos, *(pltpu.with_memory_space_constraint(x, pltpu.HBM) for x in (planck, dust, energy_old))), smem=1, space=pl.ANY,
        scratch=[VMEM((OWN, N, LANES), F32), SMEM(planck.shape, F32), pltpu.SemaphoreType.DMA((4,))],
    )
    pair = xor(pair, 1)
    near = xor(mine, 2)
    far = xor(far, 3)
    wide, e, share = call(
        early_kernel, [held((4 * SIZE, LANES)), full, held((2, 2 * LAT, LANES))],
        (pos, planck, keep(mine), keep(pair), keep(near), pltpu.with_memory_space_constraint(energy_old, pltpu.HBM)),
        smem=2, hbm=1, flops=20_000_000, scratch=[pltpu.SemaphoreType.DMA((OWN,))],
    )
    e = keep(e)
    kap, *both = call(
        late_kernel,
        [full] + [held((2 * TILES, LANES), BF)] * 4 + [held((4 * SIZE, LANES))],
        (pos, keep(columns), keep(wide), keep(far), e), smem=1,
        scratch=[VMEM((CELLS, LANES), F32)], flops=5_000_000, aliases=((2, 5),),
    )
    both = both[:4]
    kap, share = keep(kap), keep(share)
    halos, _ = swap_halos(both)
    numer, denom, *coefs, e01, ssum = call(
        inner_first, [full] * 6 + [sheet], (pos, e, kap, share), smem=1, flops=20_000_000,
    )
    coefs = [keep(x) for x in coefs]
    e01 = keep(e01)
    e, sums, edge, *rest = call(
        outer_first, [full, held((2 * N, LANES)), held((4, TILES, LANES))] + slabs + [full, full],
        (pos, e, kap, share, told, keep(ssum), keep(numer), keep(denom), *halos), smem=1,
        scratch=scratch, flops=5_000_000, aliases=((6, 7), (7, 8)),
    )
    rest = rest[:4]
    e, edge, sums = keep(e), keep(edge), keep(sums)
    halos, got = swap_halos(rest, sums)
    numer, denom = call(inner_next, [full] * 2, (pos, e, kap, e01, *coefs), smem=1, flops=20_000_000)
    e, part, temp, stot, *rest = call(
        outer_middle, [full, sheet, sheet, sheet] + slabs + [full, full],
        (pos, e, kap, share, told, sums, got, edge, keep(numer), keep(denom), *halos), smem=1,
        scratch=scratch, flops=5_000_000, aliases=((8, 8), (9, 9)),
    )
    rest = rest[:4]
    e, part = keep(e), keep(part)
    halos, got = swap_halos(rest, part)
    numer, denom = call(inner_next, [full] * 2, (pos, e, kap, e01, *coefs), smem=1, flops=20_000_000)
    eown, ahead, behind, part, up, down, _, _ = call(
        outer_last,
        [held((PART, LANES)), held((AHEAD * N, LANES)), held((PART - AHEAD * N, LANES)), sheet, sheet, sheet, full, full],
        (pos, e, kap, share, told, keep(temp), keep(stot), part, got, edge, keep(numer), keep(denom), *halos), smem=1,
        scratch=scratch + [VMEM((CELLS, LANES), F32)], flops=5_000_000, aliases=((10, 6), (11, 7)),
    )
    ahead = xor(ahead, 1)
    got = xor(part, 2)
    behind = xor(behind, 1)
    mine, = call(finish_kernel, [sheet], [keep(x) for x in (part, got, up, down)])
    other = xor(mine, 1)
    energy, temp = call(
        join_kernel,
        [jax.ShapeDtypeStruct((2 * PART, LANES), F32), jax.ShapeDtypeStruct((2 * N, LANES), F32)],
        (pos, *(keep(x) for x in (eown, ahead, behind, mine, other))), smem=1,
    )
    return energy.reshape(OWN, 2 * ROWS, LAT, LANES), temp.reshape(2 * ROWS, LAT, LANES)


def solution(mesh):
    return jax.shard_map(
        shards,
        mesh=mesh,
        in_specs=(
            P("group", "row", "theta", None),
            P(),
            P("group"),
            P("group", "row", "theta", None),
            P("row", "theta", None),
        ),
        out_specs=(P("group", "row", "theta", None), P("row", "theta", None)),
        check_vma=False,
    )
```

```python
import jax
import jax.numpy as jnp
from jax import lax
from jax.experimental import pallas as pl
from jax.experimental.pallas import tpu as pltpu
from jax.sharding import PartitionSpec as P


HEAT = 2.0
REACH = 20.0
SCALE = 2.0 / REACH


BF = jnp.bfloat16
F32 = jnp.float32
VMEM = pltpu.VMEM
SMEM = pltpu.SMEM

BINS = 8
OWN = 12
GROUPS = 24
ROWS = 8
LAT = 8
LANES = 128
TILES = GROUPS * ROWS
CELLS = TILES * LAT


def call(kernel, outs, args, smem=0, scratch=(), flops=1_000_000, space=VMEM, aliases=()):
    specs = [pl.BlockSpec(memory_space=SMEM)] * smem
    specs += [pl.BlockSpec(memory_space=space)] * (len(args) - smem)
    return pl.pallas_call(
        kernel,
        out_shape=outs,
        in_specs=specs,
        out_specs=[pl.BlockSpec(memory_space=VMEM)] * len(outs),
        scratch_shapes=list(scratch),
        input_output_aliases=dict(aliases),
        cost_estimate=pl.CostEstimate(flops=flops, bytes_accessed=1_000_000, transcendentals=0),
        compiler_params=pltpu.CompilerParams(vmem_limit_bytes=16 << 20),
    )(*args)


def held(shape, dtype=F32):
    return VMEM(shape, dtype)


def keep(x):
    return pltpu.with_memory_space_constraint(x, VMEM)


def tile(i):
    return pl.ds(pl.multiple_of(i * LAT, LAT), LAT)


UNROLL = 4
AHEAD = 6
SIZE = BINS * ROWS * LAT
PART = OWN * ROWS * LAT
N = ROWS * LAT
COEF = 0.75 / SCALE


def half_rows(half):
    return pl.ds(pl.multiple_of(N * half, N), N)


def pack_kernel(pos, planck, dust, eold, eown, pair, near, far, stage, shares, sems):
    half = pos[0]
    mine = pl.ds(pl.multiple_of(N * half, N), N)
    other = pl.ds(pl.multiple_of(N * (1 - half), N), N)
    copies = [
        pltpu.make_async_copy(dust.at[:, other, :], far, sems.at[0]),
        pltpu.make_async_copy(eold.at[:, other, :], stage, sems.at[1]),
        pltpu.make_async_copy(dust.at[:, mine, :], near, sems.at[2]),
        pltpu.make_async_copy(eold.at[:, mine, :], eown, sems.at[3]),
        pltpu.make_async_copy(planck, shares, sems.at[4]),
    ]
    for copy in copies:
        copy.start()
    copies[0].wait()
    for b in range(BINS):
        pair[pl.ds(b * N, N), :] = far[b]
    copies[1].wait()
    for g in range(OWN):
        pair[pl.ds(SIZE + g * N, N), :] = stage[g].astype(BF)
    copies[4].wait()
    row = lax.broadcasted_iota(jnp.int32, (2 * LAT, LANES), 0)
    share = jnp.zeros((2 * LAT, LANES), F32)
    for g in range(OWN):
        share = jnp.where(row == g, shares[g], share)
    for i in range(3):
        piece = share.astype(BF)
        pair[pl.ds(SIZE + PART + 2 * i * LAT, 2 * LAT), :] = piece
        share = share - piece.astype(F32)
    copies[2].wait()
    copies[3].wait()


def write_slabs(pos, src, at, t1, t2, r1, r2):
    part, tp = pos[0], pos[1]
    low = src[pl.ds(0, TILES, stride=LAT), :].astype(BF)
    high = src[pl.ds(LAT - 1, TILES, stride=LAT), :].astype(BF)
    rows = pl.ds(at, TILES)

    @pl.when(tp == 0)
    def _():
        t1[rows, :] = high
        t2[rows, :] = low

    @pl.when(tp == 1)
    def _():
        t1[rows, :] = low
        t2[rows, :] = high

    for g in range(0, GROUPS, 2):
        def edge(r):
            a = src[tile(g * ROWS + r), :]
            b = src[tile((g + 1) * ROWS + r), :]
            return jnp.concatenate([a, b], axis=0).astype(BF)

        r1[pl.ds(at + g * LAT, 2 * LAT), :] = edge((ROWS - 1) * (1 - part))
        r2[pl.ds(at + g * LAT, 2 * LAT), :] = edge((ROWS - 1) * part)


def widen(wide, tile_of, source):
    for b in range(BINS):
        for r in range(ROWS):
            wide[tile(r * 4 * BINS + source * BINS + b), :] = tile_of(b, r).astype(F32)


def early_kernel(pos, planck, mine, pair, near, eown, wide, e, share):
    place = pos[2]
    slot = place % 2
    widen(wide, lambda b, r: mine[b, tile(r), :], place)
    widen(wide, lambda b, r: near[b, tile(r), :], jnp.bitwise_xor(place, 2))
    widen(wide, lambda b, r: pair[tile(b * ROWS + r), :], jnp.bitwise_xor(place, 1))
    for g in range(OWN):
        e[half_rows(slot * OWN + g), :] = eown[g]
        e[half_rows((1 - slot) * OWN + g), :] = pair[pl.ds(SIZE + g * N, N), :].astype(F32)
    at = SIZE + PART
    pieces = [pair[pl.ds(at + 2 * LAT * i, 2 * LAT), :].astype(F32) for i in range(3)]
    row = lax.broadcasted_iota(jnp.int32, (2 * LAT, LANES), 0)
    ours = jnp.zeros((2 * LAT, LANES), F32)
    for g in range(OWN):
        ours = jnp.where(row == g, planck[g], ours)
    share[slot] = ours
    share[1 - slot] = pieces[0] + pieces[1] + pieces[2]


def late_kernel(pos, columns, wide_in, far, e, kap, t1, t2, r1, r2, wide, turned):
    place = pos[2]
    widen(wide, lambda b, r: far[b, tile(r), :], jnp.bitwise_xor(place, 3))
    lhs = columns[pl.ds(pl.multiple_of((place // 2) * GROUPS, LAT), GROUPS), :].astype(BF)

    def one(r, carry):
        bins = 4 * BINS
        rhs = [wide[pl.ds(r * bins * LAT + t, bins, stride=LAT), :] for t in range(LAT)]
        rhs = jnp.concatenate(rhs, axis=1).astype(BF)
        out = SCALE * jnp.dot(lhs, rhs, preferred_element_type=F32)
        for t in range(LAT):
            turned[pl.ds(r * GROUPS * LAT + t, GROUPS, stride=LAT), :] = out[:, t * LANES : (t + 1) * LANES]
        for g in range(GROUPS):
            kap[tile(g * ROWS + r), :] = turned[tile(r * GROUPS + g), :]
        return carry

    lax.fori_loop(0, ROWS, one, 0, unroll=2)
    write_slabs(pos, e, 0, t1, t2, r1, r2)
    write_slabs(pos, kap, TILES, t1, t2, r1, r2)


def face(ea, eb, c):
    d = eb - ea
    w = 1.0 / (c + jnp.abs(d) / (ea + eb))
    return w, w * d


def spread(row):
    return jnp.broadcast_to(row, (LAT, LANES))


def share_of(share, g):
    part = g // OWN
    return spread(share[part, pl.ds(g - part * OWN, 1), :])


def inner_body(e, kap, numer, denom, prepare):
    def one(g, carry):
        base = g * ROWS
        tiles = [e[tile(base + r), :] for r in range(ROWS)]
        ks = [kap[tile(base + r), :] for r in range(ROWS)]
        coef, olds = prepare(g, base, tiles, ks)
        out = []
        for r in range(ROWS):
            here = tiles[r]
            c_up, c_east, c_above = coef[r]
            w_up, f_up = face(here, pltpu.roll(here, LAT - 1, 0), c_up)
            w_east, f_east = face(here, pltpu.roll(here, LANES - 1, 1), c_east)
            w = (w_up + pltpu.roll(w_up, 1, 0)) + (w_east + pltpu.roll(w_east, 1, 1))
            f = (f_up - pltpu.roll(f_up, 1, 0)) + (f_east - pltpu.roll(f_east, 1, 1))
            if r > 0:
                w, f = w + w_below, f - f_below
            if r + 1 < ROWS:
                w_below, f_below = face(here, tiles[r + 1], c_above)
                w, f = w + w_below, f + f_below
            out.append((olds[r] + (here * w + f), SCALE + ks[r] + w))
        for r in range(ROWS):
            numer[tile(base + r), :], denom[tile(base + r), :] = out[r]
        return carry

    lax.fori_loop(0, GROUPS, one, 0, unroll=UNROLL)


def inner_first(pos, e, kap, share, numer, denom, up_c, east_c, above_c, e01, ssum):
    ssum[...] = jnp.zeros_like(ssum)
    top = lax.broadcasted_iota(jnp.int32, (LAT, LANES), 0) == LAT - 1

    def prepare(g, base, tiles, ks):
        sums = [ssum[tile(r), :] for r in range(ROWS)]
        share_row = share_of(share, g)
        olds = [SCALE * x for x in tiles]
        out = []
        for r in range(ROWS):
            k = ks[r]
            c_up = jnp.where(top, jnp.inf, COEF * (k + pltpu.roll(k, LAT - 1, 0)))
            c_east = COEF * (k + pltpu.roll(k, LANES - 1, 1))
            out.append((c_up, c_east, COEF * (k + ks[r + 1]) if r + 1 < ROWS else None))
        for r in range(ROWS):
            i = base + r
            up_c[tile(i), :], east_c[tile(i), :] = out[r][:2]
            if r + 1 < ROWS:
                above_c[tile(i), :] = out[r][2]
            e01[tile(i), :] = olds[r]
            ssum[tile(r), :] = sums[r] + ks[r] * share_row
        return out, olds

    inner_body(e, kap, numer, denom, prepare)


def inner_next(pos, e, kap, e01, up_c, east_c, above_c, numer, denom):
    def prepare(g, base, tiles, ks):
        at = [tile(base + r) for r in range(ROWS)]
        return [(up_c[i, :], east_c[i, :], above_c[i, :]) for i in at], [e01[i, :] for i in at]

    inner_body(e, kap, numer, denom, prepare)


def unpack_halos(pos, slabs, at, halo):
    part, tp = pos[0], pos[1]
    rows = pl.ds(at, TILES)
    halo[1 - tp] = slabs[0][rows, :].astype(F32)
    halo[tp] = slabs[1][rows, :].astype(F32)
    halo[3 - part] = slabs[2][rows, :].astype(F32)
    halo[2 + part] = slabs[3][rows, :].astype(F32)


def outer_body(e, kap, share, temp4, halo, edge, numer, denom, enew, ksum):
    def close(g, carry):
        lows = tile(g)
        base = g * ROWS * LAT
        places = [pl.ds(base, ROWS, stride=LAT), pl.ds(base + LAT - 1, ROWS, stride=LAT)]
        places += [tile(g * ROWS), tile(g * ROWS + ROWS - 1)]
        pasts = [e[i, :] for i in places]
        outs = [halo[j, lows, :] for j in range(4)]
        ws = [face(pasts[j], outs[j], edge[j, lows, :])[0] for j in range(4)]
        for j, i in enumerate(places):
            numer[i, :] = numer[i, :] + ws[j] * outs[j]
            denom[i, :] = denom[i, :] + ws[j]
        return carry

    lax.fori_loop(0, GROUPS, close, 0, unroll=8)

    def finish(g, sums):
        row_share = share_of(share, g)
        at = [tile(g * ROWS + r) for r in range(ROWS)]
        ks = [kap[i, :] for i in at]
        fresh = [(numer[at[r], :] + ks[r] * (row_share * temp4[tile(r), :])) / denom[at[r], :] for r in range(ROWS)]
        sums = tuple(sums[r] + ks[r] * fresh[r] for r in range(ROWS))
        for r in range(ROWS):
            enew[at[r], :] = fresh[r]
        return sums

    sums = lax.fori_loop(0, GROUPS, finish, (jnp.zeros((LAT, LANES), F32),) * ROWS, unroll=8)
    for r in range(ROWS):
        ksum[tile(r), :] = sums[r]


def own_rows(pos, ref):
    return ref[pl.ds(pl.multiple_of(pos[0] * N, N), N), :]


def terms(told, t, stot):
    cube = t * t * t
    return HEAT * told + 3.0 * stot * (cube * t), HEAT + 4.0 * stot * cube


def outer_first(pos, e, kap, share, told, ssum, numer_in, denom_in, h0, h1, h2, h3, *refs):
    enew, sums, edge, t1, t2, r1, r2, numer, denom = refs[:9]
    temp4, halo = refs[9:]
    slabs = (h0, h1, h2, h3)
    unpack_halos(pos, slabs, TILES, halo)
    for j, at in ((0, 0), (1, LAT - 1)):
        edge[j] = COEF * (kap[pl.ds(at, TILES, stride=LAT), :] + halo[j])
    for g in range(GROUPS):
        for j, at in ((2, 0), (3, ROWS - 1)):
            edge[j, tile(g), :] = COEF * (kap[tile(g * ROWS + at), :] + halo[j, tile(g), :])
    unpack_halos(pos, slabs, 0, halo)
    t = own_rows(pos, told)
    temp4[...] = t * t * t * t
    outer_body(e, kap, share, temp4, halo, edge, numer, denom, enew, sums.at[pl.ds(0, N)])
    sums[pl.ds(N, N), :] = ssum[...]
    write_slabs(pos, enew, 0, t1, t2, r1, r2)


def outer_middle(pos, e, kap, share, told, sums, got, edge, numer_in, denom_in, h0, h1, h2, h3, *refs):
    enew, ksum, tnow, stot, t1, t2, r1, r2, numer, denom = refs[:10]
    temp4, halo = refs[10:]
    unpack_halos(pos, (h0, h1, h2, h3), 0, halo)
    both = (sums[...] + got[...]) / SCALE
    s = both[N:]
    stot[...] = s
    t = own_rows(pos, told)
    up, down = terms(t, t, s)
    t = (up + both[:N]) / down
    tnow[...] = t
    temp4[...] = t * t * t * t
    outer_body(e, kap, share, temp4, halo, edge, numer, denom, enew, ksum)
    write_slabs(pos, enew, 0, t1, t2, r1, r2)


def outer_last(pos, e, kap, share, told, tprev, stot, part, got, edge, numer_in, denom_in, h0, h1, h2, h3, *refs):
    eown, ahead, behind, ksum, up, down, numer, denom = refs[:8]
    temp4, halo, enew = refs[8:]
    unpack_halos(pos, (h0, h1, h2, h3), 0, halo)
    s = stot[...]
    old = own_rows(pos, told)
    above, below = terms(old, tprev[...], s)
    t = (above + (part[...] + got[...]) / SCALE) / below
    temp4[...] = t * t * t * t
    outer_body(e, kap, share, temp4, halo, edge, numer, denom, enew, ksum)
    slot = pos[2] % 2
    eown[...] = enew[pl.ds(pl.multiple_of(slot * PART, PART), PART), :]
    theirs = pl.multiple_of((1 - slot) * PART, PART)
    ahead[...] = enew[pl.ds(theirs, AHEAD * N), :]
    behind[...] = enew[pl.ds(pl.multiple_of(theirs + AHEAD * N, N), PART - AHEAD * N), :]
    up[...], down[...] = terms(old, t, s)


def finish_kernel(ksum, got, up, down, temp):
    temp[...] = (up[...] + (ksum[...] + got[...]) / SCALE) / down[...]


def join_kernel(pos, eown, ahead, behind, mine, other, energy, temp):
    half = pos[0]
    for g in range(OWN):
        energy[half_rows(2 * g + half), :] = eown[pl.ds(g * N, N), :]
        src, at = (ahead, g) if g < AHEAD else (behind, g - AHEAD)
        energy[half_rows(2 * g + 1 - half), :] = src[pl.ds(at * N, N), :]
    temp[half_rows(half), :] = mine[...]
    temp[half_rows(1 - half), :] = other[...]


def theta_pairs(count, odd):
    return [p for i in range(odd, count - 1, 2) for p in ((i, i + 1), (i + 1, i))]


def row_pairs(rows, odd):
    def device(chain, position):
        row, part = position // 2, position % 2
        return row * 4 + 2 * chain + (part ^ (row & 1))

    pairs = []
    for chain in range(2):
        for i in range(odd, 2 * rows - 1, 2):
            a, b = device(chain, i), device(chain, i + 1)
            pairs += [(a, b), (b, a)]
    return pairs


def xor(x, k):
    return lax.ppermute(x, "group", [(i, i ^ k) for i in range(4)])


def swap_halos(slabs, part=None):
    t1, t2, r1, r2 = slabs
    nt, nr = lax.axis_size("theta"), lax.axis_size("row")
    t2 = lax.ppermute(t2, "theta", theta_pairs(nt, 1))
    part = part if part is None else keep(xor(part, 2))
    t1 = lax.ppermute(t1, "theta", theta_pairs(nt, 0))
    r2 = lax.ppermute(r2, ("row", "group"), row_pairs(nr, 1))
    r1 = lax.ppermute(r1, ("row", "group"), row_pairs(nr, 0))
    return tuple(keep(x) for x in (t1, t2, r1, r2)), part


def shards(dust, table, planck, energy_old, temp_old):
    place = lax.axis_index("group")
    row = lax.axis_index("row")
    pos = jnp.stack([(place ^ row) & 1, lax.axis_index("theta") & 1, place, row]).astype(jnp.int32)
    dust = dust.reshape(BINS, 2 * N, LANES)
    energy_old = energy_old.reshape(OWN, 2 * N, LANES)
    told = temp_old.reshape(-1, LANES)
    columns = table.astype(F32).T
    slabs = [held((TILES, LANES), BF)] * 4
    scratch = [VMEM((N, LANES), F32), VMEM((4, TILES, LANES), F32)]
    full = held((CELLS, LANES))
    sheet = held((N, LANES))
    block = held((BINS, N, LANES), BF)

    eown, pair, mine, far = call(
        pack_kernel,
        [held((OWN, N, LANES)), held((SIZE + PART + 6 * LAT, LANES), BF), block, block],
        (pos, *(pltpu.with_memory_space_constraint(x, pltpu.HBM) for x in (planck, dust, energy_old))), smem=1, space=pl.ANY,
        scratch=[VMEM((OWN, N, LANES), F32), SMEM(planck.shape, F32), pltpu.SemaphoreType.DMA((5,))],
    )
    pair = xor(pair, 1)
    near = xor(mine, 2)
    far = xor(far, 3)
    wide, e, share = call(
        early_kernel, [held((4 * SIZE, LANES)), full, held((2, 2 * LAT, LANES))],
        (pos, planck, keep(mine), keep(pair), keep(near), keep(eown)), smem=2, flops=20_000_000,
    )
    e = keep(e)
    kap, *both = call(
        late_kernel,
        [full] + [held((2 * TILES, LANES), BF)] * 4 + [held((4 * SIZE, LANES))],
        (pos, keep(columns), keep(wide), keep(far), e), smem=1,
        scratch=[VMEM((CELLS, LANES), F32)], flops=5_000_000, aliases=((2, 5),),
    )
    both = both[:4]
    kap, share = keep(kap), keep(share)
    halos, _ = swap_halos(both)
    numer, denom, *coefs, e01, ssum = call(
        inner_first, [full] * 6 + [sheet], (pos, e, kap, share), smem=1, flops=20_000_000,
    )
    coefs = [keep(x) for x in coefs]
    e01 = keep(e01)
    e, sums, edge, *rest = call(
        outer_first, [full, held((2 * N, LANES)), held((4, TILES, LANES))] + slabs + [full, full],
        (pos, e, kap, share, told, keep(ssum), keep(numer), keep(denom), *halos), smem=1,
        scratch=scratch, flops=5_000_000, aliases=((6, 7), (7, 8)),
    )
    rest = rest[:4]
    e, edge, sums = keep(e), keep(edge), keep(sums)
    halos, got = swap_halos(rest, sums)
    numer, denom = call(inner_next, [full] * 2, (pos, e, kap, e01, *coefs), smem=1, flops=20_000_000)
    e, part, temp, stot, *rest = call(
        outer_middle, [full, sheet, sheet, sheet] + slabs + [full, full],
        (pos, e, kap, share, told, sums, got, edge, keep(numer), keep(denom), *halos), smem=1,
        scratch=scratch, flops=5_000_000, aliases=((8, 8), (9, 9)),
    )
    rest = rest[:4]
    e, part = keep(e), keep(part)
    halos, got = swap_halos(rest, part)
    numer, denom = call(inner_next, [full] * 2, (pos, e, kap, e01, *coefs), smem=1, flops=20_000_000)
    eown, ahead, behind, part, up, down, _, _ = call(
        outer_last,
        [held((PART, LANES)), held((AHEAD * N, LANES)), held((PART - AHEAD * N, LANES)), sheet, sheet, sheet, full, full],
        (pos, e, kap, share, told, keep(temp), keep(stot), part, got, edge, keep(numer), keep(denom), *halos), smem=1,
        scratch=scratch + [VMEM((CELLS, LANES), F32)], flops=5_000_000, aliases=((10, 6), (11, 7)),
    )
    ahead = xor(ahead, 1)
    got = xor(part, 2)
    behind = xor(behind, 1)
    mine, = call(finish_kernel, [sheet], [keep(x) for x in (part, got, up, down)])
    other = xor(mine, 1)
    energy, temp = call(
        join_kernel,
        [jax.ShapeDtypeStruct((2 * PART, LANES), F32), jax.ShapeDtypeStruct((2 * N, LANES), F32)],
        (pos, *(keep(x) for x in (eown, ahead, behind, mine, other))), smem=1,
    )
    return energy.reshape(OWN, 2 * ROWS, LAT, LANES), temp.reshape(2 * ROWS, LAT, LANES)


def solution(mesh):
    return jax.shard_map(
        shards,
        mesh=mesh,
        in_specs=(
            P("group", "row", "theta", None),
            P(),
            P("group"),
            P("group", "row", "theta", None),
            P("row", "theta", None),
        ),
        out_specs=(P("group", "row", "theta", None), P("row", "theta", None)),
        check_vma=False,
    )
```
